32 devices in a mesh: dp: 8 (over z, x), seq: 4 (over y, core).
Axes of the slice: x: 2, y: 2, z: 4, core: 2. Of those that a mesh axis runs over, the one named last changes fastest.
Arguments:
- hidden_states: bfloat16 [8, 2, 1024, 1024], P('dp', None, 'seq'), may hold values from -8.5 to 8.5
- lengths: int32 [8, 2], P('dp'), may hold values from 256 to 1024, as said below
- w_query: bfloat16 [1024, 1024], replicated, may hold values from -0.1875 to 0.1875
- w_key: bfloat16 [1024, 1024], replicated, may hold values from -0.1875 to 0.1875
- w_value: bfloat16 [1024, 1024], replicated, may hold values from -0.1875 to 0.1875
- w_out: bfloat16 [1024, 1024], replicated, may hold values from -0.1875 to 0.1875
- running_cov: float32 [1024, 1024], P('seq'), as said below
Outputs:
- whitened: float32 [8, 2, 1024], P('dp')
- cov_new: float32 [1024, 1024], P('seq')
- loss: float32 [], replicated
The draws below stay inside these ranges and needn't reach their ends.
Inputs may be any that keep to these rules, and one draw needn't show every extreme that they name: `lengths`: at least a quarter of a module is valid; some module has all 1024 tokens valid. `running_cov`: Symmetric, with a diagonal larger than the sum of the magnitudes of its row's other entries.
All inputs are finite; a program needn't handle non-finite values.
Results may differ from the reference program's by a relative error of at most 0.0037.
The reference program's roundings to bfloat16 on the way count: a program that leaves them out, or rounds other values in their place, can miss the bound.
Values sent between devices are 32-bit elements; how exact they have to be, the bound alone decides.
No kernel may reach another device: no remote copies, remote signals or barrier semaphores. Data moves between devices by JAX's collectives and lax.ppermute only.
A program may use at most 128 MiB of HBM per device.

```python
import jax
import jax.numpy as jnp
from jax import lax

D = 1024
HEADS = 16
HEAD_DIM = 64
L_DEV = 256
SEQ_LEN = 1024
PAIRS = 8
N_SEQ = 4


def draw_lengths(key, part):
    first, second = jax.random.split(key)
    drawn = jax.random.randint(first, (PAIRS * 2,), SEQ_LEN // 4, SEQ_LEN + 1)
    where_full = jax.random.randint(second, (), 0, PAIRS * 2)
    drawn = jnp.where(jnp.arange(PAIRS * 2) == where_full, SEQ_LEN, drawn)
    return drawn.reshape(PAIRS, 2).astype(jnp.int32)


def draw_running_cov(key, part):
    first, second, third = jax.random.split(key, 3)
    diag = jnp.exp(jax.random.uniform(first, (D,), jnp.float32, jnp.log(0.5), jnp.log(5.0)))
    noise = jax.random.uniform(second, (D, D), jnp.float32, -1.0, 1.0)
    sym = 0.5 * (noise + noise.T)
    group_size = min(64, D)
    groups = D // group_size
    member = jax.random.permutation(third, D) % groups
    offdiag = 1.0 - jnp.eye(D, dtype=jnp.float32)
    same = (member[:, None] == member[None, :]).astype(jnp.float32) * offdiag
    lower_diag = jnp.minimum(diag[:, None], diag[None, :])
    coupling = lower_diag * (0.8 * same / (group_size - 1) + 0.1 * sym / D) * offdiag
    return (jnp.diag(diag) + coupling) / SEQ_LEN


def draw_hidden_states(key, part):
    first, second = jax.random.split(jax.random.fold_in(key, 7))
    third = jax.random.fold_in(key, 11)
    shape = (PAIRS, SEQ_LEN, D)
    ramp = 1.0 - (jnp.arange(PAIRS, dtype=jnp.float32) + 0.5) / PAIRS
    base = jnp.clip(jax.random.normal(first, shape, jnp.float32), -6.0, 6.0)
    other = jnp.clip(jax.random.normal(second, shape, jnp.float32), -6.0, 6.0)
    share = ramp
    share = share[:, None, None]
    partner = share * base + jnp.sqrt(1.0 - share * share) * other
    blocks = SEQ_LEN // L_DEV
    block_scale = jnp.exp(jax.random.uniform(third, (PAIRS, blocks), jnp.float32, jnp.log(0.25), jnp.log(2.5)))
    position_scale = jnp.repeat(block_scale, L_DEV, axis=1)[:, None, :, None]
    stacked = jnp.stack([base, partner], axis=1) * position_scale
    return jnp.clip(stacked, -8.5, 8.5).astype(jnp.bfloat16)


def scatter_about(own_key, dims, scale, reach, held_as=jnp.bfloat16):
    return jnp.clip(scale * jax.random.normal(own_key, dims, jnp.float32), -reach, reach).astype(held_as)


def setup_inputs(seed: int = 0) -> dict:
    key_of = jax.random.split(jax.random.key(seed), 8)
    hidden_states = draw_hidden_states(jax.random.fold_in(key_of[7], 71), 0)
    lengths = draw_lengths(jax.random.fold_in(key_of[7], 71), 0)
    w_query = scatter_about(key_of[2], (D, D), D ** -0.5, 0.1875)
    w_key = scatter_about(key_of[3], (D, D), D ** -0.5, 0.1875)
    w_value = scatter_about(key_of[4], (D, D), D ** -0.5, 0.1875)
    w_out = scatter_about(key_of[5], (D, D), D ** -0.5, 0.1875)
    running_cov = draw_running_cov(jax.random.fold_in(key_of[7], 71), 0)
    return {"hidden_states": hidden_states, "lengths": lengths, "w_query": w_query, "w_key": w_key, "w_value": w_value, "w_out": w_out, "running_cov": running_cov}


def feature(u):
    return jnp.where(u > 0.0, u + 1.0, jnp.exp(jnp.minimum(u, 0.0)))

def encode(seq_x, length, w_query, w_key, w_value, w_out):
    f_query = feature(jnp.dot(seq_x.astype(jnp.float32), w_query.astype(jnp.float32), preferred_element_type=jnp.float32)).astype(jnp.bfloat16)
    f_key = feature(jnp.dot(seq_x.astype(jnp.float32), w_key.astype(jnp.float32), preferred_element_type=jnp.float32)).astype(jnp.bfloat16)
    values = jnp.dot(seq_x.astype(jnp.float32), w_value.astype(jnp.float32), preferred_element_type=jnp.float32).astype(jnp.bfloat16)
    f_query = f_query.astype(jnp.float32).reshape(N_SEQ, L_DEV, HEADS, HEAD_DIM)
    f_key = f_key.astype(jnp.float32).reshape(N_SEQ, L_DEV, HEADS, HEAD_DIM)
    values = values.astype(jnp.float32).reshape(N_SEQ, L_DEV, HEADS, HEAD_DIM)
    states = jnp.einsum('blhe,blhf->bhef', f_key, values)
    norms = lax.optimization_barrier(jnp.sum(f_key, axis=1))
    prior = jnp.cumsum(states, axis=0) - states
    zprior = jnp.cumsum(norms, axis=0) - norms
    prior = prior.astype(jnp.bfloat16).astype(jnp.float32)
    scores = jnp.einsum('blhe,bmhe->bhlm', f_query, f_key)
    causal = jnp.arange(L_DEV)[:, None] >= jnp.arange(L_DEV)[None, :]
    scores = jnp.where(causal, scores, 0.0)
    weights = scores.astype(jnp.bfloat16).astype(jnp.float32)
    numer = jnp.einsum('bhlm,bmhf->blhf', weights, values) + jnp.einsum('blhe,bhef->blhf', f_query, prior)
    denom = jnp.transpose(lax.optimization_barrier(jnp.sum(scores, axis=-1)), (0, 2, 1)) + jnp.einsum('blhe,bhe->blh', f_query, zprior)
    attended = (numer / denom[..., None]).astype(jnp.bfloat16).reshape(SEQ_LEN, D)
    layer_out = seq_x.astype(jnp.float32) + jnp.dot(attended.astype(jnp.float32), w_out.astype(jnp.float32), preferred_element_type=jnp.float32)
    valid = (jnp.arange(SEQ_LEN) < length).astype(jnp.float32)
    return lax.optimization_barrier(jnp.sum(layer_out * valid[:, None], axis=0)) / length.astype(jnp.float32)

def reference(hidden_states, lengths, w_query, w_key, w_value, w_out, running_cov):
    flat = hidden_states.reshape(PAIRS * 2, SEQ_LEN, D)
    flat_len = lengths.reshape(PAIRS * 2)

    def one(item):
        return encode(item[0], item[1], w_query, w_key, w_value, w_out)
    embed = lax.map(one, (flat, flat_len))
    total = PAIRS * 2
    mean = lax.optimization_barrier(jnp.sum(embed, axis=0)) / total
    second = jnp.dot(embed.T.astype(jnp.float32), embed.astype(jnp.float32), precision=lax.Precision.HIGHEST, preferred_element_type=jnp.float32)
    batch_cov = (second - total * mean[:, None] * mean[None, :]) / (total - 1)
    cov_new = 0.5 * running_cov + 0.5 * batch_cov
    chol = jnp.linalg.cholesky(cov_new)
    whitened = lax.linalg.triangular_solve(chol, (embed - mean).T, left_side=True, lower=True).T
    normed = whitened / jnp.sqrt(lax.optimization_barrier(jnp.sum(whitened * whitened, axis=1, keepdims=True)) + 1e-06)
    normed = normed.reshape(PAIRS, 2, D)
    gap = normed[:, 0] - normed[:, 1]
    loss = jnp.sum(gap * gap) / PAIRS
    return (whitened.reshape(PAIRS, 2, D), cov_new, loss)
```

```python
import functools

import jax
import jax.numpy as jnp
from jax import lax
from jax.experimental import pallas as pl
from jax.experimental.pallas import tpu as pltpu
from jax.sharding import PartitionSpec as P

HEADS = 16
HEAD_DIM = 64
LANES = 128
COLS = 256
F32 = jnp.float32
BF16 = jnp.bfloat16
HIGHEST = lax.Precision.HIGHEST
VMEM = pltpu.VMEM
SMEM = pltpu.SMEM


def params(mib):
    return pltpu.CompilerParams(vmem_limit_bytes=mib << 20)


def feature(u):
    return jnp.where(u > 0.0, u + 1.0, jnp.exp(jnp.minimum(u, 0.0)))


def split(x, parts):
    out = []
    for _ in range(parts):
        piece = x.astype(BF16)
        out.append(piece)
        x = x - piece.astype(F32)
    return out


def dot(a, b, ca=1, cb=0):
    return lax.dot_general(a, b, (((ca,), (cb,)), ((), ())), preferred_element_type=F32)


def dot_f32(a, b, ca=1, cb=0):
    return lax.dot_general(
        a, b, (((ca,), (cb,)), ((), ())), precision=HIGHEST, preferred_element_type=F32
    )


def iota(shape, dim):
    return lax.broadcasted_iota(jnp.int32, shape, dim)


def encode_kernel(h_ref, wq_ref, wk_ref, wv_ref, fq_ref, num_ref, den_ref, state_ref):
    count, span = h_ref.shape[0], h_ref.shape[1]
    rows = h_ref[...].reshape(count * span, h_ref.shape[2])
    fq = feature(dot(rows, wq_ref[...])).astype(BF16)
    fk = feature(dot(rows, wk_ref[...])).astype(BF16)
    values = dot(rows, wv_ref[...]).astype(BF16)
    fq_ref[...] = fq.reshape(fq_ref.shape)
    causal = iota((span, span), 0) >= iota((span, span), 1)
    ones_below = causal.astype(BF16)
    low = iota((span, LANES), 1) < HEAD_DIM
    same_head = (iota((LANES, LANES), 0) < HEAD_DIM) == (iota((LANES, LANES), 1) < HEAD_DIM)
    summing = jnp.concatenate([same_head.astype(BF16)] * 2, axis=0)
    for module in range(count):
        at = slice(module * span, (module + 1) * span)
        running = dot(ones_below, fk[at])
        for pair in range(COLS // LANES):
            cols = slice(pair * LANES, (pair + 1) * LANES)
            q, k, v = fq[at, cols], fk[at, cols], values[at, cols]
            state = dot(k, v, 0, 0)
            merged = jnp.where(low[:HEAD_DIM], state[:HEAD_DIM], state[HEAD_DIM:])
            state_ref[pair, module] = jnp.concatenate(
                [merged, jnp.broadcast_to(running[span - 1 :, cols], (8, LANES))], axis=0
            )
            hi, lo = split(q.astype(F32) * running[:, cols], 2)
            den_ref[module, :, cols] = dot(jnp.concatenate([hi, lo], axis=1), summing)
            parts = []
            for half in range(2):
                own = low if half == 0 else jnp.logical_not(low)
                scores = dot(jnp.where(own, q, jnp.zeros_like(q)), k, 1, 1)
                weights = jnp.where(causal, scores, 0.0).astype(BF16)
                parts.append(dot(weights, v))
            num_ref[module, :, cols] = jnp.where(low, parts[0], parts[1])


def encode(hidden, w_query, w_key, w_value):
    count, span, width = hidden.shape
    steps = width // COLS
    weight = pl.BlockSpec((width, COLS), lambda j: (0, j))
    block = pl.BlockSpec((count, span, COLS), lambda j: (0, 0, j))
    pairs = COLS // LANES
    shape = (count, span, width)
    state_shape = (width // LANES, count, HEAD_DIM + 8, LANES)
    return pl.pallas_call(
        encode_kernel,
        grid=(steps,),
        in_specs=[pl.BlockSpec(hidden.shape, lambda j: (0, 0, 0)), weight, weight, weight],
        out_specs=[
            block,
            block,
            block,
            pl.BlockSpec((pairs,) + state_shape[1:], lambda j: (j, 0, 0, 0)),
        ],
        out_shape=[
            jax.ShapeDtypeStruct(shape, BF16),
            jax.ShapeDtypeStruct(shape, F32),
            jax.ShapeDtypeStruct(shape, F32),
            jax.ShapeDtypeStruct(state_shape, F32),
        ],
        compiler_params=params(48),
        name="encode",
    )(hidden, w_query, w_key, w_value)


def pool_kernel(len_ref, start_ref, h_ref, fq_ref, num_ref, den_ref, prior_ref, wo_ref, out_ref):
    count, span = fq_ref.shape[0], fq_ref.shape[1]
    step = pl.program_id(0)
    low = iota((HEAD_DIM, LANES), 1) < HEAD_DIM
    same_head = (iota((LANES, LANES), 0) < HEAD_DIM) == (iota((LANES, LANES), 1) < HEAD_DIM)
    summing = jnp.concatenate([same_head.astype(BF16)] * 2, axis=0)
    sums = []
    hsums = []
    for module in range(count):
        valid = iota((span, LANES), 0) + start_ref[0] < len_ref[module]
        heads = []
        plain = []
        for pair in range(COLS // LANES):
            cols = slice(pair * LANES, (pair + 1) * LANES)
            q = fq_ref[module, :, cols]
            prior = prior_ref[pair, module]
            state = prior[:HEAD_DIM].astype(BF16)
            empty = jnp.zeros_like(state)
            state = jnp.concatenate(
                [jnp.where(low, state, empty), jnp.where(low, empty, state)], axis=0
            )
            hi, lo = split(q.astype(F32) * prior[HEAD_DIM : HEAD_DIM + 1], 2)
            numer = num_ref[module, :, cols] + dot(q, state)
            denom = den_ref[module, :, cols] + dot(jnp.concatenate([hi, lo], axis=1), summing)
            attended = (numer / denom).astype(BF16).astype(F32)
            heads.append(jnp.sum(jnp.where(valid, attended, 0.0), axis=0, keepdims=True))
            plain.append(
                jnp.sum(
                    jnp.where(valid, h_ref[module, :, cols].astype(F32), 0.0), axis=0, keepdims=True
                )
            )
        sums.append(jnp.concatenate(heads, axis=1))
        hsums.append(jnp.concatenate(plain, axis=1))
    sums = jnp.concatenate(sums, axis=0)
    pieces = split(sums, 3)
    part = dot(jnp.concatenate(pieces, axis=0), wo_ref[...])
    part = part[:count] + part[count : 2 * count] + part[2 * count :]

    @pl.when(step == 0)
    def _():
        out_ref[...] = part

    @pl.when(step > 0)
    def _():
        out_ref[...] += part

    here = pl.ds(pl.multiple_of(step * COLS, COLS), COLS)
    out_ref[:, here] += jnp.concatenate(hsums, axis=0)

    @pl.when(step == pl.num_programs(0) - 1)
    def _():
        for module in range(count):
            out_ref[module : module + 1, :] /= len_ref[module].astype(F32)


def pooled_rows(flat_len, start, hidden, fq, num, den, prior, w_out):
    count, span, width = hidden.shape
    block = pl.BlockSpec((count, span, COLS), lambda j: (0, 0, j))
    pairs = COLS // LANES
    return pl.pallas_call(
        pool_kernel,
        grid=(width // COLS,),
        in_specs=[
            pl.BlockSpec(memory_space=SMEM),
            pl.BlockSpec(memory_space=SMEM),
            block,
            block,
            block,
            block,
            pl.BlockSpec((pairs,) + prior.shape[1:], lambda j: (j, 0, 0, 0)),
            pl.BlockSpec((COLS, width), lambda j: (j, 0)),
        ],
        out_specs=pl.BlockSpec((count, width), lambda j: (0, 0)),
        out_shape=jax.ShapeDtypeStruct((count, width), F32),
        compiler_params=params(40),
        name="pool",
    )(flat_len, start, hidden, fq, num, den, prior, w_out)


def leaf_factor(mat):
    groups = LANES // 8
    sub, lane = iota((8, LANES), 0), iota((8, LANES), 1)
    rows = [mat[8 * g : 8 * g + 8, :] for g in range(groups)]

    def row_of(x, i):
        return jnp.broadcast_to(x[i : i + 1, :], (8, LANES))

    def col_of(x, c):
        return jnp.broadcast_to(x[:, c : c + 1], (8, LANES))

    for g in range(groups):
        base = 8 * g
        own = (lane >= base) & (lane < base + 8)
        here = [col_of(rows[g], base + c) for c in range(8)]
        now = jnp.where(own, (lane - base == sub).astype(F32), rows[g])
        following = g + 1 < groups
        if following:
            after = [col_of(rows[g + 1], base + c) for c in range(8)]
            then = jnp.where(own, 0.0, rows[g + 1])
        done = []
        for i in range(8):
            r = lax.rsqrt(row_of(here[i], i))
            u = row_of(now, i) * r
            done.append(u)
            m = here[i] * r
            if i < 7:
                now = now - m * u
            if following:
                mh = after[i] * r
                then = then - mh * u
            for c in range(i + 1, 8):
                s = row_of(here[c], i) * r
                here[c] = here[c] - m * s
                if following:
                    after[c] = after[c] - mh * s
        final = done[0]
        for i in range(1, 8):
            final = jnp.where(sub == i, done[i], final)
        rows[g] = final
        if following:
            rows[g + 1] = then
        if g + 2 < groups:
            turned = final.T
            for h in range(g + 2, groups):
                coef = turned[8 * h : 8 * h + 8, :]
                x = jnp.where(own, 0.0, rows[h])
                for i in range(8):
                    x = x - col_of(coef, i) * done[i]
                rows[h] = x
    return jnp.concatenate(rows, axis=0)


def factor_kernel(offsets, mine_ref, *refs):
    *piece_refs, out_ref, sems = refs
    n = out_ref.shape[0]
    panels = n // LANES
    share = piece_refs[0].shape[1]
    copies = []
    slot = 0
    for ref in piece_refs:
        for b in range(ref.shape[0]):
            block = jnp.bitwise_xor(mine_ref[0], offsets[slot])
            to = pl.ds(pl.multiple_of(block * share, share), share)
            copies.append(pltpu.make_async_copy(ref.at[b], out_ref.at[to, :], sems.at[slot]))
            slot += 1
    for copy in copies:
        copy.start()
    for copy in copies:
        copy.wait()
    row, col = iota((LANES, LANES), 0), iota((LANES, LANES), 1)
    out_ref[...] = out_ref[...] * 0.5

    def run(k, carried):
        ks = pl.ds(pl.multiple_of(k * LANES, LANES), LANES)
        inverse = jnp.where(col <= row, leaf_factor(out_ref[ks, ks]), 0.0)
        out_ref[ks, :] = dot_f32(inverse, out_ref[ks, :])
        out_ref[ks, ks] = inverse

        def trail(h, carried):
            hs = pl.ds(pl.multiple_of(h * LANES, LANES), LANES)
            out_ref[hs, ks] = jnp.zeros((LANES, LANES), F32)
            out_ref[hs, :] = out_ref[hs, :] - dot_f32(out_ref[ks, hs], out_ref[ks, :], 0, 0)
            return carried

        return lax.fori_loop(k + 1, panels, trail, carried)

    lax.fori_loop(0, panels, run, 0)


def inverse_factor(mine, pieces, offsets):
    n = pieces[0].shape[2]
    return pl.pallas_call(
        functools.partial(factor_kernel, offsets),
        in_specs=[pl.BlockSpec(memory_space=SMEM)]
        + [pl.BlockSpec(memory_space=pl.ANY)] * len(pieces),
        out_specs=pl.BlockSpec(memory_space=VMEM),
        out_shape=jax.ShapeDtypeStruct((n, n), F32),
        scratch_shapes=[pltpu.SemaphoreType.DMA((len(offsets),))],
        compiler_params=params(40),
        name="factor",
        cost_estimate=pl.CostEstimate(flops=60_000_000_000, transcendentals=0, bytes_accessed=8 << 20),
    )(mine, *pieces)


def whiten_kernel(
    at_ref, embed_ref, inv_ref, cov_ref, white_ref, cov_out_ref, loss_ref, rows_ref, centred_ref
):
    total, n = embed_ref.shape
    chunks = n // LANES
    share = cov_ref.shape[0]
    embed = embed_ref[...]
    centred = embed - jnp.sum(embed, axis=0, keepdims=True) / total
    weight = 0.5 / (total - 1)
    for k in range(chunks):
        upto = (k + 1) * LANES
        rows_ref[:, k, :] = dot_f32(centred[:, :upto], inv_ref[k * LANES : upto, :upto], 1, 1)
    w = [rows_ref[a] for a in range(total)]
    pairs = [(a, b) for a in range(total) for b in range(a, total)]
    products = jnp.concatenate([w[a] * w[b] for a, b in pairs], axis=0)
    before = iota((LANES, 2 * LANES), 0) < iota((LANES, 2 * LANES), 1)
    earlier = before.astype(BF16)
    sums = [dot(piece, earlier) for piece in split(products, 3)]
    sums = sums[0] + sums[1] + sums[2]
    chunk = iota((8, LANES), 0)
    entry = {}
    for i, (a, b) in enumerate(pairs):
        inside = sums[8 * i : 8 * i + 8, :LANES]
        whole = sums[8 * i : 8 * i + 8, LANES:]
        carry = jnp.where(chunk >= 1, pltpu.roll(whole, 1, 0), 0.0)
        for by in (1, 2, 4):
            carry = carry + jnp.where(chunk >= by, pltpu.roll(carry, by, 0), 0.0)
        entry[a, b] = weight * (inside + carry) + (1.0 if a == b else 0.0)
    right = list(w)
    inverse = []
    spread = jnp.ones((8, LANES), F32)
    for p in range(total):
        inv = 1.0 / entry[p, p]
        inverse.append(inv)
        spread = spread + weight * right[p] * right[p] * inv
        for a in range(p + 1, total):
            f = entry[p, a] * inv
            for b in range(a, total):
                entry[a, b] = entry[a, b] - f * entry[p, b]
            right[a] = right[a] - f * right[p]
    scale = lax.rsqrt(spread)
    solved = [None] * total
    for p in reversed(range(total)):
        x = right[p]
        for b in range(p + 1, total):
            x = x - entry[p, b] * solved[b]
        solved[p] = x * inverse[p]
    solved = [x * scale for x in solved]
    gap = jnp.zeros((8, LANES), F32)
    normed = []
    for a in range(total):
        norm = jnp.sum(jnp.sum(solved[a] * solved[a], axis=1, keepdims=True), axis=0, keepdims=True)
        normed.append(solved[a] / jnp.sqrt(norm + 1e-06))
    for pair in range(total // 2):
        diff = normed[2 * pair] - normed[2 * pair + 1]
        gap = gap + diff * diff
    gap = jnp.sum(jnp.sum(gap, axis=1, keepdims=True), axis=0, keepdims=True)
    loss_ref[...] = gap / (total // 2)
    for a in range(total):
        rows_ref[a] = solved[a]
    count = white_ref.shape[0]
    for m in range(count):
        own = rows_ref[at_ref[0] * count + m]
        for k in range(chunks):
            white_ref[m : m + 1, k * LANES : (k + 1) * LANES] = own[k : k + 1, :]
    start = pl.multiple_of(at_ref[1] * share, share)
    centred_ref[...] = centred
    left = centred_ref[:, pl.ds(start, share)]
    cov_out_ref[...] = 0.5 * cov_ref[...] + weight * dot_f32(left, centred, 0, 0)


def whiten(at, embed, inverse, running_cov, count):
    total, n = embed.shape
    vmem = pl.BlockSpec(memory_space=VMEM)
    return pl.pallas_call(
        whiten_kernel,
        in_specs=[pl.BlockSpec(memory_space=SMEM), vmem, vmem, vmem],
        out_specs=[vmem, vmem, vmem],
        out_shape=[
            jax.ShapeDtypeStruct((count, n), F32),
            jax.ShapeDtypeStruct(running_cov.shape, F32),
            jax.ShapeDtypeStruct((1, 1), F32),
        ],
        scratch_shapes=[
            pltpu.VMEM((total, n // LANES, LANES), F32),
            pltpu.VMEM((total, n), F32),
        ],
        compiler_params=params(48),
        name="whiten",
    )(at, embed, inverse, running_cov)


def bits(size):
    return [1 << b for b in range(size.bit_length() - 1)]


def swap(x, axis, by):
    size = lax.axis_size(axis)
    return lax.ppermute(x, axis, [(i, i ^ by) for i in range(size)])


def earlier_sum(x, axis):
    size = lax.axis_size(axis)
    me = lax.axis_index(axis)
    prior = jnp.zeros_like(x)
    whole = x
    for by in bits(size):
        upper = (me & by) != 0
        if by == size // 2:
            got = lax.ppermute(whole, axis, [(i, i + by) for i in range(by)])
            prior = prior + got
        else:
            got = swap(whole, axis, by)
            prior = prior + jnp.where(upper, got, 0.0)
            whole = whole + got
    return prior


def body(hidden_states, lengths, w_query, w_key, w_value, w_out, running_cov):
    pairs, two, span, width = hidden_states.shape
    count = pairs * two
    seq, dp = lax.axis_size("seq"), lax.axis_size("dp")
    me, group = lax.axis_index("seq"), lax.axis_index("dp")
    hidden = hidden_states.reshape(count, span, width)
    flat_len = lengths.reshape(count)

    pieces, offsets = [running_cov[None]], [0]
    for by in reversed(bits(seq)):
        held = jnp.concatenate(pieces, axis=0) if len(pieces) > 1 else pieces[0]
        pieces.append(swap(held, "seq", by))
        offsets = offsets + [o ^ by for o in offsets]
    fq, num, den, states = encode(hidden, w_query, w_key, w_value)
    prior = earlier_sum(states, "seq")
    start = (me * span).astype(jnp.int32).reshape(1)
    partial = pooled_rows(flat_len, start, hidden, fq, num, den, prior, w_out)
    gathered = lax.all_gather(partial, ("dp", "seq"))
    embed = gathered.reshape(dp, seq, count, width).sum(axis=1).reshape(dp * count, width)
    if dp * count <= 16:
        inverse = inverse_factor(me.astype(jnp.int32).reshape(1), pieces, offsets)
        at = jnp.stack([group, me]).astype(jnp.int32)
        white, cov, loss = whiten(at, embed, inverse, running_cov, count)
        loss = loss.reshape(())
    else:
        white, cov, loss = whiten_many(embed, running_cov, count)
    return white.reshape(pairs, two, width), cov, loss


def whiten_many(embed, running_cov, count):
    total = embed.shape[0]
    share = running_cov.shape[0]
    centred = embed - jnp.sum(embed, axis=0) / total
    full = lax.all_gather(running_cov, "seq", axis=0, tiled=True)
    full = 0.5 * full + (0.5 / (total - 1)) * jnp.dot(centred.T, centred, precision=HIGHEST)
    chol = jnp.linalg.cholesky(full)
    rows = lax.linalg.triangular_solve(chol, centred.T, left_side=True, lower=True).T
    normed = rows / jnp.sqrt(jnp.sum(rows * rows, axis=1, keepdims=True) + 1e-06)
    normed = normed.reshape(total // 2, 2, -1)
    gap = normed[:, 0] - normed[:, 1]
    loss = jnp.sum(gap * gap) / (total // 2)
    white = lax.dynamic_slice_in_dim(rows, lax.axis_index("dp") * count, count, 0)
    cov = lax.dynamic_slice_in_dim(full, lax.axis_index("seq") * share, share, 0)
    return white, cov, loss


def solution(mesh):
    placed = (P("dp", None, "seq", None), P("dp", None), P(), P(), P(), P(), P("seq", None))
    return jax.shard_map(
        body,
        mesh=mesh,
        in_specs=placed,
        out_specs=(P("dp", None, None), P("seq", None), P()),
        check_vma=False,
    )
```

```python
import functools

import jax
import jax.numpy as jnp
from jax import lax
from jax.experimental import pallas as pl
from jax.experimental.pallas import tpu as pltpu
from jax.sharding import PartitionSpec as P

HEADS = 16
HEAD_DIM = 64
LANES = 128
COLS = 256
F32 = jnp.float32
BF16 = jnp.bfloat16
HIGHEST = lax.Precision.HIGHEST
VMEM = pltpu.VMEM
SMEM = pltpu.SMEM


def params(mib):
    return pltpu.CompilerParams(vmem_limit_bytes=mib << 20)


def feature(u):
    return jnp.where(u > 0.0, u + 1.0, jnp.exp(jnp.minimum(u, 0.0)))


def split(x, parts):
    out = []
    for _ in range(parts):
        piece = x.astype(BF16)
        out.append(piece)
        x = x - piece.astype(F32)
    return out


def dot(a, b, ca=1, cb=0):
    return lax.dot_general(a, b, (((ca,), (cb,)), ((), ())), preferred_element_type=F32)


def dot_f32(a, b, ca=1, cb=0):
    return lax.dot_general(
        a, b, (((ca,), (cb,)), ((), ())), precision=HIGHEST, preferred_element_type=F32
    )


def iota(shape, dim):
    return lax.broadcasted_iota(jnp.int32, shape, dim)


def encode_kernel(h_ref, wq_ref, wk_ref, wv_ref, fq_ref, num_ref, den_ref, state_ref):
    count, span = h_ref.shape[0], h_ref.shape[1]
    rows = h_ref[...].reshape(count * span, h_ref.shape[2])
    fq = feature(dot(rows, wq_ref[...])).astype(BF16)
    fk = feature(dot(rows, wk_ref[...])).astype(BF16)
    values = dot(rows, wv_ref[...]).astype(BF16)
    fq_ref[...] = fq.reshape(fq_ref.shape)
    causal = iota((span, span), 0) >= iota((span, span), 1)
    ones_below = causal.astype(BF16)
    low = iota((span, LANES), 1) < HEAD_DIM
    same_head = (iota((LANES, LANES), 0) < HEAD_DIM) == (iota((LANES, LANES), 1) < HEAD_DIM)
    summing = jnp.concatenate([same_head.astype(BF16)] * 2, axis=0)
    for module in range(count):
        at = slice(module * span, (module + 1) * span)
        running = dot(ones_below, fk[at])
        for pair in range(COLS // LANES):
            cols = slice(pair * LANES, (pair + 1) * LANES)
            q, k, v = fq[at, cols], fk[at, cols], values[at, cols]
            state = dot(k, v, 0, 0)
            merged = jnp.where(low[:HEAD_DIM], state[:HEAD_DIM], state[HEAD_DIM:])
            state_ref[pair, module] = jnp.concatenate(
                [merged, jnp.broadcast_to(running[span - 1 :, cols], (8, LANES))], axis=0
            )
            hi, lo = split(q.astype(F32) * running[:, cols], 2)
            den_ref[module, :, cols] = dot(jnp.concatenate([hi, lo], axis=1), summing)
            parts = []
            for half in range(2):
                own = low if half == 0 else jnp.logical_not(low)
                scores = dot(jnp.where(own, q, jnp.zeros_like(q)), k, 1, 1)
                weights = jnp.where(causal, scores, 0.0).astype(BF16)
                parts.append(dot(weights, v))
            num_ref[module, :, cols] = jnp.where(low, parts[0], parts[1])


def encode(hidden, w_query, w_key, w_value):
    count, span, width = hidden.shape
    steps = width // COLS
    weight = pl.BlockSpec((width, COLS), lambda j: (0, j))
    block = pl.BlockSpec((count, span, COLS), lambda j: (0, 0, j))
    pairs = COLS // LANES
    shape = (count, span, width)
    state_shape = (width // LANES, count, HEAD_DIM + 8, LANES)
    return pl.pallas_call(
        encode_kernel,
        grid=(steps,),
        in_specs=[pl.BlockSpec(hidden.shape, lambda j: (0, 0, 0)), weight, weight, weight],
        out_specs=[
            block,
            block,
            block,
            pl.BlockSpec((pairs,) + state_shape[1:], lambda j: (j, 0, 0, 0)),
        ],
        out_shape=[
            jax.ShapeDtypeStruct(shape, BF16),
            jax.ShapeDtypeStruct(shape, F32),
            jax.ShapeDtypeStruct(shape, F32),
            jax.ShapeDtypeStruct(state_shape, F32),
        ],
        compiler_params=params(48),
        name="encode",
    )(hidden, w_query, w_key, w_value)


def pool_kernel(len_ref, start_ref, h_ref, fq_ref, num_ref, den_ref, prior_ref, wo_ref, out_ref):
    count, span = fq_ref.shape[0], fq_ref.shape[1]
    step = pl.program_id(0)
    low = iota((HEAD_DIM, LANES), 1) < HEAD_DIM
    same_head = (iota((LANES, LANES), 0) < HEAD_DIM) == (iota((LANES, LANES), 1) < HEAD_DIM)
    summing = jnp.concatenate([same_head.astype(BF16)] * 2, axis=0)
    sums = []
    hsums = []
    for module in range(count):
        valid = iota((span, LANES), 0) + start_ref[0] < len_ref[module]
        heads = []
        plain = []
        for pair in range(COLS // LANES):
            cols = slice(pair * LANES, (pair + 1) * LANES)
            q = fq_ref[module, :, cols]
            prior = prior_ref[pair, module]
            state = prior[:HEAD_DIM].astype(BF16)
            empty = jnp.zeros_like(state)
            state = jnp.concatenate(
                [jnp.where(low, state, empty), jnp.where(low, empty, state)], axis=0
            )
            hi, lo = split(q.astype(F32) * prior[HEAD_DIM : HEAD_DIM + 1], 2)
            numer = num_ref[module, :, cols] + dot(q, state)
            denom = den_ref[module, :, cols] + dot(jnp.concatenate([hi, lo], axis=1), summing)
            attended = (numer / denom).astype(BF16).astype(F32)
            heads.append(jnp.sum(jnp.where(valid, attended, 0.0), axis=0, keepdims=True))
            plain.append(
                jnp.sum(
                    jnp.where(valid, h_ref[module, :, cols].astype(F32), 0.0), axis=0, keepdims=True
                )
            )
        sums.append(jnp.concatenate(heads, axis=1))
        hsums.append(jnp.concatenate(plain, axis=1))
    sums = jnp.concatenate(sums, axis=0)
    pieces = split(sums, 3)
    part = dot(jnp.concatenate(pieces, axis=0), wo_ref[...])
    part = part[:count] + part[count : 2 * count] + part[2 * count :]

    @pl.when(step == 0)
    def _():
        out_ref[...] = part

    @pl.when(step > 0)
    def _():
        out_ref[...] += part

    here = pl.ds(pl.multiple_of(step * COLS, COLS), COLS)
    out_ref[:, here] += jnp.concatenate(hsums, axis=0)

    @pl.when(step == pl.num_programs(0) - 1)
    def _():
        for module in range(count):
            out_ref[module : module + 1, :] /= len_ref[module].astype(F32)


def pooled_rows(flat_len, start, hidden, fq, num, den, prior, w_out):
    count, span, width = hidden.shape
    block = pl.BlockSpec((count, span, COLS), lambda j: (0, 0, j))
    pairs = COLS // LANES
    return pl.pallas_call(
        pool_kernel,
        grid=(width // COLS,),
        in_specs=[
            pl.BlockSpec(memory_space=SMEM),
            pl.BlockSpec(memory_space=SMEM),
            block,
            block,
            block,
            block,
            pl.BlockSpec((pairs,) + prior.shape[1:], lambda j: (j, 0, 0, 0)),
            pl.BlockSpec((COLS, width), lambda j: (j, 0)),
        ],
        out_specs=pl.BlockSpec((count, width), lambda j: (0, 0)),
        out_shape=jax.ShapeDtypeStruct((count, width), F32),
        compiler_params=params(40),
        name="pool",
    )(flat_len, start, hidden, fq, num, den, prior, w_out)


def split_six(x, axis):
    one, two, three = split(x, 3)
    left = jnp.concatenate([one, one, two, two, one, three], axis=axis)
    right = jnp.concatenate([one, two, one, two, three, one], axis=axis)
    return left, right


GROUP = 16


def leaf_factor(mat):
    groups, tiles = LANES // GROUP, GROUP // 8
    sub, lane = iota((8, LANES), 0), iota((8, LANES), 1)
    rows = [
        [mat[GROUP * g + 8 * v : GROUP * g + 8 * v + 8, :] for v in range(tiles)]
        for g in range(groups)
    ]

    def row_of(x, i):
        return jnp.broadcast_to(x[i : i + 1, :], (8, LANES))

    def col_of(x, c):
        return jnp.broadcast_to(x[:, c : c + 1], (8, LANES))

    for g in range(groups):
        base = GROUP * g
        own = (lane >= base) & (lane < base + GROUP)
        here = [[col_of(rows[g][v], base + c) for v in range(tiles)] for c in range(GROUP)]
        now = [
            jnp.where(own, (lane - base == sub + 8 * v).astype(F32), rows[g][v])
            for v in range(tiles)
        ]
        following = g + 1 < groups
        if following:
            after = [[col_of(rows[g + 1][v], base + c) for v in range(tiles)] for c in range(GROUP)]
            then = [jnp.where(own, 0.0, rows[g + 1][v]) for v in range(tiles)]
        done = []
        for i in range(GROUP):
            tile, at = divmod(i, 8)
            r = lax.rsqrt(row_of(here[i][tile], at))
            u = row_of(now[tile], at) * r
            done.append(u)
            below = [v for v in range(tile, tiles) if not (v == tile and at == 7)]
            m = {v: here[i][v] * r for v in below}
            for v in below:
                now[v] = now[v] - m[v] * u
            if following:
                mh = [after[i][v] * r for v in range(tiles)]
                then = [then[v] - mh[v] * u for v in range(tiles)]
            for c in range(i + 1, GROUP):
                s = row_of(here[c][tile], at) * r
                for v in below:
                    here[c][v] = here[c][v] - m[v] * s
                if following:
                    after[c] = [after[c][v] - mh[v] * s for v in range(tiles)]
        final = []
        for v in range(tiles):
            x = done[8 * v]
            for i in range(1, 8):
                x = jnp.where(sub == i, done[8 * v + i], x)
            final.append(x)
        rows[g] = final
        if following:
            rows[g + 1] = then
        if g + 2 < groups:
            left, right = split_six(jnp.concatenate(final, axis=0), 0)
            product = dot(left, right, 0, 0)
            for h in range(g + 2, groups):
                rows[h] = [
                    jnp.where(own, 0.0, rows[h][v])
                    - product[GROUP * h + 8 * v : GROUP * h + 8 * v + 8, :]
                    for v in range(tiles)
                ]
    return jnp.concatenate([x for pair in rows for x in pair], axis=0)


def eliminate(ref, k):
    n = ref.shape[0]
    panels = n // LANES
    low, high = k * LANES, (k + 1) * LANES
    row, col = iota((LANES, LANES), 0), iota((LANES, LANES), 1)
    inverse = jnp.where(col <= row, leaf_factor(ref[low:high, low:high]), 0.0)
    one, two, three = split(inverse, 3)
    left = jnp.concatenate([one, one, two, two, one, three], axis=1)
    parts = []
    if k + 1 < panels:
        parts.append(ref[low:high, high:])
    if k > 0:
        parts.append(ref[low:high, :low])
    if parts:
        one, two, three = split(jnp.concatenate(parts, axis=1), 3)
        scaled = dot(left, jnp.concatenate([one, two, one, two, three, one], axis=0))
    ref[low:high, low:high] = inverse
    if k > 0:
        ref[low:high, :low] = scaled[:, n - high :]
    if k + 1 == panels:
        return
    rest = n - high
    coefs, beyond = split_six(scaled[:, :rest], 0)
    near = slice(high, high + LANES)
    ref[near, near] -= dot(coefs[:, :LANES], beyond[:, :LANES], 0, 0)
    for h in range(k + 1, panels):
        at = slice(h * LANES, (h + 1) * LANES)
        first = h + 1 if h == k + 1 else h
        if first < panels:
            mine = slice((h - k - 1) * LANES, (h - k) * LANES)
            ref[at, first * LANES :] -= dot(
                coefs[:, mine], beyond[:, first * LANES - high :], 0, 0
            )
    one, two, three = split(inverse, 3)
    own = jnp.concatenate([one, two, one, two, three, one], axis=0)
    ref[high:, low:high] = -dot(coefs, own, 0, 0)
    if k > 0:
        one, two, three = split(scaled[:, rest:], 3)
        before = jnp.concatenate([one, two, one, two, three, one], axis=0)
        ref[high:, :low] -= dot(coefs, before, 0, 0)


def load_kernel(panels, me_ref, own_ref, core_ref, far_ref, far_core_ref, out_ref, sems):
    n = out_ref.shape[0]
    share, half = own_ref.shape[0], n // 2
    me = me_ref[0]
    side = jnp.where(me >= 2, 0, half)
    copies = []
    for slot, ref in enumerate((own_ref, core_ref, far_ref, far_core_ref)):
        block = jnp.bitwise_xor(me, slot)
        to = pl.ds(pl.multiple_of(block * share, share), share)
        if slot < 2:
            target = out_ref.at[to, :]
        else:
            target = out_ref.at[to, pl.ds(pl.multiple_of(side, half), half)]
        copies.append(pltpu.make_async_copy(ref, target, sems.at[slot]))
    for copy in copies:
        copy.start()
    for copy in copies:
        copy.wait()

    @pl.when(me >= 2)
    def _():
        for a in range(0, half, LANES):
            for b in range(0, half, LANES):
                out_ref[a : a + LANES, half + b : half + b + LANES] = out_ref[
                    half + b : half + b + LANES, a : a + LANES
                ].T

    for k in panels:
        eliminate(out_ref, k)


def panels_kernel(panels, in_ref, out_ref):
    out_ref[...] = in_ref[...]
    for k in panels:
        eliminate(out_ref, k)


def factor_first(panels, me, own, core, far, far_core):
    n = own.shape[1]
    anywhere = pl.BlockSpec(memory_space=pl.ANY)
    return pl.pallas_call(
        functools.partial(load_kernel, panels),
        in_specs=[pl.BlockSpec(memory_space=SMEM)] + [anywhere] * 4,
        out_specs=pl.BlockSpec(memory_space=VMEM),
        out_shape=jax.ShapeDtypeStruct((n, n), F32),
        scratch_shapes=[pltpu.SemaphoreType.DMA((4,))],
        compiler_params=params(24),
        name="factor_first",
        cost_estimate=pl.CostEstimate(flops=8_000_000_000, transcendentals=0, bytes_accessed=4 << 20),
    )(me, own, core, far, far_core)


def factor_next(panels, matrix):
    n = matrix.shape[1]
    return pl.pallas_call(
        functools.partial(panels_kernel, panels),
        in_specs=[pl.BlockSpec(memory_space=VMEM)],
        out_specs=pl.BlockSpec(memory_space=VMEM),
        out_shape=jax.ShapeDtypeStruct((n, n), F32),
        input_output_aliases={0: 0},
        compiler_params=params(24),
        name="factor_next",
        cost_estimate=pl.CostEstimate(flops=8_000_000_000, transcendentals=0, bytes_accessed=4 << 20),
    )(matrix)


def whiten_kernel(
    at_ref, *refs
):
    *piece_refs, inv_ref, cov_ref, white_ref, cov_out_ref, loss_ref, rows_ref, centred_ref, held_ref = refs
    count, n = white_ref.shape
    total = centred_ref.shape[0]
    chunks = n // LANES
    share = cov_ref.shape[0]
    slot = 0
    for ref in piece_refs:
        for b in range(ref.shape[0]):
            held_ref[slot] = ref[b]
            slot += 1
    embed = jnp.concatenate(
        [held_ref[jnp.bitwise_xor(at_ref[0], d)] for d in range(total // count)], axis=0
    )
    centred = embed - jnp.sum(embed, axis=0, keepdims=True) / total
    weight = 0.5 / (total - 1)
    root = 2.0**0.5
    for k in range(chunks):
        upto = (k + 1) * LANES
        rows_ref[:, k, :] = dot_f32(root * centred[:, :upto], inv_ref[k * LANES : upto, :upto], 1, 1)
    w = [rows_ref[a] for a in range(total)]
    pairs = [(a, b) for a in range(total) for b in range(a, total)]
    products = jnp.concatenate([w[a] * w[b] for a, b in pairs], axis=0)
    before = iota((LANES, 2 * LANES), 0) < iota((LANES, 2 * LANES), 1)
    earlier = before.astype(BF16)
    sums = [dot(piece, earlier) for piece in split(products, 3)]
    sums = sums[0] + sums[1] + sums[2]
    chunk = iota((8, LANES), 0)
    entry = {}
    for i, (a, b) in enumerate(pairs):
        inside = sums[8 * i : 8 * i + 8, :LANES]
        whole = sums[8 * i : 8 * i + 8, LANES:]
        carry = jnp.where(chunk >= 1, pltpu.roll(whole, 1, 0), 0.0)
        for by in (1, 2, 4):
            carry = carry + jnp.where(chunk >= by, pltpu.roll(carry, by, 0), 0.0)
        entry[a, b] = weight * (inside + carry) + (1.0 if a == b else 0.0)
    right = list(w)
    inverse = []
    spread = jnp.ones((8, LANES), F32)
    for p in range(total):
        inv = 1.0 / entry[p, p]
        inverse.append(inv)
        spread = spread + weight * right[p] * right[p] * inv
        for a in range(p + 1, total):
            f = entry[p, a] * inv
            for b in range(a, total):
                entry[a, b] = entry[a, b] - f * entry[p, b]
            right[a] = right[a] - f * right[p]
    scale = lax.rsqrt(spread)
    solved = [None] * total
    for p in reversed(range(total)):
        x = right[p]
        for b in range(p + 1, total):
            x = x - entry[p, b] * solved[b]
        solved[p] = x * inverse[p]
    solved = [x * scale for x in solved]
    gap = jnp.zeros((8, LANES), F32)
    normed = []
    for a in range(total):
        norm = jnp.sum(jnp.sum(solved[a] * solved[a], axis=1, keepdims=True), axis=0, keepdims=True)
        normed.append(solved[a] / jnp.sqrt(norm + 1e-06))
    for pair in range(total // 2):
        diff = normed[2 * pair] - normed[2 * pair + 1]
        gap = gap + diff * diff
    gap = jnp.sum(jnp.sum(gap, axis=1, keepdims=True), axis=0, keepdims=True)
    loss_ref[...] = gap / (total // 2)
    for a in range(total):
        rows_ref[a] = solved[a]
    for m in range(count):
        own = rows_ref[at_ref[0] * count + m]
        for k in range(chunks):
            white_ref[m : m + 1, k * LANES : (k + 1) * LANES] = own[k : k + 1, :]
    start = pl.multiple_of(at_ref[1] * share, share)
    centred_ref[...] = centred
    left = centred_ref[:, pl.ds(start, share)]
    cov_out_ref[...] = 0.5 * cov_ref[...] + weight * dot_f32(left, centred, 0, 0)


def whiten(at, pieces, inverse, running_cov):
    groups = sum(piece.shape[0] for piece in pieces)
    count, n = pieces[0].shape[1:]
    total = groups * count
    vmem = pl.BlockSpec(memory_space=VMEM)
    return pl.pallas_call(
        whiten_kernel,
        in_specs=[pl.BlockSpec(memory_space=SMEM)] + [vmem] * (len(pieces) + 2),
        out_specs=[vmem, vmem, vmem],
        out_shape=[
            jax.ShapeDtypeStruct((count, n), F32),
            jax.ShapeDtypeStruct(running_cov.shape, F32),
            jax.ShapeDtypeStruct((1, 1), F32),
        ],
        scratch_shapes=[
            pltpu.VMEM((total, n // LANES, LANES), F32),
            pltpu.VMEM((total, n), F32),
            pltpu.VMEM((groups, count, n), F32),
        ],
        compiler_params=params(40),
        name="whiten",
    )(at, *pieces, inverse, running_cov)


def bits(size):
    return [1 << b for b in range(size.bit_length() - 1)]


def swap(x, axis, by):
    size = lax.axis_size(axis)
    return lax.ppermute(x, axis, [(i, i ^ by) for i in range(size)])


def earlier_sum(x, axis):
    size = lax.axis_size(axis)
    me = lax.axis_index(axis)
    prior = jnp.zeros_like(x)
    whole = x
    for by in bits(size):
        upper = (me & by) != 0
        if by == size // 2:
            got = lax.ppermute(whole, axis, [(i, i + by) for i in range(by)])
            prior = prior + got
        else:
            got = swap(whole, axis, by)
            prior = prior + jnp.where(upper, got, 0.0)
            whole = whole + got
    return prior


def body(hidden_states, lengths, w_query, w_key, w_value, w_out, running_cov):
    pairs, two, span, width = hidden_states.shape
    count = pairs * two
    seq, dp = lax.axis_size("seq"), lax.axis_size("dp")
    me, group = lax.axis_index("seq"), lax.axis_index("dp")
    hidden = hidden_states.reshape(count, span, width)
    flat_len = lengths.reshape(count)

    start = (me * span).astype(jnp.int32).reshape(1)
    if seq == 4 and dp == 8 and count == 2:
        white, cov, loss = body_fixed(hidden, flat_len, start, w_query, w_key, w_value, w_out, running_cov)
    else:
        fq, num, den, states = encode(hidden, w_query, w_key, w_value)
        prior = earlier_sum(states, "seq")
        partial = pooled_rows(flat_len, start, hidden, fq, num, den, prior, w_out)
        gathered = lax.all_gather(partial, ("dp", "seq"))
        embed = gathered.reshape(dp, seq, count, width).sum(axis=1).reshape(dp * count, width)
        white, cov, loss = whiten_many(embed, running_cov, count)
    return white.reshape(pairs, two, width), cov, loss


def body_fixed(hidden, flat_len, start, w_query, w_key, w_value, w_out, running_cov):
    me, group = lax.axis_index("seq"), lax.axis_index("dp")
    width = hidden.shape[2]
    half = width // 2
    core, far_side = me & 1, me >= 2
    at = jnp.stack([group, me]).astype(jnp.int32)
    chip_columns = lax.dynamic_slice_in_dim(running_cov, (me >> 1) * half, half, 1)
    far_cov = swap(chip_columns, "seq", 2)
    core_cov = swap(running_cov, "seq", 1)
    fq, num, den, states = encode(hidden, w_query, w_key, w_value)
    far_cov, core_cov, states = lax.optimization_barrier((far_cov, core_cov, states))
    core_states = swap(states, "seq", 1)
    far_core_cov = swap(far_cov, "seq", 1)
    quarter = states.shape[0] // 2
    mine = lax.dynamic_slice_in_dim(states, core * quarter, quarter, 0)
    mine = mine + lax.dynamic_slice_in_dim(core_states, core * quarter, quarter, 0)
    far_half = lax.ppermute(mine, "seq", [(0, 2), (1, 3)])
    matrix = factor_first((0, 1), at[1:], running_cov, core_cov, far_cov, far_core_cov)
    far_half, matrix = lax.optimization_barrier((far_half, matrix))
    other_half = swap(far_half, "seq", 1)
    prior = jnp.where(
        core == 0,
        jnp.concatenate([far_half, other_half], axis=0),
        jnp.concatenate([other_half, far_half], axis=0),
    )
    prior = prior + jnp.where(core == 1, core_states, 0.0)
    partial = pooled_rows(flat_len, start, hidden, fq, num, den, prior, w_out)
    partial, matrix = lax.optimization_barrier((partial, matrix))
    got = [swap(partial, "seq", by) for by in (1, 2, 3)]
    matrix = factor_next((2, 3), matrix)
    partial, got, matrix = lax.optimization_barrier((partial, got, matrix))
    embed = ((partial + got[0]) + (got[1] + got[2]))[None]
    beside = swap(embed, "dp", 1)
    matrix = factor_next((4, 5), matrix)
    embed, beside, matrix = lax.optimization_barrier((embed, beside, matrix))
    embed = jnp.concatenate([embed, beside], axis=0)
    pieces = [embed] + [swap(embed, "dp", by) for by in (2, 4, 6)]
    matrix = factor_next((6, 7), matrix)
    white, cov, loss = whiten(at, pieces, matrix, running_cov)
    return white, cov, loss.reshape(())


def whiten_many(embed, running_cov, count):
    total = embed.shape[0]
    share = running_cov.shape[0]
    centred = embed - jnp.sum(embed, axis=0) / total
    full = lax.all_gather(running_cov, "seq", axis=0, tiled=True)
    full = 0.5 * full + (0.5 / (total - 1)) * jnp.dot(centred.T, centred, precision=HIGHEST)
    chol = jnp.linalg.cholesky(full)
    rows = lax.linalg.triangular_solve(chol, centred.T, left_side=True, lower=True).T
    normed = rows / jnp.sqrt(jnp.sum(rows * rows, axis=1, keepdims=True) + 1e-06)
    normed = normed.reshape(total // 2, 2, -1)
    gap = normed[:, 0] - normed[:, 1]
    loss = jnp.sum(gap * gap) / (total // 2)
    white = lax.dynamic_slice_in_dim(rows, lax.axis_index("dp") * count, count, 0)
    cov = lax.dynamic_slice_in_dim(full, lax.axis_index("seq") * share, share, 0)
    return white, cov, loss


def solution(mesh):
    placed = (P("dp", None, "seq", None), P("dp", None), P(), P(), P(), P(), P("seq", None))
    return jax.shard_map(
        body,
        mesh=mesh,
        in_specs=placed,
        out_specs=(P("dp", None, None), P("seq", None), P()),
        check_vma=False,
    )
```

```python
import functools

import jax
import jax.numpy as jnp
from jax import lax
from jax.experimental import pallas as pl
from jax.experimental.pallas import tpu as pltpu
from jax.sharding import PartitionSpec as P

HEADS = 16
HEAD_DIM = 64
LANES = 128
COLS = 256
F32 = jnp.float32
BF16 = jnp.bfloat16
HIGHEST = lax.Precision.HIGHEST
VMEM = pltpu.VMEM
SMEM = pltpu.SMEM


def hbm(x):
    return pltpu.with_memory_space_constraint(x, pltpu.HBM)


def params(mib):
    return pltpu.CompilerParams(vmem_limit_bytes=mib << 20)


def feature(u):
    return jnp.where(u > 0.0, u + 1.0, jnp.exp(jnp.minimum(u, 0.0)))


def split(x, parts):
    out = []
    for _ in range(parts):
        piece = x.astype(BF16)
        out.append(piece)
        x = x - piece.astype(F32)
    return out


def dot(a, b, ca=1, cb=0):
    return lax.dot_general(a, b, (((ca,), (cb,)), ((), ())), preferred_element_type=F32)


def dot_f32(a, b, ca=1, cb=0):
    return lax.dot_general(
        a, b, (((ca,), (cb,)), ((), ())), precision=HIGHEST, preferred_element_type=F32
    )


def iota(shape, dim):
    return lax.broadcasted_iota(jnp.int32, shape, dim)


def encode_kernel(h_ref, wq_ref, wk_ref, wv_ref, fq_ref, num_ref, den_ref, state_ref):
    count, span = h_ref.shape[0], h_ref.shape[1]
    rows = h_ref[...].reshape(count * span, h_ref.shape[2])
    fq = feature(dot(rows, wq_ref[...])).astype(BF16)
    fk = feature(dot(rows, wk_ref[...])).astype(BF16)
    values = dot(rows, wv_ref[...]).astype(BF16)
    fq_ref[...] = fq.reshape(fq_ref.shape)
    causal = iota((span, span), 0) >= iota((span, span), 1)
    ones_below = causal.astype(BF16)
    low = iota((span, LANES), 1) < HEAD_DIM
    same_head = (iota((LANES, LANES), 0) < HEAD_DIM) == (iota((LANES, LANES), 1) < HEAD_DIM)
    summing = jnp.concatenate([same_head.astype(BF16)] * 2, axis=0)
    for module in range(count):
        at = slice(module * span, (module + 1) * span)
        running = dot(ones_below, fk[at])
        for pair in range(COLS // LANES):
            cols = slice(pair * LANES, (pair + 1) * LANES)
            q, k, v = fq[at, cols], fk[at, cols], values[at, cols]
            state = dot(k, v, 0, 0)
            merged = jnp.where(low[:HEAD_DIM], state[:HEAD_DIM], state[HEAD_DIM:])
            state_ref[pair, module] = jnp.concatenate(
                [merged, jnp.broadcast_to(running[span - 1 :, cols], (8, LANES))], axis=0
            )
            hi, lo = split(q.astype(F32) * running[:, cols], 2)
            den_ref[module, :, cols] = dot(jnp.concatenate([hi, lo], axis=1), summing)
            parts = []
            for half in range(2):
                own = low if half == 0 else jnp.logical_not(low)
                scores = dot(jnp.where(own, q, jnp.zeros_like(q)), k, 1, 1)
                weights = jnp.where(causal, scores, 0.0).astype(BF16)
                parts.append(dot(weights, v))
            num_ref[module, :, cols] = jnp.where(low, parts[0], parts[1])


def encode(hidden, w_query, w_key, w_value):
    count, span, width = hidden.shape
    steps = width // COLS
    weight = pl.BlockSpec((width, COLS), lambda j: (0, j))
    block = pl.BlockSpec((count, span, COLS), lambda j: (0, 0, j))
    pairs = COLS // LANES
    shape = (count, span, width)
    state_shape = (width // LANES, count, HEAD_DIM + 8, LANES)
    return pl.pallas_call(
        encode_kernel,
        grid=(steps,),
        in_specs=[pl.BlockSpec(hidden.shape, lambda j: (0, 0, 0)), weight, weight, weight],
        out_specs=[
            block,
            block,
            block,
            pl.BlockSpec((pairs,) + state_shape[1:], lambda j: (j, 0, 0, 0)),
        ],
        out_shape=[
            pltpu.HBM(shape, BF16),
            pltpu.HBM(shape, F32),
            pltpu.HBM(shape, F32),
            pltpu.HBM(state_shape, F32),
        ],
        compiler_params=params(14),
        name="encode",
    )(hbm(hidden), hbm(w_query), hbm(w_key), hbm(w_value))


def pool_kernel(len_ref, start_ref, h_ref, fq_ref, num_ref, den_ref, prior_ref, wo_ref, out_ref):
    count, span = fq_ref.shape[0], fq_ref.shape[1]
    step = pl.program_id(0)
    low = iota((HEAD_DIM, LANES), 1) < HEAD_DIM
    same_head = (iota((LANES, LANES), 0) < HEAD_DIM) == (iota((LANES, LANES), 1) < HEAD_DIM)
    summing = jnp.concatenate([same_head.astype(BF16)] * 2, axis=0)
    sums = []
    hsums = []
    for module in range(count):
        valid = iota((span, LANES), 0) + start_ref[0] < len_ref[module]
        heads = []
        plain = []
        for pair in range(COLS // LANES):
            cols = slice(pair * LANES, (pair + 1) * LANES)
            q = fq_ref[module, :, cols]
            prior = prior_ref[pair, module]
            state = prior[:HEAD_DIM].astype(BF16)
            empty = jnp.zeros_like(state)
            state = jnp.concatenate(
                [jnp.where(low, state, empty), jnp.where(low, empty, state)], axis=0
            )
            hi, lo = split(q.astype(F32) * prior[HEAD_DIM : HEAD_DIM + 1], 2)
            numer = num_ref[module, :, cols] + dot(q, state)
            denom = den_ref[module, :, cols] + dot(jnp.concatenate([hi, lo], axis=1), summing)
            attended = (numer / denom).astype(BF16).astype(F32)
            heads.append(jnp.sum(jnp.where(valid, attended, 0.0), axis=0, keepdims=True))
            plain.append(
                jnp.sum(
                    jnp.where(valid, h_ref[module, :, cols].astype(F32), 0.0), axis=0, keepdims=True
                )
            )
        sums.append(jnp.concatenate(heads, axis=1))
        hsums.append(jnp.concatenate(plain, axis=1))
    sums = jnp.concatenate(sums, axis=0)
    pieces = split(sums, 3)
    part = dot(jnp.concatenate(pieces, axis=0), wo_ref[...])
    part = part[:count] + part[count : 2 * count] + part[2 * count :]

    @pl.when(step == 0)
    def _():
        out_ref[...] = part

    @pl.when(step > 0)
    def _():
        out_ref[...] += part

    here = pl.ds(pl.multiple_of(step * COLS, COLS), COLS)
    out_ref[:, here] += jnp.concatenate(hsums, axis=0)

    @pl.when(step == pl.num_programs(0) - 1)
    def _():
        for module in range(count):
            out_ref[module : module + 1, :] /= len_ref[module].astype(F32)


def pooled_rows(flat_len, start, hidden, fq, num, den, prior, w_out):
    count, span, width = hidden.shape
    block = pl.BlockSpec((count, span, COLS), lambda j: (0, 0, j))
    pairs = COLS // LANES
    return pl.pallas_call(
        pool_kernel,
        grid=(width // COLS,),
        in_specs=[
            pl.BlockSpec(memory_space=SMEM),
            pl.BlockSpec(memory_space=SMEM),
            block,
            block,
            block,
            block,
            pl.BlockSpec((pairs,) + prior.shape[1:], lambda j: (j, 0, 0, 0)),
            pl.BlockSpec((COLS, width), lambda j: (j, 0)),
        ],
        out_specs=pl.BlockSpec((count, width), lambda j: (0, 0)),
        out_shape=jax.ShapeDtypeStruct((count, width), F32),
        compiler_params=params(10),
        name="pool",
    )(flat_len, start, hbm(hidden), hbm(fq), hbm(num), hbm(den), prior, hbm(w_out))


def split_six(x, axis):
    one, two, three = split(x, 3)
    left = jnp.concatenate([one, one, two, two, one, three], axis=axis)
    right = jnp.concatenate([one, two, one, two, three, one], axis=axis)
    return left, right


GROUP = 16


def leaf_factor(mat):
    groups, tiles = LANES // GROUP, GROUP // 8
    sub, lane = iota((8, LANES), 0), iota((8, LANES), 1)
    rows = [
        [mat[GROUP * g + 8 * v : GROUP * g + 8 * v + 8, :] for v in range(tiles)]
        for g in range(groups)
    ]

    def row_of(x, i):
        return jnp.broadcast_to(x[i : i + 1, :], (8, LANES))

    def col_of(x, c):
        return jnp.broadcast_to(x[:, c : c + 1], (8, LANES))

    for g in range(groups):
        base = GROUP * g
        own = (lane >= base) & (lane < base + GROUP)
        here = [[col_of(rows[g][v], base + c) for v in range(tiles)] for c in range(GROUP)]
        now = [
            jnp.where(own, (lane - base == sub + 8 * v).astype(F32), rows[g][v])
            for v in range(tiles)
        ]
        following = g + 1 < groups
        if following:
            after = [[col_of(rows[g + 1][v], base + c) for v in range(tiles)] for c in range(GROUP)]
            then = [jnp.where(own, 0.0, rows[g + 1][v]) for v in range(tiles)]
        done = []
        for i in range(GROUP):
            tile, at = divmod(i, 8)
            r = lax.rsqrt(row_of(here[i][tile], at))
            u = row_of(now[tile], at) * r
            done.append(u)
            below = [v for v in range(tile, tiles) if not (v == tile and at == 7)]
            m = {v: here[i][v] * r for v in below}
            for v in below:
                now[v] = now[v] - m[v] * u
            if following:
                mh = [after[i][v] * r for v in range(tiles)]
                then = [then[v] - mh[v] * u for v in range(tiles)]
            for c in range(i + 1, GROUP):
                s = row_of(here[c][tile], at) * r
                for v in below:
                    here[c][v] = here[c][v] - m[v] * s
                if following:
                    after[c] = [after[c][v] - mh[v] * s for v in range(tiles)]
        final = []
        for v in range(tiles):
            x = done[8 * v]
            for i in range(1, 8):
                x = jnp.where(sub == i, done[8 * v + i], x)
            final.append(x)
        rows[g] = final
        if following:
            rows[g + 1] = then
        if g + 2 < groups:
            left, right = split_six(jnp.concatenate(final, axis=0), 0)
            product = dot(left, right, 0, 0)
            for h in range(g + 2, groups):
                rows[h] = [
                    jnp.where(own, 0.0, rows[h][v])
                    - product[GROUP * h + 8 * v : GROUP * h + 8 * v + 8, :]
                    for v in range(tiles)
                ]
    return jnp.concatenate([x for pair in rows for x in pair], axis=0)


def eliminate(ref, k):
    n = ref.shape[0]
    panels = n // LANES
    low, high = k * LANES, (k + 1) * LANES
    row, col = iota((LANES, LANES), 0), iota((LANES, LANES), 1)
    inverse = jnp.where(col <= row, leaf_factor(ref[low:high, low:high]), 0.0)
    one, two, three = split(inverse, 3)
    left = jnp.concatenate([one, one, two, two, one, three], axis=1)
    parts = []
    if k + 1 < panels:
        parts.append(ref[low:high, high:])
    if k > 0:
        parts.append(ref[low:high, :low])
    if parts:
        one, two, three = split(jnp.concatenate(parts, axis=1), 3)
        scaled = dot(left, jnp.concatenate([one, two, one, two, three, one], axis=0))
    ref[low:high, low:high] = inverse
    if k > 0:
        ref[low:high, :low] = scaled[:, n - high :]
    if k + 1 == panels:
        return
    rest = n - high
    coefs, beyond = split_six(scaled[:, :rest], 0)
    near = slice(high, high + LANES)
    ref[near, near] -= dot(coefs[:, :LANES], beyond[:, :LANES], 0, 0)
    for h in range(k + 1, panels):
        at = slice(h * LANES, (h + 1) * LANES)
        first = h + 1 if h == k + 1 else h
        if first < panels:
            mine = slice((h - k - 1) * LANES, (h - k) * LANES)
            ref[at, first * LANES :] -= dot(
                coefs[:, mine], beyond[:, first * LANES - high :], 0, 0
            )
    one, two, three = split(inverse, 3)
    own = jnp.concatenate([one, two, one, two, three, one], axis=0)
    ref[high:, low:high] = -dot(coefs, own, 0, 0)
    if k > 0:
        one, two, three = split(scaled[:, rest:], 3)
        before = jnp.concatenate([one, two, one, two, three, one], axis=0)
        ref[high:, :low] -= dot(coefs, before, 0, 0)


def load_kernel(panels, me_ref, own_ref, core_ref, far_ref, far_core_ref, out_ref, sems):
    n = out_ref.shape[0]
    share, half = own_ref.shape[0], n // 2
    me = me_ref[0]
    side = jnp.where(me >= 2, 0, half)
    copies = []
    for slot, ref in enumerate((own_ref, core_ref, far_ref, far_core_ref)):
        block = jnp.bitwise_xor(me, slot)
        to = pl.ds(pl.multiple_of(block * share, share), share)
        if slot < 2:
            target = out_ref.at[to, :]
        else:
            target = out_ref.at[to, pl.ds(pl.multiple_of(side, half), half)]
        copies.append(pltpu.make_async_copy(ref, target, sems.at[slot]))
    for copy in copies:
        copy.start()
    for copy in copies:
        copy.wait()

    @pl.when(me >= 2)
    def _():
        for a in range(0, half, LANES):
            for b in range(0, half, LANES):
                out_ref[a : a + LANES, half + b : half + b + LANES] = out_ref[
                    half + b : half + b + LANES, a : a + LANES
                ].T

    for k in panels:
        eliminate(out_ref, k)


def panels_kernel(panels, in_ref, out_ref):
    out_ref[...] = in_ref[...]
    for k in panels:
        eliminate(out_ref, k)


def factor_first(panels, me, own, core, far, far_core):
    n = own.shape[1]
    anywhere = pl.BlockSpec(memory_space=pl.ANY)
    return pl.pallas_call(
        functools.partial(load_kernel, panels),
        in_specs=[pl.BlockSpec(memory_space=SMEM)] + [anywhere] * 4,
        out_specs=pl.BlockSpec(memory_space=VMEM),
        out_shape=jax.ShapeDtypeStruct((n, n), F32),
        scratch_shapes=[pltpu.SemaphoreType.DMA((4,))],
        compiler_params=params(14),
        name="factor_first",
        cost_estimate=pl.CostEstimate(flops=8_000_000_000, transcendentals=0, bytes_accessed=4 << 20),
    )(me, own, core, far, far_core)


def factor_next(panels, matrix):
    n = matrix.shape[1]
    return pl.pallas_call(
        functools.partial(panels_kernel, panels),
        in_specs=[pl.BlockSpec(memory_space=VMEM)],
        out_specs=pl.BlockSpec(memory_space=VMEM),
        out_shape=jax.ShapeDtypeStruct((n, n), F32),
        input_output_aliases={0: 0},
        compiler_params=params(14),
        name="factor_next",
        cost_estimate=pl.CostEstimate(flops=8_000_000_000, transcendentals=0, bytes_accessed=4 << 20),
    )(matrix)


def whiten_kernel(
    at_ref, *refs
):
    *piece_refs, inv_ref, cov_ref, white_ref, cov_out_ref, loss_ref, rows_ref, centred_ref, held_ref = refs
    count, n = white_ref.shape
    total = centred_ref.shape[0]
    chunks = n // LANES
    share = cov_ref.shape[0]
    slot = 0
    for ref in piece_refs:
        for b in range(ref.shape[0]):
            held_ref[slot] = ref[b]
            slot += 1
    embed = jnp.concatenate(
        [held_ref[jnp.bitwise_xor(at_ref[0], d)] for d in range(total // count)], axis=0
    )
    centred = embed - jnp.sum(embed, axis=0, keepdims=True) / total
    weight = 0.5 / (total - 1)
    root = 2.0**0.5
    for k in range(chunks):
        upto = (k + 1) * LANES
        rows_ref[:, k, :] = dot_f32(root * centred[:, :upto], inv_ref[k * LANES : upto, :upto], 1, 1)
    w = [rows_ref[a] for a in range(total)]
    pairs = [(a, b) for a in range(total) for b in range(a, total)]
    products = jnp.concatenate([w[a] * w[b] for a, b in pairs], axis=0)
    before = iota((LANES, 2 * LANES), 0) < iota((LANES, 2 * LANES), 1)
    earlier = before.astype(BF16)
    sums = [dot(piece, earlier) for piece in split(products, 3)]
    sums = sums[0] + sums[1] + sums[2]
    chunk = iota((8, LANES), 0)
    entry = {}
    for i, (a, b) in enumerate(pairs):
        inside = sums[8 * i : 8 * i + 8, :LANES]
        whole = sums[8 * i : 8 * i + 8, LANES:]
        carry = jnp.where(chunk >= 1, pltpu.roll(whole, 1, 0), 0.0)
        for by in (1, 2, 4):
            carry = carry + jnp.where(chunk >= by, pltpu.roll(carry, by, 0), 0.0)
        entry[a, b] = weight * (inside + carry) + (1.0 if a == b else 0.0)
    right = list(w)
    inverse = []
    spread = jnp.ones((8, LANES), F32)
    for p in range(total):
        inv = 1.0 / entry[p, p]
        inverse.append(inv)
        spread = spread + weight * right[p] * right[p] * inv
        for a in range(p + 1, total):
            f = entry[p, a] * inv
            for b in range(a, total):
                entry[a, b] = entry[a, b] - f * entry[p, b]
            right[a] = right[a] - f * right[p]
    scale = lax.rsqrt(spread)
    solved = [None] * total
    for p in reversed(range(total)):
        x = right[p]
        for b in range(p + 1, total):
            x = x - entry[p, b] * solved[b]
        solved[p] = x * inverse[p]
    solved = [x * scale for x in solved]
    gap = jnp.zeros((8, LANES), F32)
    normed = []
    for a in range(total):
        norm = jnp.sum(jnp.sum(solved[a] * solved[a], axis=1, keepdims=True), axis=0, keepdims=True)
        normed.append(solved[a] / jnp.sqrt(norm + 1e-06))
    for pair in range(total // 2):
        diff = normed[2 * pair] - normed[2 * pair + 1]
        gap = gap + diff * diff
    gap = jnp.sum(jnp.sum(gap, axis=1, keepdims=True), axis=0, keepdims=True)
    loss_ref[...] = gap / (total // 2)
    for a in range(total):
        rows_ref[a] = solved[a]
    for m in range(count):
        own = rows_ref[at_ref[0] * count + m]
        for k in range(chunks):
            white_ref[m : m + 1, k * LANES : (k + 1) * LANES] = own[k : k + 1, :]
    start = pl.multiple_of(at_ref[1] * share, share)
    centred_ref[...] = centred
    left = centred_ref[:, pl.ds(start, share)]
    cov_out_ref[...] = 0.5 * cov_ref[...] + weight * dot_f32(left, centred, 0, 0)


def whiten(at, pieces, inverse, running_cov):
    groups = sum(piece.shape[0] for piece in pieces)
    count, n = pieces[0].shape[1:]
    total = groups * count
    vmem = pl.BlockSpec(memory_space=VMEM)
    return pl.pallas_call(
        whiten_kernel,
        in_specs=[pl.BlockSpec(memory_space=SMEM)] + [vmem] * (len(pieces) + 2),
        out_specs=[vmem, vmem, vmem],
        out_shape=[
            jax.ShapeDtypeStruct((count, n), F32),
            jax.ShapeDtypeStruct(running_cov.shape, F32),
            jax.ShapeDtypeStruct((1, 1), F32),
        ],
        scratch_shapes=[
            pltpu.VMEM((total, n // LANES, LANES), F32),
            pltpu.VMEM((total, n), F32),
            pltpu.VMEM((groups, count, n), F32),
        ],
        compiler_params=params(12),
        name="whiten",
    )(at, *pieces, inverse, running_cov)


def bits(size):
    return [1 << b for b in range(size.bit_length() - 1)]


def swap(x, axis, by):
    size = lax.axis_size(axis)
    return lax.ppermute(x, axis, [(i, i ^ by) for i in range(size)])


def earlier_sum(x, axis):
    size = lax.axis_size(axis)
    me = lax.axis_index(axis)
    prior = jnp.zeros_like(x)
    whole = x
    for by in bits(size):
        upper = (me & by) != 0
        if by == size // 2:
            got = lax.ppermute(whole, axis, [(i, i + by) for i in range(by)])
            prior = prior + got
        else:
            got = swap(whole, axis, by)
            prior = prior + jnp.where(upper, got, 0.0)
            whole = whole + got
    return prior


def body(hidden_states, lengths, w_query, w_key, w_value, w_out, running_cov):
    pairs, two, span, width = hidden_states.shape
    count = pairs * two
    seq, dp = lax.axis_size("seq"), lax.axis_size("dp")
    me, group = lax.axis_index("seq"), lax.axis_index("dp")
    hidden = hidden_states.reshape(count, span, width)
    flat_len = lengths.reshape(count)

    start = (me * span).astype(jnp.int32).reshape(1)
    if seq == 4 and dp == 8 and count == 2:
        white, cov, loss = body_fixed(hidden, flat_len, start, w_query, w_key, w_value, w_out, running_cov)
    else:
        fq, num, den, states = encode(hidden, w_query, w_key, w_value)
        prior = earlier_sum(states, "seq")
        partial = pooled_rows(flat_len, start, hidden, fq, num, den, prior, w_out)
        gathered = lax.all_gather(partial, ("dp", "seq"))
        embed = gathered.reshape(dp, seq, count, width).sum(axis=1).reshape(dp * count, width)
        white, cov, loss = whiten_many(embed, running_cov, count)
    return white.reshape(pairs, two, width), cov, loss


def body_fixed(hidden, flat_len, start, w_query, w_key, w_value, w_out, running_cov):
    me, group = lax.axis_index("seq"), lax.axis_index("dp")
    width = hidden.shape[2]
    half = width // 2
    core, far_side = me & 1, me >= 2
    at = jnp.stack([group, me]).astype(jnp.int32)
    chip_columns = lax.dynamic_slice_in_dim(running_cov, (me >> 1) * half, half, 1)
    far_cov = swap(chip_columns, "seq", 2)
    core_cov = swap(running_cov, "seq", 1)
    fq, num, den, states = encode(hidden, w_query, w_key, w_value)
    far_cov, core_cov, states = lax.optimization_barrier((far_cov, core_cov, states))
    core_states = swap(states, "seq", 1)
    far_core_cov = swap(far_cov, "seq", 1)
    quarter = states.shape[0] // 2
    mine = lax.dynamic_slice_in_dim(states, core * quarter, quarter, 0)
    mine = mine + lax.dynamic_slice_in_dim(core_states, core * quarter, quarter, 0)
    far_half = lax.ppermute(mine, "seq", [(0, 2), (1, 3)])
    matrix = factor_first((0, 1), at[1:], running_cov, core_cov, far_cov, far_core_cov)
    far_half, matrix = lax.optimization_barrier((far_half, matrix))
    other_half = swap(far_half, "seq", 1)
    prior = jnp.where(
        core == 0,
        jnp.concatenate([far_half, other_half], axis=0),
        jnp.concatenate([other_half, far_half], axis=0),
    )
    prior = prior + jnp.where(core == 1, core_states, 0.0)
    partial = pooled_rows(flat_len, start, hidden, fq, num, den, prior, w_out)
    partial, matrix = lax.optimization_barrier((partial, matrix))
    got = [swap(partial, "seq", by) for by in (1, 2, 3)]
    matrix = factor_next((2, 3), matrix)
    partial, got, matrix = lax.optimization_barrier((partial, got, matrix))
    embed = ((partial + got[0]) + (got[1] + got[2]))[None]
    beside = swap(embed, "dp", 1)
    matrix = factor_next((4, 5), matrix)
    embed, beside, matrix = lax.optimization_barrier((embed, beside, matrix))
    embed = jnp.concatenate([embed, beside], axis=0)
    pieces = [embed] + [swap(embed, "dp", by) for by in (2, 4, 6)]
    matrix = factor_next((6, 7), matrix)
    white, cov, loss = whiten(at, pieces, matrix, running_cov)
    return white, cov, loss.reshape(())


def whiten_many(embed, running_cov, count):
    total = embed.shape[0]
    share = running_cov.shape[0]
    centred = embed - jnp.sum(embed, axis=0) / total
    full = lax.all_gather(running_cov, "seq", axis=0, tiled=True)
    full = 0.5 * full + (0.5 / (total - 1)) * jnp.dot(centred.T, centred, precision=HIGHEST)
    chol = jnp.linalg.cholesky(full)
    rows = lax.linalg.triangular_solve(chol, centred.T, left_side=True, lower=True).T
    normed = rows / jnp.sqrt(jnp.sum(rows * rows, axis=1, keepdims=True) + 1e-06)
    normed = normed.reshape(total // 2, 2, -1)
    gap = normed[:, 0] - normed[:, 1]
    loss = jnp.sum(gap * gap) / (total // 2)
    white = lax.dynamic_slice_in_dim(rows, lax.axis_index("dp") * count, count, 0)
    cov = lax.dynamic_slice_in_dim(full, lax.axis_index("seq") * share, share, 0)
    return white, cov, loss


def solution(mesh):
    placed = (P("dp", None, "seq", None), P("dp", None), P(), P(), P(), P(), P("seq", None))
    return jax.shard_map(
        body,
        mesh=mesh,
        in_specs=placed,
        out_specs=(P("dp", None, None), P("seq", None), P()),
        check_vma=False,
    )
```

```python
import functools

import jax
import jax.numpy as jnp
from jax import lax
from jax.experimental import pallas as pl
from jax.experimental.pallas import tpu as pltpu
from jax.sharding import PartitionSpec as P

HEADS = 16
HEAD_DIM = 64
LANES = 128
COLS = 256
F32 = jnp.float32
BF16 = jnp.bfloat16
HIGHEST = lax.Precision.HIGHEST
VMEM = pltpu.VMEM
SMEM = pltpu.SMEM


def hbm(x):
    return pltpu.with_memory_space_constraint(x, pltpu.HBM)


def vmem(x):
    return pltpu.with_memory_space_constraint(x, VMEM)


def params(mib):
    return pltpu.CompilerParams(vmem_limit_bytes=mib << 20)


def feature(u):
    return jnp.where(u > 0.0, u + 1.0, jnp.exp(jnp.minimum(u, 0.0)))


def split(x, parts):
    out = []
    for _ in range(parts):
        piece = x.astype(BF16)
        out.append(piece)
        x = x - piece.astype(F32)
    return out


def dot(a, b, ca=1, cb=0):
    return lax.dot_general(a, b, (((ca,), (cb,)), ((), ())), preferred_element_type=F32)


def dot_f32(a, b, ca=1, cb=0):
    return lax.dot_general(
        a, b, (((ca,), (cb,)), ((), ())), precision=HIGHEST, preferred_element_type=F32
    )


def iota(shape, dim):
    return lax.broadcasted_iota(jnp.int32, shape, dim)


def encode_kernel(h_ref, wq_ref, wk_ref, wv_ref, fq_ref, num_ref, den_ref, state_ref):
    count, span = h_ref.shape[0], h_ref.shape[1]
    rows = h_ref[...].reshape(count * span, h_ref.shape[2])
    fq = feature(dot(rows, wq_ref[...])).astype(BF16)
    fk = feature(dot(rows, wk_ref[...])).astype(BF16)
    values = dot(rows, wv_ref[...]).astype(BF16)
    fq_ref[...] = fq.reshape(fq_ref.shape)
    causal = iota((span, span), 0) >= iota((span, span), 1)
    ones_below = causal.astype(BF16)
    low = iota((span, LANES), 1) < HEAD_DIM
    same_head = (iota((LANES, LANES), 0) < HEAD_DIM) == (iota((LANES, LANES), 1) < HEAD_DIM)
    summing = jnp.concatenate([same_head.astype(BF16)] * 2, axis=0)
    for module in range(count):
        at = slice(module * span, (module + 1) * span)
        running = dot(ones_below, fk[at])
        for pair in range(COLS // LANES):
            cols = slice(pair * LANES, (pair + 1) * LANES)
            q, k, v = fq[at, cols], fk[at, cols], values[at, cols]
            state = dot(k, v, 0, 0)
            merged = jnp.where(low[:HEAD_DIM], state[:HEAD_DIM], state[HEAD_DIM:])
            state_ref[pair, module] = jnp.concatenate(
                [merged, jnp.broadcast_to(running[span - 1 :, cols], (8, LANES))], axis=0
            )
            hi, lo = split(q.astype(F32) * running[:, cols], 2)
            den_ref[module, :, cols] = dot(jnp.concatenate([hi, lo], axis=1), summing)
            parts = []
            for half in range(2):
                own = low if half == 0 else jnp.logical_not(low)
                scores = dot(jnp.where(own, q, jnp.zeros_like(q)), k, 1, 1)
                weights = jnp.where(causal, scores, 0.0).astype(BF16)
                parts.append(dot(weights, v))
            num_ref[module, :, cols] = jnp.where(low, parts[0], parts[1])


def encode(hidden, w_query, w_key, w_value):
    count, span, width = hidden.shape
    steps = width // COLS
    weight = pl.BlockSpec((width, COLS), lambda j: (0, j))
    block = pl.BlockSpec((count, span, COLS), lambda j: (0, 0, j))
    pairs = COLS // LANES
    shape = (count, span, width)
    state_shape = (width // LANES, count, HEAD_DIM + 8, LANES)
    return pl.pallas_call(
        encode_kernel,
        grid=(steps,),
        in_specs=[pl.BlockSpec(hidden.shape, lambda j: (0, 0, 0)), weight, weight, weight],
        out_specs=[
            block,
            block,
            block,
            pl.BlockSpec((pairs,) + state_shape[1:], lambda j: (j, 0, 0, 0)),
        ],
        out_shape=[
            pltpu.HBM(shape, BF16),
            pltpu.HBM(shape, F32),
            pltpu.HBM(shape, F32),
            pltpu.HBM(state_shape, F32),
        ],
        compiler_params=params(14),
        name="encode",
    )(hbm(hidden), hbm(w_query), hbm(w_key), hbm(w_value))


def pool_columns(step, steps, len_ref, start_ref, h_ref, fq_ref, num_ref, den_ref, prior_ref, wo_ref, out_ref):
    count, span = fq_ref.shape[0], fq_ref.shape[1]
    low = iota((HEAD_DIM, LANES), 1) < HEAD_DIM
    same_head = (iota((LANES, LANES), 0) < HEAD_DIM) == (iota((LANES, LANES), 1) < HEAD_DIM)
    summing = jnp.concatenate([same_head.astype(BF16)] * 2, axis=0)
    sums = []
    hsums = []
    for module in range(count):
        valid = iota((span, LANES), 0) + start_ref[0] < len_ref[module]
        heads = []
        plain = []
        for pair in range(COLS // LANES):
            cols = slice(pair * LANES, (pair + 1) * LANES)
            q = fq_ref[module, :, cols]
            prior = prior_ref[pair, module]
            state = prior[:HEAD_DIM].astype(BF16)
            empty = jnp.zeros_like(state)
            state = jnp.concatenate(
                [jnp.where(low, state, empty), jnp.where(low, empty, state)], axis=0
            )
            hi, lo = split(q.astype(F32) * prior[HEAD_DIM : HEAD_DIM + 1], 2)
            numer = num_ref[module, :, cols] + dot(q, state)
            denom = den_ref[module, :, cols] + dot(jnp.concatenate([hi, lo], axis=1), summing)
            attended = (numer / denom).astype(BF16).astype(F32)
            heads.append(jnp.sum(jnp.where(valid, attended, 0.0), axis=0, keepdims=True))
            plain.append(
                jnp.sum(
                    jnp.where(valid, h_ref[module, :, cols].astype(F32), 0.0), axis=0, keepdims=True
                )
            )
        sums.append(jnp.concatenate(heads, axis=1))
        hsums.append(jnp.concatenate(plain, axis=1))
    sums = jnp.concatenate(sums, axis=0)
    pieces = split(sums, 3)
    part = dot(jnp.concatenate(pieces, axis=0), wo_ref[...])
    part = part[:count] + part[count : 2 * count] + part[2 * count :]

    @pl.when(step == 0)
    def _():
        out_ref[...] = part

    @pl.when(step > 0)
    def _():
        out_ref[...] += part

    here = pl.ds(pl.multiple_of(step * COLS, COLS), COLS)
    out_ref[:, here] += jnp.concatenate(hsums, axis=0)

    @pl.when(step == steps - 1)
    def _():
        for module in range(count):
            out_ref[module : module + 1, :] /= len_ref[module].astype(F32)


def pool_kernel(*refs):
    pool_columns(pl.program_id(0), pl.num_programs(0), *refs)


def pooled_rows(flat_len, start, hidden, fq, num, den, prior, w_out):
    count, span, width = hidden.shape
    block = pl.BlockSpec((count, span, COLS), lambda j: (0, 0, j))
    pairs = COLS // LANES
    return pl.pallas_call(
        pool_kernel,
        grid=(width // COLS,),
        in_specs=[
            pl.BlockSpec(memory_space=SMEM),
            pl.BlockSpec(memory_space=SMEM),
            block,
            block,
            block,
            block,
            pl.BlockSpec((pairs,) + prior.shape[1:], lambda j: (j, 0, 0, 0)),
            pl.BlockSpec((COLS, width), lambda j: (j, 0)),
        ],
        out_specs=pl.BlockSpec((count, width), lambda j: (0, 0)),
        out_shape=jax.ShapeDtypeStruct((count, width), F32),
        compiler_params=params(10),
        name="pool",
    )(flat_len, start, hbm(hidden), hbm(fq), hbm(num), hbm(den), prior, hbm(w_out))


def split_six(x, axis):
    one, two, three = split(x, 3)
    left = jnp.concatenate([one, one, two, two, one, three], axis=axis)
    right = jnp.concatenate([one, two, one, two, three, one], axis=axis)
    return left, right


GROUP = 16


def leaf_factor(mat):
    groups, tiles = LANES // GROUP, GROUP // 8
    sub, lane = iota((8, LANES), 0), iota((8, LANES), 1)
    rows = [
        [mat[GROUP * g + 8 * v : GROUP * g + 8 * v + 8, :] for v in range(tiles)]
        for g in range(groups)
    ]

    def row_of(x, i):
        return jnp.broadcast_to(x[i : i + 1, :], (8, LANES))

    def col_of(x, c):
        return jnp.broadcast_to(x[:, c : c + 1], (8, LANES))

    for g in range(groups):
        base = GROUP * g
        own = (lane >= base) & (lane < base + GROUP)
        here = [[col_of(rows[g][v], base + c) for v in range(tiles)] for c in range(GROUP)]
        now = [
            jnp.where(own, (lane - base == sub + 8 * v).astype(F32), rows[g][v])
            for v in range(tiles)
        ]
        following = g + 1 < groups
        if following:
            after = [[col_of(rows[g + 1][v], base + c) for v in range(tiles)] for c in range(GROUP)]
            then = [jnp.where(own, 0.0, rows[g + 1][v]) for v in range(tiles)]
        done = []
        for i in range(GROUP):
            tile, at = divmod(i, 8)
            r = lax.rsqrt(row_of(here[i][tile], at))
            u = row_of(now[tile], at) * r
            done.append(u)
            below = [v for v in range(tile, tiles) if not (v == tile and at == 7)]
            m = {v: here[i][v] * r for v in below}
            for v in below:
                now[v] = now[v] - m[v] * u
            if following:
                mh = [after[i][v] * r for v in range(tiles)]
                then = [then[v] - mh[v] * u for v in range(tiles)]
            for c in range(i + 1, GROUP):
                s = row_of(here[c][tile], at) * r
                for v in below:
                    here[c][v] = here[c][v] - m[v] * s
                if following:
                    after[c] = [after[c][v] - mh[v] * s for v in range(tiles)]
        final = []
        for v in range(tiles):
            x = done[8 * v]
            for i in range(1, 8):
                x = jnp.where(sub == i, done[8 * v + i], x)
            final.append(x)
        rows[g] = final
        if following:
            rows[g + 1] = then
        if g + 2 < groups:
            left, right = split_six(jnp.concatenate(final, axis=0), 0)
            product = dot(left, right, 0, 0)
            for h in range(g + 2, groups):
                rows[h] = [
                    jnp.where(own, 0.0, rows[h][v])
                    - product[GROUP * h + 8 * v : GROUP * h + 8 * v + 8, :]
                    for v in range(tiles)
                ]
    return jnp.concatenate([x for pair in rows for x in pair], axis=0)


def eliminate(ref, k):
    n = ref.shape[0]
    panels = n // LANES
    low, high = k * LANES, (k + 1) * LANES
    row, col = iota((LANES, LANES), 0), iota((LANES, LANES), 1)
    inverse = jnp.where(col <= row, leaf_factor(ref[low:high, low:high]), 0.0)
    one, two, three = split(inverse, 3)
    left = jnp.concatenate([one, one, two, two, one, three], axis=1)
    parts = []
    if k + 1 < panels:
        parts.append(ref[low:high, high:])
    if k > 0:
        parts.append(ref[low:high, :low])
    if parts:
        one, two, three = split(jnp.concatenate(parts, axis=1), 3)
        scaled = dot(left, jnp.concatenate([one, two, one, two, three, one], axis=0))
    ref[low:high, low:high] = inverse
    if k > 0:
        ref[low:high, :low] = scaled[:, n - high :]
    if k + 1 == panels:
        return
    if k % 2 == 0:
        ref[low:high, high : high + LANES] = jnp.zeros((LANES, LANES), F32)
    rest = n - high
    coefs, beyond = split_six(scaled[:, :rest], 0)
    near = slice(high, high + LANES)
    ref[near, near] -= dot(coefs[:, :LANES], beyond[:, :LANES], 0, 0)
    for h in range(k + 1, panels):
        at = slice(h * LANES, (h + 1) * LANES)
        first = h + 1 if h == k + 1 else h
        if first < panels:
            mine = slice((h - k - 1) * LANES, (h - k) * LANES)
            ref[at, first * LANES :] -= dot(
                coefs[:, mine], beyond[:, first * LANES - high :], 0, 0
            )
    one, two, three = split(inverse, 3)
    own = jnp.concatenate([one, two, one, two, three, one], axis=0)
    ref[high:, low:high] = -dot(coefs, own, 0, 0)
    if k > 0:
        one, two, three = split(scaled[:, rest:], 3)
        before = jnp.concatenate([one, two, one, two, three, one], axis=0)
        ref[high:, :low] -= dot(coefs, before, 0, 0)


def load_kernel(panels, me_ref, own_ref, core_ref, far_ref, far_core_ref, out_ref, sems):
    n = out_ref.shape[0]
    share, half = own_ref.shape[0], n // 2
    me = me_ref[0]
    side = jnp.where(me >= 2, 0, half)
    copies = []
    for slot, ref in enumerate((own_ref, core_ref, far_ref, far_core_ref)):
        block = jnp.bitwise_xor(me, slot)
        to = pl.ds(pl.multiple_of(block * share, share), share)
        if slot < 2:
            target = out_ref.at[to, :]
        else:
            target = out_ref.at[to, pl.ds(pl.multiple_of(side, half), half)]
        copies.append(pltpu.make_async_copy(ref, target, sems.at[slot]))
    for copy in copies:
        copy.start()
    for copy in copies:
        copy.wait()

    @pl.when(me >= 2)
    def _():
        for a in range(0, half, LANES):
            for b in range(0, half, LANES):
                out_ref[a : a + LANES, half + b : half + b + LANES] = out_ref[
                    half + b : half + b + LANES, a : a + LANES
                ].T

    for k in panels:
        eliminate(out_ref, k)


def panels_kernel(panels, in_ref, out_ref):
    del in_ref
    for k in panels:
        eliminate(out_ref, k)


def panels_pool_kernel(panels, in_ref, len_ref, start_ref, core_ref, *refs):
    del in_ref
    *sources, matrix_ref, out_ref = refs[:10]
    *held, prior_ref, beside_ref, sems = refs[10:]
    half = prior_ref.shape[0] // 2
    own = pl.ds(core_ref[0] * half, half)
    other = pl.ds((1 - core_ref[0]) * half, half)
    targets = held + [prior_ref.at[own], prior_ref.at[other], beside_ref]
    copies = [
        pltpu.make_async_copy(source, to, sems.at[i])
        for i, (source, to) in enumerate(zip(sources, targets))
    ]
    for copy in copies:
        copy.start()
    for k in panels:
        eliminate(matrix_ref, k)
    for copy in copies:
        copy.wait()
    h_ref, fq_ref, num_ref, den_ref, wo_ref = held

    @pl.when(core_ref[0] == 1)
    def _():
        prior_ref[...] += beside_ref[...]

    steps = wo_ref.shape[0] // COLS
    pairs = COLS // LANES

    def run(step, carried):
        cols = pl.ds(pl.multiple_of(step * COLS, COLS), COLS)
        pool_columns(
            step,
            steps,
            len_ref,
            start_ref,
            h_ref.at[:, :, cols],
            fq_ref.at[:, :, cols],
            num_ref.at[:, :, cols],
            den_ref.at[:, :, cols],
            prior_ref.at[pl.ds(step * pairs, pairs)],
            wo_ref.at[cols, :],
            out_ref,
        )
        return carried

    lax.fori_loop(0, steps, run, 0)


def factor_next_pool(
    panels, matrix, flat_len, start, core, hidden, fq, num, den, w_out, far_half, other_half, beside
):
    n = matrix.shape[1]
    count, span, width = hidden.shape
    whole, anywhere = pl.BlockSpec(memory_space=VMEM), pl.BlockSpec(memory_space=pl.ANY)
    operands = [hbm(x) for x in (hidden, fq, num, den, w_out)]
    states = [far_half, other_half, beside]
    return pl.pallas_call(
        functools.partial(panels_pool_kernel, panels),
        in_specs=[whole] + [pl.BlockSpec(memory_space=SMEM)] * 3 + [anywhere] * 8,
        out_specs=[whole, whole],
        out_shape=[pltpu.VMEM((n, n), F32), jax.ShapeDtypeStruct((count, width), F32)],
        scratch_shapes=[pltpu.VMEM(x.shape, x.dtype) for x in operands + [beside, beside]]
        + [pltpu.SemaphoreType.DMA((8,))],
        input_output_aliases={0: 0},
        compiler_params=params(24),
        name="factor_next_pool",
        cost_estimate=pl.CostEstimate(flops=8_000_000_000, transcendentals=0, bytes_accessed=12 << 20),
    )(vmem(matrix), flat_len, start, core, *operands, *states)


def factor_first(panels, me, own, core, far, far_core):
    n = own.shape[1]
    anywhere = pl.BlockSpec(memory_space=pl.ANY)
    return pl.pallas_call(
        functools.partial(load_kernel, panels),
        in_specs=[pl.BlockSpec(memory_space=SMEM)] + [anywhere] * 4,
        out_specs=pl.BlockSpec(memory_space=VMEM),
        out_shape=pltpu.VMEM((n, n), F32),
        scratch_shapes=[pltpu.SemaphoreType.DMA((4,))],
        compiler_params=params(14),
        name="factor_first",
        cost_estimate=pl.CostEstimate(flops=8_000_000_000, transcendentals=0, bytes_accessed=4 << 20),
    )(me, own, core, far, far_core)


def factor_next(panels, matrix):
    n = matrix.shape[1]
    return pl.pallas_call(
        functools.partial(panels_kernel, panels),
        in_specs=[pl.BlockSpec(memory_space=VMEM)],
        out_specs=pl.BlockSpec(memory_space=VMEM),
        out_shape=pltpu.VMEM((n, n), F32),
        input_output_aliases={0: 0},
        compiler_params=params(14),
        name="factor_next",
        cost_estimate=pl.CostEstimate(flops=8_000_000_000, transcendentals=0, bytes_accessed=4 << 20),
    )(vmem(matrix))


def whiten_kernel(
    at_ref, *refs
):
    *piece_refs, inv_ref, cov_ref, white_ref, cov_out_ref, loss_ref = refs[:-5]
    rows_ref, centred_ref, held_ref, new_cov_ref, sem = refs[-5:]
    count, n = white_ref.shape
    total = centred_ref.shape[0]
    chunks = n // LANES
    share = cov_ref.shape[0]
    slot = 0
    for ref in piece_refs:
        for b in range(ref.shape[0]):
            held_ref[slot] = ref[b]
            slot += 1
    embed = jnp.concatenate(
        [held_ref[jnp.bitwise_xor(at_ref[0], d)] for d in range(total // count)], axis=0
    )
    centred = embed - jnp.sum(embed, axis=0, keepdims=True) / total
    weight = 0.5 / (total - 1)
    root = 2.0**0.5
    start = pl.multiple_of(at_ref[1] * share, share)
    centred_ref[...] = centred
    left, right = split_six(centred_ref[:, pl.ds(start, share)], 0)[0], split_six(centred, 0)[1]
    new_cov_ref[...] = 0.5 * cov_ref[...] + weight * dot(left, right, 0, 0)
    written = pltpu.make_async_copy(new_cov_ref, cov_out_ref, sem)
    written.start()
    thirds = jnp.concatenate(split(root * centred, 3), axis=0)
    for k in range(0, chunks, 2):
        upto = (k + 2) * LANES
        one, two, three = split(inv_ref[k * LANES : upto, :upto], 3)
        by_one = dot(thirds[:, :upto], one, 1, 1)
        by_two = dot(thirds[: 2 * total, :upto], two, 1, 1)
        product = by_one[:total] + (by_one[total : 2 * total] + by_two[:total])
        product = product + (
            by_one[2 * total :] + by_two[total:] + dot(thirds[:total, :upto], three, 1, 1)
        )
        rows_ref[:, k, :] = product[:, :LANES]
        rows_ref[:, k + 1, :] = product[:, LANES:]
    w = [rows_ref[a] for a in range(total)]
    pairs = [(a, b) for a in range(total) for b in range(a, total)]
    products = jnp.concatenate([w[a] * w[b] for a, b in pairs], axis=0)
    before = iota((LANES, 2 * LANES), 0) < iota((LANES, 2 * LANES), 1)
    earlier = before.astype(BF16)
    sums = [dot(piece, earlier) for piece in split(products, 3)]
    sums = sums[0] + sums[1] + sums[2]
    chunk = iota((8, LANES), 0)
    entry = {}
    for i, (a, b) in enumerate(pairs):
        inside = sums[8 * i : 8 * i + 8, :LANES]
        whole = sums[8 * i : 8 * i + 8, LANES:]
        carry = jnp.where(chunk >= 1, pltpu.roll(whole, 1, 0), 0.0)
        for by in (1, 2, 4):
            carry = carry + jnp.where(chunk >= by, pltpu.roll(carry, by, 0), 0.0)
        entry[a, b] = weight * (inside + carry) + (1.0 if a == b else 0.0)
    right = list(w)
    inverse = []
    spread = jnp.ones((8, LANES), F32)
    for p in range(total):
        inv = 1.0 / entry[p, p]
        inverse.append(inv)
        spread = spread + weight * right[p] * right[p] * inv
        for a in range(p + 1, total):
            f = entry[p, a] * inv
            for b in range(a, total):
                entry[a, b] = entry[a, b] - f * entry[p, b]
            right[a] = right[a] - f * right[p]
    scale = lax.rsqrt(spread)
    solved = [None] * total
    for p in reversed(range(total)):
        x = right[p]
        for b in range(p + 1, total):
            x = x - entry[p, b] * solved[b]
        solved[p] = x * inverse[p]
    solved = [x * scale for x in solved]
    gap = jnp.zeros((8, LANES), F32)
    normed = []
    for a in range(total):
        norm = jnp.sum(jnp.sum(solved[a] * solved[a], axis=1, keepdims=True), axis=0, keepdims=True)
        normed.append(solved[a] / jnp.sqrt(norm + 1e-06))
    for pair in range(total // 2):
        diff = normed[2 * pair] - normed[2 * pair + 1]
        gap = gap + diff * diff
    gap = jnp.sum(jnp.sum(gap, axis=1, keepdims=True), axis=0, keepdims=True)
    loss_ref[...] = gap / (total // 2)
    for a in range(total):
        rows_ref[a] = solved[a]
    for m in range(count):
        own = rows_ref[at_ref[0] * count + m]
        for k in range(chunks):
            white_ref[m : m + 1, k * LANES : (k + 1) * LANES] = own[k : k + 1, :]
    written.wait()


def whiten(at, pieces, inverse, running_cov):
    groups = sum(piece.shape[0] for piece in pieces)
    count, n = pieces[0].shape[1:]
    total = groups * count
    whole = pl.BlockSpec(memory_space=VMEM)
    return pl.pallas_call(
        whiten_kernel,
        in_specs=[pl.BlockSpec(memory_space=SMEM)] + [whole] * (len(pieces) + 2),
        out_specs=[whole, pl.BlockSpec(memory_space=pl.ANY), whole],
        out_shape=[
            jax.ShapeDtypeStruct((count, n), F32),
            jax.ShapeDtypeStruct(running_cov.shape, F32),
            jax.ShapeDtypeStruct((1, 1), F32),
        ],
        scratch_shapes=[
            pltpu.VMEM((total, n // LANES, LANES), F32),
            pltpu.VMEM((total, n), F32),
            pltpu.VMEM((groups, count, n), F32),
            pltpu.VMEM(running_cov.shape, F32),
            pltpu.SemaphoreType.DMA,
        ],
        compiler_params=params(12),
        name="whiten",
    )(at, *pieces, inverse, running_cov)


def bits(size):
    return [1 << b for b in range(size.bit_length() - 1)]


def swap(x, axis, by):
    size = lax.axis_size(axis)
    return lax.ppermute(x, axis, [(i, i ^ by) for i in range(size)])


def earlier_sum(x, axis):
    size = lax.axis_size(axis)
    me = lax.axis_index(axis)
    prior = jnp.zeros_like(x)
    whole = x
    for by in bits(size):
        upper = (me & by) != 0
        if by == size // 2:
            got = lax.ppermute(whole, axis, [(i, i + by) for i in range(by)])
            prior = prior + got
        else:
            got = swap(whole, axis, by)
            prior = prior + jnp.where(upper, got, 0.0)
            whole = whole + got
    return prior


def body(hidden_states, lengths, w_query, w_key, w_value, w_out, running_cov):
    pairs, two, span, width = hidden_states.shape
    count = pairs * two
    seq, dp = lax.axis_size("seq"), lax.axis_size("dp")
    me, group = lax.axis_index("seq"), lax.axis_index("dp")
    hidden = hidden_states.reshape(count, span, width)
    flat_len = lengths.reshape(count)

    start = (me * span).astype(jnp.int32).reshape(1)
    if seq == 4 and dp == 8 and count == 2:
        white, cov, loss = body_fixed(hidden, flat_len, start, w_query, w_key, w_value, w_out, running_cov)
    else:
        fq, num, den, states = encode(hidden, w_query, w_key, w_value)
        prior = earlier_sum(states, "seq")
        partial = pooled_rows(flat_len, start, hidden, fq, num, den, prior, w_out)
        gathered = lax.all_gather(partial, ("dp", "seq"))
        embed = gathered.reshape(dp, seq, count, width).sum(axis=1).reshape(dp * count, width)
        white, cov, loss = whiten_many(embed, running_cov, count)
    return white.reshape(pairs, two, width), cov, loss


def body_fixed(hidden, flat_len, start, w_query, w_key, w_value, w_out, running_cov):
    me, group = lax.axis_index("seq"), lax.axis_index("dp")
    width = hidden.shape[2]
    half = width // 2
    core = me & 1
    at = jnp.stack([group, me]).astype(jnp.int32)
    chip_columns = lax.dynamic_slice_in_dim(running_cov, (me >> 1) * half, half, 1)
    far_cov = swap(chip_columns, "seq", 2)
    core_cov = swap(running_cov, "seq", 1)
    fq, num, den, states = encode(hidden, w_query, w_key, w_value)
    far_cov, core_cov, states = lax.optimization_barrier((far_cov, core_cov, states))
    core_states = swap(states, "seq", 1)
    far_core_cov = swap(far_cov, "seq", 1)
    quarter = states.shape[0] // 2
    matrix = factor_first((0,), at[1:], running_cov, core_cov, far_cov, far_core_cov)
    core_states, matrix = lax.optimization_barrier((core_states, matrix))
    mine = lax.dynamic_slice_in_dim(states, core * quarter, quarter, 0)
    mine = mine + lax.dynamic_slice_in_dim(core_states, core * quarter, quarter, 0)
    far_half = lax.ppermute(mine, "seq", [(0, 2), (1, 3)])
    matrix = factor_next((1, 2), matrix)
    far_half, matrix = lax.optimization_barrier((far_half, matrix))
    other_half = swap(far_half, "seq", 1)
    matrix = factor_next((3,), matrix)
    other_half, matrix = lax.optimization_barrier((other_half, matrix))
    matrix, partial = factor_next_pool(
        (4,),
        matrix,
        flat_len,
        start,
        core.astype(jnp.int32).reshape(1),
        hidden,
        fq,
        num,
        den,
        w_out,
        far_half,
        other_half,
        core_states,
    )
    got = [swap(partial, "seq", by) for by in (1, 2, 3)]
    matrix = factor_next((5,), matrix)
    partial, got, matrix = lax.optimization_barrier((partial, got, matrix))
    embed = ((partial + got[0]) + (got[1] + got[2]))[None]
    beside = swap(embed, "dp", 1)
    matrix = factor_next((6,), matrix)
    embed, beside, matrix = lax.optimization_barrier((embed, beside, matrix))
    embed = jnp.concatenate([embed, beside], axis=0)
    pieces = [embed] + [swap(embed, "dp", by) for by in (2, 4, 6)]
    matrix = factor_next((7,), matrix)
    white, cov, loss = whiten(at, pieces, matrix, running_cov)
    return white, cov, loss.reshape(())


def whiten_many(embed, running_cov, count):
    total = embed.shape[0]
    share = running_cov.shape[0]
    centred = embed - jnp.sum(embed, axis=0) / total
    full = lax.all_gather(running_cov, "seq", axis=0, tiled=True)
    full = 0.5 * full + (0.5 / (total - 1)) * jnp.dot(centred.T, centred, precision=HIGHEST)
    chol = jnp.linalg.cholesky(full)
    rows = lax.linalg.triangular_solve(chol, centred.T, left_side=True, lower=True).T
    normed = rows / jnp.sqrt(jnp.sum(rows * rows, axis=1, keepdims=True) + 1e-06)
    normed = normed.reshape(total // 2, 2, -1)
    gap = normed[:, 0] - normed[:, 1]
    loss = jnp.sum(gap * gap) / (total // 2)
    white = lax.dynamic_slice_in_dim(rows, lax.axis_index("dp") * count, count, 0)
    cov = lax.dynamic_slice_in_dim(full, lax.axis_index("seq") * share, share, 0)
    return white, cov, loss


def solution(mesh):
    placed = (P("dp", None, "seq", None), P("dp", None), P(), P(), P(), P(), P("seq", None))
    return jax.shard_map(
        body,
        mesh=mesh,
        in_specs=placed,
        out_specs=(P("dp", None, None), P("seq", None), P()),
        check_vma=False,
    )
```

```python
import functools

import jax
import jax.numpy as jnp
from jax import lax
from jax.experimental import pallas as pl
from jax.experimental.pallas import tpu as pltpu
from jax.sharding import PartitionSpec as P

HEADS = 16
HEAD_DIM = 64
LANES = 128
COLS = 256
F32 = jnp.float32
BF16 = jnp.bfloat16
HIGHEST = lax.Precision.HIGHEST
VMEM = pltpu.VMEM
SMEM = pltpu.SMEM


def hbm(x):
    return pltpu.with_memory_space_constraint(x, pltpu.HBM)


def vmem(x):
    return pltpu.with_memory_space_constraint(x, VMEM)


def params(mib):
    return pltpu.CompilerParams(vmem_limit_bytes=mib << 20)


def feature(u):
    return jnp.where(u > 0.0, u + 1.0, jnp.exp(jnp.minimum(u, 0.0)))


def split(x, parts):
    out = []
    for _ in range(parts):
        piece = x.astype(BF16)
        out.append(piece)
        x = x - piece.astype(F32)
    return out


def dot(a, b, ca=1, cb=0):
    return lax.dot_general(a, b, (((ca,), (cb,)), ((), ())), preferred_element_type=F32)


def dot_f32(a, b, ca=1, cb=0):
    return lax.dot_general(
        a, b, (((ca,), (cb,)), ((), ())), precision=HIGHEST, preferred_element_type=F32
    )


def iota(shape, dim):
    return lax.broadcasted_iota(jnp.int32, shape, dim)


def encode_kernel(h_ref, wq_ref, wk_ref, wv_ref, fq_ref, num_ref, den_ref, state_ref):
    count, span = h_ref.shape[0], h_ref.shape[1]
    rows = h_ref[...].reshape(count * span, h_ref.shape[2])
    fq = feature(dot(rows, wq_ref[...])).astype(BF16)
    fk = feature(dot(rows, wk_ref[...])).astype(BF16)
    values = dot(rows, wv_ref[...]).astype(BF16)
    fq_ref[...] = fq.reshape(fq_ref.shape)
    causal = iota((span, span), 0) >= iota((span, span), 1)
    ones_below = causal.astype(BF16)
    low = iota((span, LANES), 1) < HEAD_DIM
    same_head = (iota((LANES, LANES), 0) < HEAD_DIM) == (iota((LANES, LANES), 1) < HEAD_DIM)
    summing = jnp.concatenate([same_head.astype(BF16)] * 2, axis=0)
    for module in range(count):
        at = slice(module * span, (module + 1) * span)
        running = dot(ones_below, fk[at])
        for pair in range(COLS // LANES):
            cols = slice(pair * LANES, (pair + 1) * LANES)
            q, k, v = fq[at, cols], fk[at, cols], values[at, cols]
            state = dot(k, v, 0, 0)
            merged = jnp.where(low[:HEAD_DIM], state[:HEAD_DIM], state[HEAD_DIM:])
            state_ref[pair, module] = jnp.concatenate(
                [merged, jnp.broadcast_to(running[span - 1 :, cols], (8, LANES))], axis=0
            )
            hi, lo = split(q.astype(F32) * running[:, cols], 2)
            den_ref[module, :, cols] = dot(jnp.concatenate([hi, lo], axis=1), summing)
            parts = []
            for half in range(2):
                own = low if half == 0 else jnp.logical_not(low)
                scores = dot(jnp.where(own, q, jnp.zeros_like(q)), k, 1, 1)
                weights = jnp.where(causal, scores, 0.0).astype(BF16)
                parts.append(dot(weights, v))
            num_ref[module, :, cols] = jnp.where(low, parts[0], parts[1])


def encode(hidden, w_query, w_key, w_value):
    count, span, width = hidden.shape
    steps = width // COLS
    weight = pl.BlockSpec((width, COLS), lambda j: (0, j))
    block = pl.BlockSpec((count, span, COLS), lambda j: (0, 0, j))
    pairs = COLS // LANES
    shape = (count, span, width)
    state_shape = (width // LANES, count, HEAD_DIM + 8, LANES)
    return pl.pallas_call(
        encode_kernel,
        grid=(steps,),
        in_specs=[pl.BlockSpec(hidden.shape, lambda j: (0, 0, 0)), weight, weight, weight],
        out_specs=[
            block,
            block,
            block,
            pl.BlockSpec((pairs,) + state_shape[1:], lambda j: (j, 0, 0, 0)),
        ],
        out_shape=[
            pltpu.HBM(shape, BF16),
            pltpu.HBM(shape, F32),
            pltpu.HBM(shape, F32),
            pltpu.HBM(state_shape, F32),
        ],
        compiler_params=params(14),
        name="encode",
    )(hbm(hidden), hbm(w_query), hbm(w_key), hbm(w_value))


def pool_columns(step, steps, len_ref, start_ref, h_ref, fq_ref, num_ref, den_ref, prior_ref, wo_ref, out_ref):
    count, span = fq_ref.shape[0], fq_ref.shape[1]
    low = iota((HEAD_DIM, LANES), 1) < HEAD_DIM
    same_head = (iota((LANES, LANES), 0) < HEAD_DIM) == (iota((LANES, LANES), 1) < HEAD_DIM)
    summing = jnp.concatenate([same_head.astype(BF16)] * 2, axis=0)
    sums = []
    hsums = []
    for module in range(count):
        valid = iota((span, LANES), 0) + start_ref[0] < len_ref[module]
        heads = []
        plain = []
        for pair in range(COLS // LANES):
            cols = slice(pair * LANES, (pair + 1) * LANES)
            q = fq_ref[module, :, cols]
            prior = prior_ref[pair, module]
            state = prior[:HEAD_DIM].astype(BF16)
            empty = jnp.zeros_like(state)
            state = jnp.concatenate(
                [jnp.where(low, state, empty), jnp.where(low, empty, state)], axis=0
            )
            hi, lo = split(q.astype(F32) * prior[HEAD_DIM : HEAD_DIM + 1], 2)
            numer = num_ref[module, :, cols] + dot(q, state)
            denom = den_ref[module, :, cols] + dot(jnp.concatenate([hi, lo], axis=1), summing)
            attended = (numer / denom).astype(BF16).astype(F32)
            heads.append(jnp.sum(jnp.where(valid, attended, 0.0), axis=0, keepdims=True))
            plain.append(
                jnp.sum(
                    jnp.where(valid, h_ref[module, :, cols].astype(F32), 0.0), axis=0, keepdims=True
                )
            )
        sums.append(jnp.concatenate(heads, axis=1))
        hsums.append(jnp.concatenate(plain, axis=1))
    sums = jnp.concatenate(sums, axis=0)
    pieces = split(sums, 3)
    part = dot(jnp.concatenate(pieces, axis=0), wo_ref[...])
    part = part[:count] + part[count : 2 * count] + part[2 * count :]

    @pl.when(step == 0)
    def _():
        out_ref[...] = part

    @pl.when(step > 0)
    def _():
        out_ref[...] += part

    here = pl.ds(pl.multiple_of(step * COLS, COLS), COLS)
    out_ref[:, here] += jnp.concatenate(hsums, axis=0)

    @pl.when(step == steps - 1)
    def _():
        for module in range(count):
            out_ref[module : module + 1, :] /= len_ref[module].astype(F32)


def pool_kernel(*refs):
    pool_columns(pl.program_id(0), pl.num_programs(0), *refs)


def pooled_rows(flat_len, start, hidden, fq, num, den, prior, w_out):
    count, span, width = hidden.shape
    block = pl.BlockSpec((count, span, COLS), lambda j: (0, 0, j))
    pairs = COLS // LANES
    return pl.pallas_call(
        pool_kernel,
        grid=(width // COLS,),
        in_specs=[
            pl.BlockSpec(memory_space=SMEM),
            pl.BlockSpec(memory_space=SMEM),
            block,
            block,
            block,
            block,
            pl.BlockSpec((pairs,) + prior.shape[1:], lambda j: (j, 0, 0, 0)),
            pl.BlockSpec((COLS, width), lambda j: (j, 0)),
        ],
        out_specs=pl.BlockSpec((count, width), lambda j: (0, 0)),
        out_shape=jax.ShapeDtypeStruct((count, width), F32),
        compiler_params=params(10),
        name="pool",
    )(flat_len, start, hbm(hidden), hbm(fq), hbm(num), hbm(den), prior, hbm(w_out))


def split_six(x, axis):
    one, two, three = split(x, 3)
    left = jnp.concatenate([one, one, two, two, one, three], axis=axis)
    right = jnp.concatenate([one, two, one, two, three, one], axis=axis)
    return left, right


GROUP = 16


def leaf_factor(mat, jobs=()):
    groups, tiles = LANES // GROUP, GROUP // 8
    sub, lane = iota((8, LANES), 0), iota((8, LANES), 1)
    rows = [
        [mat[GROUP * g + 8 * v : GROUP * g + 8 * v + 8, :] for v in range(tiles)]
        for g in range(groups)
    ]

    def row_of(x, i):
        return jnp.broadcast_to(x[i : i + 1, :], (8, LANES))

    def col_of(x, c):
        return jnp.broadcast_to(x[:, c : c + 1], (8, LANES))

    for g in range(groups):
        for job in jobs[g::groups]:
            job()
        base = GROUP * g
        own = (lane >= base) & (lane < base + GROUP)
        here = [[col_of(rows[g][v], base + c) for v in range(tiles)] for c in range(GROUP)]
        now = [
            jnp.where(own, (lane - base == sub + 8 * v).astype(F32), rows[g][v])
            for v in range(tiles)
        ]
        following = g + 1 < groups
        if following:
            after = [[col_of(rows[g + 1][v], base + c) for v in range(tiles)] for c in range(GROUP)]
            then = [jnp.where(own, 0.0, rows[g + 1][v]) for v in range(tiles)]
        done = []
        for i in range(GROUP):
            tile, at = divmod(i, 8)
            r = lax.rsqrt(row_of(here[i][tile], at))
            u = row_of(now[tile], at) * r
            done.append(u)
            below = [v for v in range(tile, tiles) if not (v == tile and at == 7)]
            m = {v: here[i][v] * r for v in below}
            for v in below:
                now[v] = now[v] - m[v] * u
            if following:
                mh = [after[i][v] * r for v in range(tiles)]
                then = [then[v] - mh[v] * u for v in range(tiles)]
            for c in range(i + 1, GROUP):
                s = row_of(here[c][tile], at) * r
                for v in below:
                    here[c][v] = here[c][v] - m[v] * s
                if following:
                    after[c] = [after[c][v] - mh[v] * s for v in range(tiles)]
        final = []
        for v in range(tiles):
            x = done[8 * v]
            for i in range(1, 8):
                x = jnp.where(sub == i, done[8 * v + i], x)
            final.append(x)
        rows[g] = final
        if following:
            rows[g + 1] = then
        if g + 2 < groups:
            left, right = split_six(jnp.concatenate(final, axis=0), 0)
            product = dot(left, right, 0, 0)
            for h in range(g + 2, groups):
                rows[h] = [
                    jnp.where(own, 0.0, rows[h][v])
                    - product[GROUP * h + 8 * v : GROUP * h + 8 * v + 8, :]
                    for v in range(tiles)
                ]
    return jnp.concatenate([x for pair in rows for x in pair], axis=0)


def deferred(ref, p):
    n = ref.shape[0]
    panels, k = n // LANES, p + 1
    low, high = p * LANES, k * LANES
    one, two, three = split(ref[low:high, :], 3)
    right = jnp.concatenate([one, two, one, two, three, one], axis=0)
    one, two, three = one[:, high:], two[:, high:], three[:, high:]
    left = jnp.concatenate([one, one, two, two, one, three], axis=0)

    def job(rows, lanes, fresh=False):
        def run():
            product = dot(left[:, : rows.stop - high], right[:, lanes], 0, 0)
            if fresh:
                ref[rows, lanes] = -product
            else:
                ref[rows, lanes] -= product

        return run

    below = slice(high, n)
    jobs = [job(below, slice(low, high), fresh=True)]
    for at in range(0, low, COLS):
        jobs.append(job(below, slice(at, min(at + COLS, low))))
    for b in range(k + 1, panels, 2):
        end = min(b + 2, panels) * LANES
        jobs.append(job(slice(high, end), slice(b * LANES, end)))
    return jobs


def eliminate(ref, k):
    n = ref.shape[0]
    panels = n // LANES
    low, high = k * LANES, (k + 1) * LANES
    row, col = iota((LANES, LANES), 0), iota((LANES, LANES), 1)
    jobs = deferred(ref, k - 1) if k > 0 else ()
    inverse = jnp.where(col <= row, leaf_factor(ref[low:high, low:high], jobs), 0.0)
    if k % 2 == 1:
        ref[low - LANES : low, low:high] = jnp.zeros((LANES, LANES), F32)
    one, two, three = split(inverse, 3)
    left = jnp.concatenate([one, one, two, two, one, three], axis=1)
    ref[low:high, low:high] = inverse
    if k + 1 < panels:
        one, two, three = split(ref[low:high, high:], 3)
        scaled = dot(left, jnp.concatenate([one, two, one, two, three, one], axis=0))
        ref[low:high, high:] = scaled
        coefs, beyond = split_six(scaled[:, :LANES], 0)
        near = slice(high, high + LANES)
        ref[near, near] -= dot(coefs, beyond, 0, 0)
    if k > 0:
        one, two, three = split(ref[low:high, :low], 3)
        ref[low:high, :low] = dot(
            left, jnp.concatenate([one, two, one, two, three, one], axis=0)
        )


def load_kernel(panels, me_ref, own_ref, core_ref, far_ref, far_core_ref, out_ref, sems):
    n = out_ref.shape[0]
    share, half = own_ref.shape[0], n // 2
    me = me_ref[0]
    side = jnp.where(me >= 2, 0, half)
    copies = []
    for slot, ref in enumerate((own_ref, core_ref, far_ref, far_core_ref)):
        block = jnp.bitwise_xor(me, slot)
        to = pl.ds(pl.multiple_of(block * share, share), share)
        if slot < 2:
            target = out_ref.at[to, :]
        else:
            target = out_ref.at[to, pl.ds(pl.multiple_of(side, half), half)]
        copies.append(pltpu.make_async_copy(ref, target, sems.at[slot]))
    for copy in copies:
        copy.start()
    for copy in copies:
        copy.wait()

    @pl.when(me >= 2)
    def _():
        for a in range(0, half, LANES):
            for b in range(0, half, LANES):
                out_ref[a : a + LANES, half + b : half + b + LANES] = out_ref[
                    half + b : half + b + LANES, a : a + LANES
                ].T

    for k in panels:
        eliminate(out_ref, k)


def panels_kernel(panels, in_ref, out_ref):
    del in_ref
    for k in panels:
        eliminate(out_ref, k)


def panels_pool_kernel(panels, in_ref, len_ref, start_ref, core_ref, *refs):
    del in_ref
    *sources, matrix_ref, out_ref = refs[:10]
    *held, prior_ref, beside_ref, sems = refs[10:]
    half = prior_ref.shape[0] // 2
    own = pl.ds(core_ref[0] * half, half)
    other = pl.ds((1 - core_ref[0]) * half, half)
    targets = held + [prior_ref.at[own], prior_ref.at[other], beside_ref]
    copies = [
        pltpu.make_async_copy(source, to, sems.at[i])
        for i, (source, to) in enumerate(zip(sources, targets))
    ]
    for copy in copies:
        copy.start()
    for k in panels:
        eliminate(matrix_ref, k)
    for copy in copies:
        copy.wait()
    h_ref, fq_ref, num_ref, den_ref, wo_ref = held

    @pl.when(core_ref[0] == 1)
    def _():
        prior_ref[...] += beside_ref[...]

    steps = wo_ref.shape[0] // COLS
    pairs = COLS // LANES

    def run(step, carried):
        cols = pl.ds(pl.multiple_of(step * COLS, COLS), COLS)
        pool_columns(
            step,
            steps,
            len_ref,
            start_ref,
            h_ref.at[:, :, cols],
            fq_ref.at[:, :, cols],
            num_ref.at[:, :, cols],
            den_ref.at[:, :, cols],
            prior_ref.at[pl.ds(step * pairs, pairs)],
            wo_ref.at[cols, :],
            out_ref,
        )
        return carried

    lax.fori_loop(0, steps, run, 0)


def factor_next_pool(
    panels, matrix, flat_len, start, core, hidden, fq, num, den, w_out, far_half, other_half, beside
):
    n = matrix.shape[1]
    count, span, width = hidden.shape
    whole, anywhere = pl.BlockSpec(memory_space=VMEM), pl.BlockSpec(memory_space=pl.ANY)
    operands = [hbm(x) for x in (hidden, fq, num, den, w_out)]
    states = [far_half, other_half, beside]
    return pl.pallas_call(
        functools.partial(panels_pool_kernel, panels),
        in_specs=[whole] + [pl.BlockSpec(memory_space=SMEM)] * 3 + [anywhere] * 8,
        out_specs=[whole, whole],
        out_shape=[pltpu.VMEM((n, n), F32), jax.ShapeDtypeStruct((count, width), F32)],
        scratch_shapes=[pltpu.VMEM(x.shape, x.dtype) for x in operands + [beside, beside]]
        + [pltpu.SemaphoreType.DMA((8,))],
        input_output_aliases={0: 0},
        compiler_params=params(24),
        name="factor_next_pool",
        cost_estimate=pl.CostEstimate(flops=8_000_000_000, transcendentals=0, bytes_accessed=12 << 20),
    )(vmem(matrix), flat_len, start, core, *operands, *states)


def factor_first(panels, me, own, core, far, far_core):
    n = own.shape[1]
    anywhere = pl.BlockSpec(memory_space=pl.ANY)
    return pl.pallas_call(
        functools.partial(load_kernel, panels),
        in_specs=[pl.BlockSpec(memory_space=SMEM)] + [anywhere] * 4,
        out_specs=pl.BlockSpec(memory_space=VMEM),
        out_shape=pltpu.VMEM((n, n), F32),
        scratch_shapes=[pltpu.SemaphoreType.DMA((4,))],
        compiler_params=params(14),
        name="factor_first",
        cost_estimate=pl.CostEstimate(flops=8_000_000_000, transcendentals=0, bytes_accessed=4 << 20),
    )(me, own, core, far, far_core)


def factor_next(panels, matrix):
    n = matrix.shape[1]
    return pl.pallas_call(
        functools.partial(panels_kernel, panels),
        in_specs=[pl.BlockSpec(memory_space=VMEM)],
        out_specs=pl.BlockSpec(memory_space=VMEM),
        out_shape=pltpu.VMEM((n, n), F32),
        input_output_aliases={0: 0},
        compiler_params=params(14),
        name="factor_next",
        cost_estimate=pl.CostEstimate(flops=8_000_000_000, transcendentals=0, bytes_accessed=4 << 20),
    )(vmem(matrix))


def whiten_kernel(
    at_ref, *refs
):
    *piece_refs, inv_ref, cov_ref, white_ref, cov_out_ref, loss_ref = refs[:-5]
    rows_ref, centred_ref, held_ref, new_cov_ref, sem = refs[-5:]
    count, n = white_ref.shape
    total = centred_ref.shape[0]
    chunks = n // LANES
    share = cov_ref.shape[0]
    slot = 0
    for ref in piece_refs:
        for b in range(ref.shape[0]):
            held_ref[slot] = ref[b]
            slot += 1
    embed = jnp.concatenate(
        [held_ref[jnp.bitwise_xor(at_ref[0], d)] for d in range(total // count)], axis=0
    )
    centred = embed - jnp.sum(embed, axis=0, keepdims=True) / total
    weight = 0.5 / (total - 1)
    root = 2.0**0.5
    start = pl.multiple_of(at_ref[1] * share, share)
    centred_ref[...] = centred
    left, right = split_six(centred_ref[:, pl.ds(start, share)], 0)[0], split_six(centred, 0)[1]
    new_cov_ref[...] = 0.5 * cov_ref[...] + weight * dot(left, right, 0, 0)
    written = pltpu.make_async_copy(new_cov_ref, cov_out_ref, sem)
    written.start()
    thirds = jnp.concatenate(split(root * centred, 3), axis=0)
    for k in range(0, chunks, 2):
        upto = (k + 2) * LANES
        one, two, three = split(inv_ref[k * LANES : upto, :upto], 3)
        by_one = dot(thirds[:, :upto], one, 1, 1)
        by_two = dot(thirds[: 2 * total, :upto], two, 1, 1)
        product = by_one[:total] + (by_one[total : 2 * total] + by_two[:total])
        product = product + (
            by_one[2 * total :] + by_two[total:] + dot(thirds[:total, :upto], three, 1, 1)
        )
        rows_ref[:, k, :] = product[:, :LANES]
        rows_ref[:, k + 1, :] = product[:, LANES:]
    w = [rows_ref[a] for a in range(total)]
    pairs = [(a, b) for a in range(total) for b in range(a, total)]
    products = jnp.concatenate([w[a] * w[b] for a, b in pairs], axis=0)
    before = iota((LANES, 2 * LANES), 0) < iota((LANES, 2 * LANES), 1)
    earlier = before.astype(BF16)
    sums = [dot(piece, earlier) for piece in split(products, 3)]
    sums = sums[0] + sums[1] + sums[2]
    chunk = iota((8, LANES), 0)
    entry = {}
    for i, (a, b) in enumerate(pairs):
        inside = sums[8 * i : 8 * i + 8, :LANES]
        whole = sums[8 * i : 8 * i + 8, LANES:]
        carry = jnp.where(chunk >= 1, pltpu.roll(whole, 1, 0), 0.0)
        for by in (1, 2, 4):
            carry = carry + jnp.where(chunk >= by, pltpu.roll(carry, by, 0), 0.0)
        entry[a, b] = weight * (inside + carry) + (1.0 if a == b else 0.0)
    right = list(w)
    inverse = []
    spread = jnp.ones((8, LANES), F32)
    for p in range(total):
        inv = 1.0 / entry[p, p]
        inverse.append(inv)
        spread = spread + weight * right[p] * right[p] * inv
        for a in range(p + 1, total):
            f = entry[p, a] * inv
            for b in range(a, total):
                entry[a, b] = entry[a, b] - f * entry[p, b]
            right[a] = right[a] - f * right[p]
    scale = lax.rsqrt(spread)
    solved = [None] * total
    for p in reversed(range(total)):
        x = right[p]
        for b in range(p + 1, total):
            x = x - entry[p, b] * solved[b]
        solved[p] = x * inverse[p]
    solved = [x * scale for x in solved]
    gap = jnp.zeros((8, LANES), F32)
    normed = []
    for a in range(total):
        norm = jnp.sum(jnp.sum(solved[a] * solved[a], axis=1, keepdims=True), axis=0, keepdims=True)
        normed.append(solved[a] / jnp.sqrt(norm + 1e-06))
    for pair in range(total // 2):
        diff = normed[2 * pair] - normed[2 * pair + 1]
        gap = gap + diff * diff
    gap = jnp.sum(jnp.sum(gap, axis=1, keepdims=True), axis=0, keepdims=True)
    loss_ref[...] = gap / (total // 2)
    for a in range(total):
        rows_ref[a] = solved[a]
    for m in range(count):
        own = rows_ref[at_ref[0] * count + m]
        for k in range(chunks):
            white_ref[m : m + 1, k * LANES : (k + 1) * LANES] = own[k : k + 1, :]
    written.wait()


def whiten(at, pieces, inverse, running_cov):
    groups = sum(piece.shape[0] for piece in pieces)
    count, n = pieces[0].shape[1:]
    total = groups * count
    whole = pl.BlockSpec(memory_space=VMEM)
    return pl.pallas_call(
        whiten_kernel,
        in_specs=[pl.BlockSpec(memory_space=SMEM)] + [whole] * (len(pieces) + 2),
        out_specs=[whole, pl.BlockSpec(memory_space=pl.ANY), whole],
        out_shape=[
            jax.ShapeDtypeStruct((count, n), F32),
            jax.ShapeDtypeStruct(running_cov.shape, F32),
            jax.ShapeDtypeStruct((1, 1), F32),
        ],
        scratch_shapes=[
            pltpu.VMEM((total, n // LANES, LANES), F32),
            pltpu.VMEM((total, n), F32),
            pltpu.VMEM((groups, count, n), F32),
            pltpu.VMEM(running_cov.shape, F32),
            pltpu.SemaphoreType.DMA,
        ],
        compiler_params=params(12),
        name="whiten",
    )(at, *pieces, inverse, running_cov)


def bits(size):
    return [1 << b for b in range(size.bit_length() - 1)]


def swap(x, axis, by):
    size = lax.axis_size(axis)
    return lax.ppermute(x, axis, [(i, i ^ by) for i in range(size)])


def earlier_sum(x, axis):
    size = lax.axis_size(axis)
    me = lax.axis_index(axis)
    prior = jnp.zeros_like(x)
    whole = x
    for by in bits(size):
        upper = (me & by) != 0
        if by == size // 2:
            got = lax.ppermute(whole, axis, [(i, i + by) for i in range(by)])
            prior = prior + got
        else:
            got = swap(whole, axis, by)
            prior = prior + jnp.where(upper, got, 0.0)
            whole = whole + got
    return prior


def body(hidden_states, lengths, w_query, w_key, w_value, w_out, running_cov):
    pairs, two, span, width = hidden_states.shape
    count = pairs * two
    seq, dp = lax.axis_size("seq"), lax.axis_size("dp")
    me, group = lax.axis_index("seq"), lax.axis_index("dp")
    hidden = hidden_states.reshape(count, span, width)
    flat_len = lengths.reshape(count)

    start = (me * span).astype(jnp.int32).reshape(1)
    if seq == 4 and dp == 8 and count == 2:
        white, cov, loss = body_fixed(hidden, flat_len, start, w_query, w_key, w_value, w_out, running_cov)
    else:
        fq, num, den, states = encode(hidden, w_query, w_key, w_value)
        prior = earlier_sum(states, "seq")
        partial = pooled_rows(flat_len, start, hidden, fq, num, den, prior, w_out)
        gathered = lax.all_gather(partial, ("dp", "seq"))
        embed = gathered.reshape(dp, seq, count, width).sum(axis=1).reshape(dp * count, width)
        white, cov, loss = whiten_many(embed, running_cov, count)
    return white.reshape(pairs, two, width), cov, loss


def body_fixed(hidden, flat_len, start, w_query, w_key, w_value, w_out, running_cov):
    me, group = lax.axis_index("seq"), lax.axis_index("dp")
    width = hidden.shape[2]
    half = width // 2
    core = me & 1
    at = jnp.stack([group, me]).astype(jnp.int32)
    chip_columns = lax.dynamic_slice_in_dim(running_cov, (me >> 1) * half, half, 1)
    far_cov = swap(chip_columns, "seq", 2)
    core_cov = swap(running_cov, "seq", 1)
    fq, num, den, states = encode(hidden, w_query, w_key, w_value)
    far_cov, core_cov, states = lax.optimization_barrier((far_cov, core_cov, states))
    core_states = swap(states, "seq", 1)
    far_core_cov = swap(far_cov, "seq", 1)
    quarter = states.shape[0] // 2
    matrix = factor_first((0,), at[1:], running_cov, core_cov, far_cov, far_core_cov)
    core_states, matrix = lax.optimization_barrier((core_states, matrix))
    mine = lax.dynamic_slice_in_dim(states, core * quarter, quarter, 0)
    mine = mine + lax.dynamic_slice_in_dim(core_states, core * quarter, quarter, 0)
    far_half = lax.ppermute(mine, "seq", [(0, 2), (1, 3)])
    matrix = factor_next((1, 2), matrix)
    far_half, matrix = lax.optimization_barrier((far_half, matrix))
    other_half = swap(far_half, "seq", 1)
    matrix = factor_next((3,), matrix)
    other_half, matrix = lax.optimization_barrier((other_half, matrix))
    matrix, partial = factor_next_pool(
        (4,),
        matrix,
        flat_len,
        start,
        core.astype(jnp.int32).reshape(1),
        hidden,
        fq,
        num,
        den,
        w_out,
        far_half,
        other_half,
        core_states,
    )
    got = [swap(partial, "seq", by) for by in (1, 2, 3)]
    matrix = factor_next((5,), matrix)
    partial, got, matrix = lax.optimization_barrier((partial, got, matrix))
    embed = ((partial + got[0]) + (got[1] + got[2]))[None]
    beside = swap(embed, "dp", 1)
    matrix = factor_next((6,), matrix)
    embed, beside, matrix = lax.optimization_barrier((embed, beside, matrix))
    embed = jnp.concatenate([embed, beside], axis=0)
    pieces = [embed] + [swap(embed, "dp", by) for by in (2, 4, 6)]
    matrix = factor_next((7,), matrix)
    white, cov, loss = whiten(at, pieces, matrix, running_cov)
    return white, cov, loss.reshape(())


def whiten_many(embed, running_cov, count):
    total = embed.shape[0]
    share = running_cov.shape[0]
    centred = embed - jnp.sum(embed, axis=0) / total
    full = lax.all_gather(running_cov, "seq", axis=0, tiled=True)
    full = 0.5 * full + (0.5 / (total - 1)) * jnp.dot(centred.T, centred, precision=HIGHEST)
    chol = jnp.linalg.cholesky(full)
    rows = lax.linalg.triangular_solve(chol, centred.T, left_side=True, lower=True).T
    normed = rows / jnp.sqrt(jnp.sum(rows * rows, axis=1, keepdims=True) + 1e-06)
    normed = normed.reshape(total // 2, 2, -1)
    gap = normed[:, 0] - normed[:, 1]
    loss = jnp.sum(gap * gap) / (total // 2)
    white = lax.dynamic_slice_in_dim(rows, lax.axis_index("dp") * count, count, 0)
    cov = lax.dynamic_slice_in_dim(full, lax.axis_index("seq") * share, share, 0)
    return white, cov, loss


def solution(mesh):
    placed = (P("dp", None, "seq", None), P("dp", None), P(), P(), P(), P(), P("seq", None))
    return jax.shard_map(
        body,
        mesh=mesh,
        in_specs=placed,
        out_specs=(P("dp", None, None), P("seq", None), P()),
        check_vma=False,
    )
```

```python
import functools

import jax
import jax.numpy as jnp
from jax import lax
from jax.experimental import pallas as pl
from jax.experimental.pallas import tpu as pltpu
from jax.sharding import PartitionSpec as P

HEADS = 16
HEAD_DIM = 64
LANES = 128
COLS = 256
F32 = jnp.float32
BF16 = jnp.bfloat16
HIGHEST = lax.Precision.HIGHEST
VMEM = pltpu.VMEM
SMEM = pltpu.SMEM


def hbm(x):
    return pltpu.with_memory_space_constraint(x, pltpu.HBM)


def vmem(x):
    return pltpu.with_memory_space_constraint(x, VMEM)


def params(mib):
    return pltpu.CompilerParams(vmem_limit_bytes=mib << 20)


def feature(u):
    return jnp.where(u > 0.0, u + 1.0, jnp.exp(jnp.minimum(u, 0.0)))


def split(x, parts):
    out = []
    for _ in range(parts):
        piece = x.astype(BF16)
        out.append(piece)
        x = x - piece.astype(F32)
    return out


def dot(a, b, ca=1, cb=0):
    return lax.dot_general(a, b, (((ca,), (cb,)), ((), ())), preferred_element_type=F32)


def dot_f32(a, b, ca=1, cb=0):
    return lax.dot_general(
        a, b, (((ca,), (cb,)), ((), ())), precision=HIGHEST, preferred_element_type=F32
    )


def iota(shape, dim):
    return lax.broadcasted_iota(jnp.int32, shape, dim)


def encode_kernel(*refs):
    (hidden_ref, *weight_refs), results = refs[:4], refs[4:8]
    (h_ref, w_ref, *held), (in_sems, out_sems) = refs[8:14], refs[14:]
    steps = w_ref.shape[2] // COLS
    pairs = COLS // LANES

    def window(j):
        return pl.ds(pl.multiple_of(j * COLS, COLS), COLS)

    def arriving(i, j):
        return pltpu.make_async_copy(
            weight_refs[i].at[:, window(j)], w_ref.at[i, :, window(j)], in_sems.at[i, j]
        )

    def blocks(refs, j):
        *arrays, state_ref = refs
        return [x.at[:, :, window(j)] for x in arrays] + [state_ref.at[pl.ds(j * pairs, pairs)]]

    def leaving(j):
        return [
            pltpu.make_async_copy(source, target, out_sems.at[i, j])
            for i, (source, target) in enumerate(zip(blocks(held, j), blocks(results, j)))
        ]

    first = pltpu.make_async_copy(hidden_ref, h_ref, in_sems.at[3, 0])
    first.start()
    for j in range(steps):
        for i in range(3):
            arriving(i, j).start()
    first.wait()

    def run(j, carried):
        for i in range(3):
            arriving(i, j).wait()
        encode_columns(h_ref, *[w_ref.at[i, :, window(j)] for i in range(3)], *blocks(held, j))
        for copy in leaving(j):
            copy.start()
        return carried

    lax.fori_loop(0, steps, run, 0)
    for j in range(steps):
        for copy in leaving(j):
            copy.wait()


def encode_columns(h_ref, wq_ref, wk_ref, wv_ref, fq_ref, num_ref, den_ref, state_ref):
    count, span = h_ref.shape[0], h_ref.shape[1]
    rows = h_ref[...].reshape(count * span, h_ref.shape[2])
    fq = feature(dot(rows, wq_ref[...])).astype(BF16)
    fk = feature(dot(rows, wk_ref[...])).astype(BF16)
    values = dot(rows, wv_ref[...]).astype(BF16)
    fq_ref[...] = fq.reshape(fq_ref.shape)
    causal = iota((span, span), 0) >= iota((span, span), 1)
    ones_below = causal.astype(BF16)
    low = iota((span, LANES), 1) < HEAD_DIM
    same_head = (iota((LANES, LANES), 0) < HEAD_DIM) == (iota((LANES, LANES), 1) < HEAD_DIM)
    summing = jnp.concatenate([same_head.astype(BF16)] * 2, axis=0)
    for module in range(count):
        at = slice(module * span, (module + 1) * span)
        running = dot(ones_below, fk[at])
        for pair in range(COLS // LANES):
            cols = slice(pair * LANES, (pair + 1) * LANES)
            q, k, v = fq[at, cols], fk[at, cols], values[at, cols]
            state = dot(k, v, 0, 0)
            merged = jnp.where(low[:HEAD_DIM], state[:HEAD_DIM], state[HEAD_DIM:])
            state_ref[pair, module] = jnp.concatenate(
                [merged, jnp.broadcast_to(running[span - 1 :, cols], (8, LANES))], axis=0
            )
            hi, lo = split(q.astype(F32) * running[:, cols], 2)
            den_ref[module, :, cols] = dot(jnp.concatenate([hi, lo], axis=1), summing)
            parts = []
            for half in range(2):
                own = low if half == 0 else jnp.logical_not(low)
                scores = dot(jnp.where(own, q, jnp.zeros_like(q)), k, 1, 1)
                weights = jnp.where(causal, scores, 0.0).astype(BF16)
                parts.append(dot(weights, v))
            num_ref[module, :, cols] = jnp.where(low, parts[0], parts[1])


def encode(hidden, w_query, w_key, w_value):
    count, span, width = hidden.shape
    steps = width // COLS
    shape = (count, span, width)
    state_shape = (width // LANES, count, HEAD_DIM + 8, LANES)
    anywhere = pl.BlockSpec(memory_space=pl.ANY)
    results = [(shape, BF16), (shape, F32), (shape, F32), (state_shape, F32)]
    return pl.pallas_call(
        encode_kernel,
        in_specs=[anywhere] * 4,
        out_specs=[anywhere] * 4,
        out_shape=[pltpu.HBM(*x) for x in results],
        scratch_shapes=[VMEM(shape, BF16), VMEM((3, width, width), BF16)]
        + [VMEM(*x) for x in results]
        + [pltpu.SemaphoreType.DMA((4, steps)), pltpu.SemaphoreType.DMA((4, steps))],
        compiler_params=params(24),
        name="encode",
    )(hbm(hidden), hbm(w_query), hbm(w_key), hbm(w_value))


def pool_columns(step, steps, len_ref, start_ref, h_ref, fq_ref, num_ref, den_ref, prior_ref, wo_ref, out_ref):
    count, span = fq_ref.shape[0], fq_ref.shape[1]
    low = iota((HEAD_DIM, LANES), 1) < HEAD_DIM
    same_head = (iota((LANES, LANES), 0) < HEAD_DIM) == (iota((LANES, LANES), 1) < HEAD_DIM)
    summing = jnp.concatenate([same_head.astype(BF16)] * 2, axis=0)
    sums = []
    hsums = []
    for module in range(count):
        valid = iota((span, LANES), 0) + start_ref[0] < len_ref[module]
        heads = []
        plain = []
        for pair in range(COLS // LANES):
            cols = slice(pair * LANES, (pair + 1) * LANES)
            q = fq_ref[module, :, cols]
            prior = prior_ref[pair, module]
            state = prior[:HEAD_DIM].astype(BF16)
            empty = jnp.zeros_like(state)
            state = jnp.concatenate(
                [jnp.where(low, state, empty), jnp.where(low, empty, state)], axis=0
            )
            hi, lo = split(q.astype(F32) * prior[HEAD_DIM : HEAD_DIM + 1], 2)
            numer = num_ref[module, :, cols] + dot(q, state)
            denom = den_ref[module, :, cols] + dot(jnp.concatenate([hi, lo], axis=1), summing)
            attended = (numer / denom).astype(BF16).astype(F32)
            heads.append(jnp.sum(jnp.where(valid, attended, 0.0), axis=0, keepdims=True))
            plain.append(
                jnp.sum(
                    jnp.where(valid, h_ref[module, :, cols].astype(F32), 0.0), axis=0, keepdims=True
                )
            )
        sums.append(jnp.concatenate(heads, axis=1))
        hsums.append(jnp.concatenate(plain, axis=1))
    sums = jnp.concatenate(sums, axis=0)
    pieces = split(sums, 3)
    part = dot(jnp.concatenate(pieces, axis=0), wo_ref[...])
    part = part[:count] + part[count : 2 * count] + part[2 * count :]

    @pl.when(step == 0)
    def _():
        out_ref[...] = part

    @pl.when(step > 0)
    def _():
        out_ref[...] += part

    here = pl.ds(pl.multiple_of(step * COLS, COLS), COLS)
    out_ref[:, here] += jnp.concatenate(hsums, axis=0)

    @pl.when(step == steps - 1)
    def _():
        for module in range(count):
            out_ref[module : module + 1, :] /= len_ref[module].astype(F32)


def pool_kernel(*refs):
    pool_columns(pl.program_id(0), pl.num_programs(0), *refs)


def pooled_rows(flat_len, start, hidden, fq, num, den, prior, w_out):
    count, span, width = hidden.shape
    block = pl.BlockSpec((count, span, COLS), lambda j: (0, 0, j))
    pairs = COLS // LANES
    return pl.pallas_call(
        pool_kernel,
        grid=(width // COLS,),
        in_specs=[
            pl.BlockSpec(memory_space=SMEM),
            pl.BlockSpec(memory_space=SMEM),
            block,
            block,
            block,
            block,
            pl.BlockSpec((pairs,) + prior.shape[1:], lambda j: (j, 0, 0, 0)),
            pl.BlockSpec((COLS, width), lambda j: (j, 0)),
        ],
        out_specs=pl.BlockSpec((count, width), lambda j: (0, 0)),
        out_shape=jax.ShapeDtypeStruct((count, width), F32),
        compiler_params=params(10),
        name="pool",
    )(flat_len, start, hbm(hidden), hbm(fq), hbm(num), hbm(den), prior, hbm(w_out))


def split_six(x, axis):
    one, two, three = split(x, 3)
    left = jnp.concatenate([one, one, two, two, one, three], axis=axis)
    right = jnp.concatenate([one, two, one, two, three, one], axis=axis)
    return left, right


GROUP = 16


def leaf_factor(mat, jobs=()):
    groups, tiles = LANES // GROUP, GROUP // 8
    sub, lane = iota((8, LANES), 0), iota((8, LANES), 1)
    rows = [
        [mat[GROUP * g + 8 * v : GROUP * g + 8 * v + 8, :] for v in range(tiles)]
        for g in range(groups)
    ]

    def row_of(x, i):
        return jnp.broadcast_to(x[i : i + 1, :], (8, LANES))

    def col_of(x, c):
        return jnp.broadcast_to(x[:, c : c + 1], (8, LANES))

    for g in range(groups):
        for job in jobs[g::groups]:
            job()
        base = GROUP * g
        own = (lane >= base) & (lane < base + GROUP)
        here = [[col_of(rows[g][v], base + c) for v in range(tiles)] for c in range(GROUP)]
        now = [
            jnp.where(own, (lane - base == sub + 8 * v).astype(F32), rows[g][v])
            for v in range(tiles)
        ]
        following = g + 1 < groups
        if following:
            after = [[col_of(rows[g + 1][v], base + c) for v in range(tiles)] for c in range(GROUP)]
            then = [jnp.where(own, 0.0, rows[g + 1][v]) for v in range(tiles)]
        done = []
        for i in range(GROUP):
            tile, at = divmod(i, 8)
            r = lax.rsqrt(row_of(here[i][tile], at))
            u = row_of(now[tile], at) * r
            done.append(u)
            below = [v for v in range(tile, tiles) if not (v == tile and at == 7)]
            m = {v: here[i][v] * r for v in below}
            for v in below:
                now[v] = now[v] - m[v] * u
            if following:
                mh = [after[i][v] * r for v in range(tiles)]
                then = [then[v] - mh[v] * u for v in range(tiles)]
            for c in range(i + 1, GROUP):
                s = row_of(here[c][tile], at) * r
                for v in below:
                    here[c][v] = here[c][v] - m[v] * s
                if following:
                    after[c] = [after[c][v] - mh[v] * s for v in range(tiles)]
        final = []
        for v in range(tiles):
            x = done[8 * v]
            for i in range(1, 8):
                x = jnp.where(sub == i, done[8 * v + i], x)
            final.append(x)
        rows[g] = final
        if following:
            rows[g + 1] = then
        if g + 2 < groups:
            left, right = split_six(jnp.concatenate(final, axis=0), 0)
            product = dot(left, right, 0, 0)
            for h in range(g + 2, groups):
                rows[h] = [
                    jnp.where(own, 0.0, rows[h][v])
                    - product[GROUP * h + 8 * v : GROUP * h + 8 * v + 8, :]
                    for v in range(tiles)
                ]
    return jnp.concatenate([x for pair in rows for x in pair], axis=0)


def deferred(ref, p):
    n = ref.shape[0]
    panels, k = n // LANES, p + 1
    low, high = p * LANES, k * LANES
    one, two, three = split(ref[low:high, :], 3)
    right = jnp.concatenate([one, two, one, two, three, one], axis=0)
    one, two, three = one[:, high:], two[:, high:], three[:, high:]
    left = jnp.concatenate([one, one, two, two, one, three], axis=0)

    def job(rows, lanes, fresh=False):
        def run():
            product = dot(left[:, : rows.stop - high], right[:, lanes], 0, 0)
            if fresh:
                ref[rows, lanes] = -product
            else:
                ref[rows, lanes] -= product

        return run

    below = slice(high, n)
    jobs = [job(below, slice(low, high), fresh=True)]
    for at in range(0, low, COLS):
        jobs.append(job(below, slice(at, min(at + COLS, low))))
    for b in range(k + 1, panels, 2):
        end = min(b + 2, panels) * LANES
        jobs.append(job(slice(high, end), slice(b * LANES, end)))
    return jobs


def eliminate(ref, k):
    n = ref.shape[0]
    panels = n // LANES
    low, high = k * LANES, (k + 1) * LANES
    row, col = iota((LANES, LANES), 0), iota((LANES, LANES), 1)
    jobs = deferred(ref, k - 1) if k > 0 else ()
    inverse = jnp.where(col <= row, leaf_factor(ref[low:high, low:high], jobs), 0.0)
    if k % 2 == 1:
        ref[low - LANES : low, low:high] = jnp.zeros((LANES, LANES), F32)
    one, two, three = split(inverse, 3)
    left = jnp.concatenate([one, one, two, two, one, three], axis=1)
    ref[low:high, low:high] = inverse
    if k + 1 < panels:
        one, two, three = split(ref[low:high, high:], 3)
        scaled = dot(left, jnp.concatenate([one, two, one, two, three, one], axis=0))
        ref[low:high, high:] = scaled
        coefs, beyond = split_six(scaled[:, :LANES], 0)
        near = slice(high, high + LANES)
        ref[near, near] -= dot(coefs, beyond, 0, 0)
    if k > 0:
        one, two, three = split(ref[low:high, :low], 3)
        ref[low:high, :low] = dot(
            left, jnp.concatenate([one, two, one, two, three, one], axis=0)
        )


def load_kernel(panels, me_ref, own_ref, core_ref, far_ref, far_core_ref, out_ref, sems):
    n = out_ref.shape[0]
    share, half = own_ref.shape[0], n // 2
    me = me_ref[0]
    side = jnp.where(me >= 2, 0, half)
    copies = []
    for slot, ref in enumerate((own_ref, core_ref, far_ref, far_core_ref)):
        block = jnp.bitwise_xor(me, slot)
        to = pl.ds(pl.multiple_of(block * share, share), share)
        if slot < 2:
            target = out_ref.at[to, :]
        else:
            target = out_ref.at[to, pl.ds(pl.multiple_of(side, half), half)]
        copies.append(pltpu.make_async_copy(ref, target, sems.at[slot]))
    for copy in copies:
        copy.start()
    for copy in copies:
        copy.wait()

    @pl.when(me >= 2)
    def _():
        for a in range(0, half, LANES):
            for b in range(0, half, LANES):
                out_ref[a : a + LANES, half + b : half + b + LANES] = out_ref[
                    half + b : half + b + LANES, a : a + LANES
                ].T

    for k in panels:
        eliminate(out_ref, k)


def panels_kernel(panels, in_ref, out_ref):
    del in_ref
    for k in panels:
        eliminate(out_ref, k)


def panels_pool_kernel(panels, in_ref, len_ref, start_ref, core_ref, *refs):
    del in_ref
    *sources, matrix_ref, out_ref = refs[:10]
    *held, prior_ref, beside_ref, sems = refs[10:]
    half = prior_ref.shape[0] // 2
    own = pl.ds(core_ref[0] * half, half)
    other = pl.ds((1 - core_ref[0]) * half, half)
    targets = held + [prior_ref.at[own], prior_ref.at[other], beside_ref]
    copies = [
        pltpu.make_async_copy(source, to, sems.at[i])
        for i, (source, to) in enumerate(zip(sources, targets))
    ]
    for copy in copies:
        copy.start()
    for k in panels:
        eliminate(matrix_ref, k)
    for copy in copies:
        copy.wait()
    h_ref, fq_ref, num_ref, den_ref, wo_ref = held

    @pl.when(core_ref[0] == 1)
    def _():
        prior_ref[...] += beside_ref[...]

    steps = wo_ref.shape[0] // COLS
    pairs = COLS // LANES

    for step in range(steps):
        cols = slice(step * COLS, (step + 1) * COLS)
        pool_columns(
            step,
            steps,
            len_ref,
            start_ref,
            h_ref.at[:, :, cols],
            fq_ref.at[:, :, cols],
            num_ref.at[:, :, cols],
            den_ref.at[:, :, cols],
            prior_ref.at[step * pairs : (step + 1) * pairs],
            wo_ref.at[cols, :],
            out_ref,
        )


def factor_next_pool(
    panels, matrix, flat_len, start, core, hidden, fq, num, den, w_out, far_half, other_half, beside
):
    n = matrix.shape[1]
    count, span, width = hidden.shape
    whole, anywhere = pl.BlockSpec(memory_space=VMEM), pl.BlockSpec(memory_space=pl.ANY)
    operands = [hbm(x) for x in (hidden, fq, num, den, w_out)]
    states = [far_half, other_half, beside]
    return pl.pallas_call(
        functools.partial(panels_pool_kernel, panels),
        in_specs=[whole] + [pl.BlockSpec(memory_space=SMEM)] * 3 + [anywhere] * 8,
        out_specs=[whole, whole],
        out_shape=[pltpu.VMEM((n, n), F32), jax.ShapeDtypeStruct((count, width), F32)],
        scratch_shapes=[pltpu.VMEM(x.shape, x.dtype) for x in operands + [beside, beside]]
        + [pltpu.SemaphoreType.DMA((8,))],
        input_output_aliases={0: 0},
        compiler_params=params(24),
        name="factor_next_pool",
        cost_estimate=pl.CostEstimate(flops=8_000_000_000, transcendentals=0, bytes_accessed=12 << 20),
    )(vmem(matrix), flat_len, start, core, *operands, *states)


def factor_first(panels, me, own, core, far, far_core):
    n = own.shape[1]
    anywhere = pl.BlockSpec(memory_space=pl.ANY)
    return pl.pallas_call(
        functools.partial(load_kernel, panels),
        in_specs=[pl.BlockSpec(memory_space=SMEM)] + [anywhere] * 4,
        out_specs=pl.BlockSpec(memory_space=VMEM),
        out_shape=pltpu.VMEM((n, n), F32),
        scratch_shapes=[pltpu.SemaphoreType.DMA((4,))],
        compiler_params=params(14),
        name="factor_first",
        cost_estimate=pl.CostEstimate(flops=8_000_000_000, transcendentals=0, bytes_accessed=4 << 20),
    )(me, own, core, far, far_core)


def factor_next(panels, matrix):
    n = matrix.shape[1]
    return pl.pallas_call(
        functools.partial(panels_kernel, panels),
        in_specs=[pl.BlockSpec(memory_space=VMEM)],
        out_specs=pl.BlockSpec(memory_space=VMEM),
        out_shape=pltpu.VMEM((n, n), F32),
        input_output_aliases={0: 0},
        compiler_params=params(14),
        name="factor_next",
        cost_estimate=pl.CostEstimate(flops=8_000_000_000, transcendentals=0, bytes_accessed=4 << 20),
    )(vmem(matrix))


def whiten_kernel(
    at_ref, *refs
):
    *piece_refs, inv_ref, cov_ref, white_ref, cov_out_ref, loss_ref = refs[:-5]
    rows_ref, centred_ref, held_ref, new_cov_ref, sem = refs[-5:]
    count, n = white_ref.shape
    total = centred_ref.shape[0]
    chunks = n // LANES
    share = cov_ref.shape[0]
    slot = 0
    for ref in piece_refs:
        for b in range(ref.shape[0]):
            held_ref[slot] = ref[b]
            slot += 1
    embed = jnp.concatenate(
        [held_ref[jnp.bitwise_xor(at_ref[0], d)] for d in range(total // count)], axis=0
    )
    centred = embed - jnp.sum(embed, axis=0, keepdims=True) / total
    weight = 0.5 / (total - 1)
    root = 2.0**0.5
    start = pl.multiple_of(at_ref[1] * share, share)
    centred_ref[...] = centred
    left, right = split_six(centred_ref[:, pl.ds(start, share)], 0)[0], split_six(centred, 0)[1]
    new_cov_ref[...] = 0.5 * cov_ref[...] + weight * dot(left, right, 0, 0)
    written = pltpu.make_async_copy(new_cov_ref, cov_out_ref, sem)
    written.start()
    thirds = jnp.concatenate(split(root * centred, 3), axis=0)
    for k in range(0, chunks, 2):
        upto = (k + 2) * LANES
        one, two, three = split(inv_ref[k * LANES : upto, :upto], 3)
        by_one = dot(thirds[:, :upto], one, 1, 1)
        by_two = dot(thirds[: 2 * total, :upto], two, 1, 1)
        product = by_one[:total] + (by_one[total : 2 * total] + by_two[:total])
        product = product + (
            by_one[2 * total :] + by_two[total:] + dot(thirds[:total, :upto], three, 1, 1)
        )
        rows_ref[:, k, :] = product[:, :LANES]
        rows_ref[:, k + 1, :] = product[:, LANES:]
    w = [rows_ref[a] for a in range(total)]
    pairs = [(a, b) for a in range(total) for b in range(a, total)]
    products = jnp.concatenate([w[a] * w[b] for a, b in pairs], axis=0)
    before = iota((LANES, 2 * LANES), 0) < iota((LANES, 2 * LANES), 1)
    earlier = before.astype(BF16)
    sums = [dot(piece, earlier) for piece in split(products, 3)]
    sums = sums[0] + sums[1] + sums[2]
    chunk = iota((8, LANES), 0)
    entry = {}
    for i, (a, b) in enumerate(pairs):
        inside = sums[8 * i : 8 * i + 8, :LANES]
        whole = sums[8 * i : 8 * i + 8, LANES:]
        carry = jnp.where(chunk >= 1, pltpu.roll(whole, 1, 0), 0.0)
        for by in (1, 2, 4):
            carry = carry + jnp.where(chunk >= by, pltpu.roll(carry, by, 0), 0.0)
        entry[a, b] = weight * (inside + carry) + (1.0 if a == b else 0.0)
    right = list(w)
    inverse = []
    spread = jnp.ones((8, LANES), F32)
    for p in range(total):
        inv = 1.0 / entry[p, p]
        inverse.append(inv)
        spread = spread + weight * right[p] * right[p] * inv
        for a in range(p + 1, total):
            f = entry[p, a] * inv
            for b in range(a, total):
                entry[a, b] = entry[a, b] - f * entry[p, b]
            right[a] = right[a] - f * right[p]
    scale = lax.rsqrt(spread)
    solved = [None] * total
    for p in reversed(range(total)):
        x = right[p]
        for b in range(p + 1, total):
            x = x - entry[p, b] * solved[b]
        solved[p] = x * inverse[p]
    solved = [x * scale for x in solved]
    gap = jnp.zeros((8, LANES), F32)
    normed = []
    for a in range(total):
        norm = jnp.sum(jnp.sum(solved[a] * solved[a], axis=1, keepdims=True), axis=0, keepdims=True)
        normed.append(solved[a] / jnp.sqrt(norm + 1e-06))
    for pair in range(total // 2):
        diff = normed[2 * pair] - normed[2 * pair + 1]
        gap = gap + diff * diff
    gap = jnp.sum(jnp.sum(gap, axis=1, keepdims=True), axis=0, keepdims=True)
    loss_ref[...] = gap / (total // 2)
    for a in range(total):
        rows_ref[a] = solved[a]
    for m in range(count):
        own = rows_ref[at_ref[0] * count + m]
        for k in range(chunks):
            white_ref[m : m + 1, k * LANES : (k + 1) * LANES] = own[k : k + 1, :]
    written.wait()


def whiten(at, pieces, inverse, running_cov):
    groups = sum(piece.shape[0] for piece in pieces)
    count, n = pieces[0].shape[1:]
    total = groups * count
    whole = pl.BlockSpec(memory_space=VMEM)
    return pl.pallas_call(
        whiten_kernel,
        in_specs=[pl.BlockSpec(memory_space=SMEM)] + [whole] * (len(pieces) + 2),
        out_specs=[whole, pl.BlockSpec(memory_space=pl.ANY), whole],
        out_shape=[
            jax.ShapeDtypeStruct((count, n), F32),
            jax.ShapeDtypeStruct(running_cov.shape, F32),
            jax.ShapeDtypeStruct((1, 1), F32),
        ],
        scratch_shapes=[
            pltpu.VMEM((total, n // LANES, LANES), F32),
            pltpu.VMEM((total, n), F32),
            pltpu.VMEM((groups, count, n), F32),
            pltpu.VMEM(running_cov.shape, F32),
            pltpu.SemaphoreType.DMA,
        ],
        compiler_params=params(12),
        name="whiten",
    )(at, *pieces, inverse, running_cov)


def bits(size):
    return [1 << b for b in range(size.bit_length() - 1)]


def swap(x, axis, by):
    size = lax.axis_size(axis)
    return lax.ppermute(x, axis, [(i, i ^ by) for i in range(size)])


def earlier_sum(x, axis):
    size = lax.axis_size(axis)
    me = lax.axis_index(axis)
    prior = jnp.zeros_like(x)
    whole = x
    for by in bits(size):
        upper = (me & by) != 0
        if by == size // 2:
            got = lax.ppermute(whole, axis, [(i, i + by) for i in range(by)])
            prior = prior + got
        else:
            got = swap(whole, axis, by)
            prior = prior + jnp.where(upper, got, 0.0)
            whole = whole + got
    return prior


def body(hidden_states, lengths, w_query, w_key, w_value, w_out, running_cov):
    pairs, two, span, width = hidden_states.shape
    count = pairs * two
    seq, dp = lax.axis_size("seq"), lax.axis_size("dp")
    me, group = lax.axis_index("seq"), lax.axis_index("dp")
    hidden = hidden_states.reshape(count, span, width)
    flat_len = lengths.reshape(count)

    start = (me * span).astype(jnp.int32).reshape(1)
    if seq == 4 and dp == 8 and count == 2:
        white, cov, loss = body_fixed(hidden, flat_len, start, w_query, w_key, w_value, w_out, running_cov)
    else:
        fq, num, den, states = encode(hidden, w_query, w_key, w_value)
        prior = earlier_sum(states, "seq")
        partial = pooled_rows(flat_len, start, hidden, fq, num, den, prior, w_out)
        gathered = lax.all_gather(partial, ("dp", "seq"))
        embed = gathered.reshape(dp, seq, count, width).sum(axis=1).reshape(dp * count, width)
        white, cov, loss = whiten_many(embed, running_cov, count)
    return white.reshape(pairs, two, width), cov, loss


def body_fixed(hidden, flat_len, start, w_query, w_key, w_value, w_out, running_cov):
    me, group = lax.axis_index("seq"), lax.axis_index("dp")
    width = hidden.shape[2]
    half = width // 2
    core = me & 1
    at = jnp.stack([group, me]).astype(jnp.int32)
    chip_columns = lax.dynamic_slice_in_dim(running_cov, (me >> 1) * half, half, 1)
    far_cov = swap(chip_columns, "seq", 2)
    core_cov = swap(running_cov, "seq", 1)
    fq, num, den, states = encode(hidden, w_query, w_key, w_value)
    far_cov, core_cov, states = lax.optimization_barrier((far_cov, core_cov, states))
    core_states = swap(states, "seq", 1)
    far_core_cov = swap(far_cov, "seq", 1)
    quarter = states.shape[0] // 2
    matrix = factor_first((0,), at[1:], running_cov, core_cov, far_cov, far_core_cov)
    core_states, matrix = lax.optimization_barrier((core_states, matrix))
    mine = lax.dynamic_slice_in_dim(states, core * quarter, quarter, 0)
    mine = mine + lax.dynamic_slice_in_dim(core_states, core * quarter, quarter, 0)
    far_half = lax.ppermute(mine, "seq", [(0, 2), (1, 3)])
    matrix = factor_next((1, 2), matrix)
    far_half, matrix = lax.optimization_barrier((far_half, matrix))
    other_half = swap(far_half, "seq", 1)
    matrix = factor_next((3,), matrix)
    other_half, matrix = lax.optimization_barrier((other_half, matrix))
    matrix, partial = factor_next_pool(
        (4,),
        matrix,
        flat_len,
        start,
        core.astype(jnp.int32).reshape(1),
        hidden,
        fq,
        num,
        den,
        w_out,
        far_half,
        other_half,
        core_states,
    )
    got = [swap(partial, "seq", by) for by in (1, 2, 3)]
    matrix = factor_next((5,), matrix)
    partial, got, matrix = lax.optimization_barrier((partial, got, matrix))
    embed = ((partial + got[0]) + (got[1] + got[2]))[None]
    beside = swap(embed, "dp", 1)
    matrix = factor_next((6,), matrix)
    embed, beside, matrix = lax.optimization_barrier((embed, beside, matrix))
    embed = jnp.concatenate([embed, beside], axis=0)
    pieces = [embed] + [swap(embed, "dp", by) for by in (2, 4, 6)]
    matrix = factor_next((7,), matrix)
    white, cov, loss = whiten(at, pieces, matrix, running_cov)
    return white, cov, loss.reshape(())


def whiten_many(embed, running_cov, count):
    total = embed.shape[0]
    share = running_cov.shape[0]
    centred = embed - jnp.sum(embed, axis=0) / total
    full = lax.all_gather(running_cov, "seq", axis=0, tiled=True)
    full = 0.5 * full + (0.5 / (total - 1)) * jnp.dot(centred.T, centred, precision=HIGHEST)
    chol = jnp.linalg.cholesky(full)
    rows = lax.linalg.triangular_solve(chol, centred.T, left_side=True, lower=True).T
    normed = rows / jnp.sqrt(jnp.sum(rows * rows, axis=1, keepdims=True) + 1e-06)
    normed = normed.reshape(total // 2, 2, -1)
    gap = normed[:, 0] - normed[:, 1]
    loss = jnp.sum(gap * gap) / (total // 2)
    white = lax.dynamic_slice_in_dim(rows, lax.axis_index("dp") * count, count, 0)
    cov = lax.dynamic_slice_in_dim(full, lax.axis_index("seq") * share, share, 0)
    return white, cov, loss


def solution(mesh):
    placed = (P("dp", None, "seq", None), P("dp", None), P(), P(), P(), P(), P("seq", None))
    return jax.shard_map(
        body,
        mesh=mesh,
        in_specs=placed,
        out_specs=(P("dp", None, None), P("seq", None), P()),
        check_vma=False,
    )
```

```python
import functools

import jax
import jax.numpy as jnp
from jax import lax
from jax.experimental import pallas as pl
from jax.experimental.pallas import tpu as pltpu
from jax.sharding import PartitionSpec as P

HEADS = 16
HEAD_DIM = 64
LANES = 128
COLS = 256
F32 = jnp.float32
BF16 = jnp.bfloat16
HIGHEST = lax.Precision.HIGHEST
VMEM = pltpu.VMEM
SMEM = pltpu.SMEM


def hbm(x):
    return pltpu.with_memory_space_constraint(x, pltpu.HBM)


def vmem(x):
    return pltpu.with_memory_space_constraint(x, VMEM)


def params(mib):
    return pltpu.CompilerParams(vmem_limit_bytes=mib << 20)


def feature(u):
    return jnp.where(u > 0.0, u + 1.0, jnp.exp(jnp.minimum(u, 0.0)))


def split(x, parts):
    out = []
    for _ in range(parts):
        piece = x.astype(BF16)
        out.append(piece)
        x = x - piece.astype(F32)
    return out


def dot(a, b, ca=1, cb=0):
    return lax.dot_general(a, b, (((ca,), (cb,)), ((), ())), preferred_element_type=F32)


def dot_f32(a, b, ca=1, cb=0):
    return lax.dot_general(
        a, b, (((ca,), (cb,)), ((), ())), precision=HIGHEST, preferred_element_type=F32
    )


def iota(shape, dim):
    return lax.broadcasted_iota(jnp.int32, shape, dim)


def encode_kernel(*refs):
    (hidden_ref, *weight_refs), results = refs[:4], refs[4:8]
    (h_ref, w_ref, *held), (in_sems, out_sems) = refs[8:14], refs[14:]
    steps = w_ref.shape[2] // COLS
    pairs = COLS // LANES

    def window(j):
        return pl.ds(pl.multiple_of(j * COLS, COLS), COLS)

    def arriving(i, j):
        return pltpu.make_async_copy(
            weight_refs[i].at[:, window(j)], w_ref.at[i, :, window(j)], in_sems.at[i, j]
        )

    def blocks(refs, j):
        *arrays, state_ref = refs
        return [x.at[:, :, window(j)] for x in arrays] + [state_ref.at[pl.ds(j * pairs, pairs)]]

    def leaving(j):
        return [
            pltpu.make_async_copy(source, target, out_sems.at[i, j])
            for i, (source, target) in enumerate(zip(blocks(held, j), blocks(results, j)))
        ]

    first = pltpu.make_async_copy(hidden_ref, h_ref, in_sems.at[3, 0])
    first.start()
    for j in range(steps):
        for i in range(3):
            arriving(i, j).start()
    first.wait()

    def run(j, carried):
        for i in range(3):
            arriving(i, j).wait()
        encode_columns(h_ref, *[w_ref.at[i, :, window(j)] for i in range(3)], *blocks(held, j))
        for copy in leaving(j):
            copy.start()
        return carried

    lax.fori_loop(0, steps, run, 0)
    for j in range(steps):
        for copy in leaving(j):
            copy.wait()


def encode_columns(h_ref, wq_ref, wk_ref, wv_ref, fq_ref, num_ref, den_ref, state_ref):
    count, span = h_ref.shape[0], h_ref.shape[1]
    rows = h_ref[...].reshape(count * span, h_ref.shape[2])
    fq = feature(dot(rows, wq_ref[...])).astype(BF16)
    fk = feature(dot(rows, wk_ref[...])).astype(BF16)
    values = dot(rows, wv_ref[...]).astype(BF16)
    fq_ref[...] = fq.reshape(fq_ref.shape)
    causal = iota((span, span), 0) >= iota((span, span), 1)
    ones_below = causal.astype(BF16)
    low = iota((span, LANES), 1) < HEAD_DIM
    same_head = (iota((LANES, LANES), 0) < HEAD_DIM) == (iota((LANES, LANES), 1) < HEAD_DIM)
    summing = jnp.concatenate([same_head.astype(BF16)] * 2, axis=0)
    for module in range(count):
        at = slice(module * span, (module + 1) * span)
        running = dot(ones_below, fk[at])
        for pair in range(COLS // LANES):
            cols = slice(pair * LANES, (pair + 1) * LANES)
            q, k, v = fq[at, cols], fk[at, cols], values[at, cols]
            state = dot(k, v, 0, 0)
            merged = jnp.where(low[:HEAD_DIM], state[:HEAD_DIM], state[HEAD_DIM:])
            state_ref[pair, module] = jnp.concatenate(
                [merged, jnp.broadcast_to(running[span - 1 :, cols], (8, LANES))], axis=0
            )
            hi, lo = split(q.astype(F32) * running[:, cols], 2)
            den_ref[module, :, cols] = dot(jnp.concatenate([hi, lo], axis=1), summing)
            parts = []
            for half in range(2):
                own = low if half == 0 else jnp.logical_not(low)
                scores = dot(jnp.where(own, q, jnp.zeros_like(q)), k, 1, 1)
                weights = jnp.where(causal, scores, 0.0).astype(BF16)
                parts.append(dot(weights, v))
            num_ref[module, :, cols] = jnp.where(low, parts[0], parts[1])


def encode(hidden, w_query, w_key, w_value):
    count, span, width = hidden.shape
    steps = width // COLS
    shape = (count, span, width)
    state_shape = (width // LANES, count, HEAD_DIM + 8, LANES)
    anywhere = pl.BlockSpec(memory_space=pl.ANY)
    results = [(shape, BF16), (shape, F32), (shape, F32), (state_shape, F32)]
    return pl.pallas_call(
        encode_kernel,
        in_specs=[anywhere] * 4,
        out_specs=[anywhere] * 4,
        out_shape=[pltpu.HBM(*x) for x in results],
        scratch_shapes=[VMEM(shape, BF16), VMEM((3, width, width), BF16)]
        + [VMEM(*x) for x in results]
        + [pltpu.SemaphoreType.DMA((4, steps)), pltpu.SemaphoreType.DMA((4, steps))],
        compiler_params=params(24),
        name="encode",
    )(hbm(hidden), hbm(w_query), hbm(w_key), hbm(w_value))


def pool_unit(module, pair, cols, len_ref, start_ref, h_ref, fq_ref, num_ref, den_ref, prior_ref):
    span = fq_ref.shape[1]
    low = iota((HEAD_DIM, LANES), 1) < HEAD_DIM
    same_head = (iota((LANES, LANES), 0) < HEAD_DIM) == (iota((LANES, LANES), 1) < HEAD_DIM)
    summing = jnp.concatenate([same_head.astype(BF16)] * 2, axis=0)
    valid = iota((span, LANES), 0) + start_ref[0] < len_ref[module]
    q = fq_ref[module, :, cols]
    prior = prior_ref[pair, module]
    state = prior[:HEAD_DIM].astype(BF16)
    empty = jnp.zeros_like(state)
    state = jnp.concatenate([jnp.where(low, state, empty), jnp.where(low, empty, state)], axis=0)
    hi, lo = split(q.astype(F32) * prior[HEAD_DIM : HEAD_DIM + 1], 2)
    numer = num_ref[module, :, cols] + dot(q, state)
    denom = den_ref[module, :, cols] + dot(jnp.concatenate([hi, lo], axis=1), summing)
    attended = (numer / denom).astype(BF16).astype(F32)
    plain = h_ref[module, :, cols].astype(F32)
    return [
        jnp.sum(jnp.where(valid, x, 0.0), axis=0, keepdims=True) for x in (attended, plain)
    ]


def project(sums, w_out):
    count = sums.shape[0]
    part = dot(jnp.concatenate(split(sums, 3), axis=0), w_out)
    return part[:count] + part[count : 2 * count] + part[2 * count :]


def pool_columns(step, steps, *refs):
    *sources, wo_ref, out_ref = refs
    len_ref = refs[0]
    count = sources[2].shape[0]
    units = [
        [
            pool_unit(module, pair, slice(pair * LANES, (pair + 1) * LANES), *sources)
            for pair in range(COLS // LANES)
        ]
        for module in range(count)
    ]
    sums, plain = [
        jnp.concatenate([jnp.concatenate([u[i] for u in row], axis=1) for row in units], axis=0)
        for i in range(2)
    ]
    part = project(sums, wo_ref[...])

    @pl.when(step == 0)
    def _():
        out_ref[...] = part

    @pl.when(step > 0)
    def _():
        out_ref[...] += part

    here = pl.ds(pl.multiple_of(step * COLS, COLS), COLS)
    out_ref[:, here] += plain

    @pl.when(step == steps - 1)
    def _():
        for module in range(count):
            out_ref[module : module + 1, :] /= len_ref[module].astype(F32)


def pool_kernel(*refs):
    pool_columns(pl.program_id(0), pl.num_programs(0), *refs)


def pooled_rows(flat_len, start, hidden, fq, num, den, prior, w_out):
    count, span, width = hidden.shape
    block = pl.BlockSpec((count, span, COLS), lambda j: (0, 0, j))
    pairs = COLS // LANES
    return pl.pallas_call(
        pool_kernel,
        grid=(width // COLS,),
        in_specs=[
            pl.BlockSpec(memory_space=SMEM),
            pl.BlockSpec(memory_space=SMEM),
            block,
            block,
            block,
            block,
            pl.BlockSpec((pairs,) + prior.shape[1:], lambda j: (j, 0, 0, 0)),
            pl.BlockSpec((COLS, width), lambda j: (j, 0)),
        ],
        out_specs=pl.BlockSpec((count, width), lambda j: (0, 0)),
        out_shape=jax.ShapeDtypeStruct((count, width), F32),
        compiler_params=params(10),
        name="pool",
    )(flat_len, start, hbm(hidden), hbm(fq), hbm(num), hbm(den), prior, hbm(w_out))


def split_six(x, axis):
    one, two, three = split(x, 3)
    left = jnp.concatenate([one, one, two, two, one, three], axis=axis)
    right = jnp.concatenate([one, two, one, two, three, one], axis=axis)
    return left, right


GROUP = 16
POOL_GAPS = 2


def leaf_factor(mat, jobs=(), later={}):
    groups, tiles = LANES // GROUP, GROUP // 8
    sub, lane = iota((8, LANES), 0), iota((8, LANES), 1)
    rows = [
        [mat[GROUP * g + 8 * v : GROUP * g + 8 * v + 8, :] for v in range(tiles)]
        for g in range(groups)
    ]

    def row_of(x, i):
        return jnp.broadcast_to(x[i : i + 1, :], (8, LANES))

    def col_of(x, c):
        return jnp.broadcast_to(x[:, c : c + 1], (8, LANES))

    for g in range(groups):
        for job in jobs[g::groups]:
            job()
        for job in later.get(g, ()):
            job()
        base = GROUP * g
        own = (lane >= base) & (lane < base + GROUP)
        here = [[col_of(rows[g][v], base + c) for v in range(tiles)] for c in range(GROUP)]
        now = [
            jnp.where(own, (lane - base == sub + 8 * v).astype(F32), rows[g][v])
            for v in range(tiles)
        ]
        following = g + 1 < groups
        if following:
            after = [[col_of(rows[g + 1][v], base + c) for v in range(tiles)] for c in range(GROUP)]
            then = [jnp.where(own, 0.0, rows[g + 1][v]) for v in range(tiles)]
        done = []
        for i in range(GROUP):
            tile, at = divmod(i, 8)
            r = lax.rsqrt(row_of(here[i][tile], at))
            u = row_of(now[tile], at) * r
            done.append(u)
            below = [v for v in range(tile, tiles) if not (v == tile and at == 7)]
            m = {v: here[i][v] * r for v in below}
            for v in below:
                now[v] = now[v] - m[v] * u
            if following:
                mh = [after[i][v] * r for v in range(tiles)]
                then = [then[v] - mh[v] * u for v in range(tiles)]
            for c in range(i + 1, GROUP):
                s = row_of(here[c][tile], at) * r
                for v in below:
                    here[c][v] = here[c][v] - m[v] * s
                if following:
                    after[c] = [after[c][v] - mh[v] * s for v in range(tiles)]
        final = []
        for v in range(tiles):
            x = done[8 * v]
            for i in range(1, 8):
                x = jnp.where(sub == i, done[8 * v + i], x)
            final.append(x)
        rows[g] = final
        if following:
            rows[g + 1] = then
        if g + 2 < groups:
            left, right = split_six(jnp.concatenate(final, axis=0), 0)
            product = dot(left, right, 0, 0)
            for h in range(g + 2, groups):
                rows[h] = [
                    jnp.where(own, 0.0, rows[h][v])
                    - product[GROUP * h + 8 * v : GROUP * h + 8 * v + 8, :]
                    for v in range(tiles)
                ]
    return jnp.concatenate([x for pair in rows for x in pair], axis=0)


def deferred(ref, p):
    n = ref.shape[0]
    panels, k = n // LANES, p + 1
    low, high = p * LANES, k * LANES
    one, two, three = split(ref[low:high, :], 3)
    right = jnp.concatenate([one, two, one, two, three, one], axis=0)
    one, two, three = one[:, high:], two[:, high:], three[:, high:]
    left = jnp.concatenate([one, one, two, two, one, three], axis=0)

    def job(rows, lanes, fresh=False):
        def run():
            product = dot(left[:, : rows.stop - high], right[:, lanes], 0, 0)
            if fresh:
                ref[rows, lanes] = -product
            else:
                ref[rows, lanes] -= product

        return run

    below = slice(high, n)
    jobs = [job(below, slice(low, high), fresh=True)]
    for at in range(0, low, COLS):
        jobs.append(job(below, slice(at, min(at + COLS, low))))
    for b in range(k + 1, panels, 2):
        end = min(b + 2, panels) * LANES
        jobs.append(job(slice(high, end), slice(b * LANES, end)))
    return jobs


def eliminate(ref, k, later={}):
    n = ref.shape[0]
    panels = n // LANES
    low, high = k * LANES, (k + 1) * LANES
    row, col = iota((LANES, LANES), 0), iota((LANES, LANES), 1)
    jobs = deferred(ref, k - 1) if k > 0 else ()
    inverse = jnp.where(col <= row, leaf_factor(ref[low:high, low:high], jobs, later), 0.0)
    if k % 2 == 1:
        ref[low - LANES : low, low:high] = jnp.zeros((LANES, LANES), F32)
    one, two, three = split(inverse, 3)
    left = jnp.concatenate([one, one, two, two, one, three], axis=1)
    ref[low:high, low:high] = inverse
    if k + 1 < panels:
        one, two, three = split(ref[low:high, high:], 3)
        scaled = dot(left, jnp.concatenate([one, two, one, two, three, one], axis=0))
        ref[low:high, high:] = scaled
        coefs, beyond = split_six(scaled[:, :LANES], 0)
        near = slice(high, high + LANES)
        ref[near, near] -= dot(coefs, beyond, 0, 0)
    if k > 0:
        one, two, three = split(ref[low:high, :low], 3)
        ref[low:high, :low] = dot(
            left, jnp.concatenate([one, two, one, two, three, one], axis=0)
        )


def load_kernel(panels, me_ref, own_ref, core_ref, far_ref, far_core_ref, out_ref, sems):
    n = out_ref.shape[0]
    share, half = own_ref.shape[0], n // 2
    me = me_ref[0]
    side = jnp.where(me >= 2, 0, half)
    copies = []
    for slot, ref in enumerate((own_ref, core_ref, far_ref, far_core_ref)):
        block = jnp.bitwise_xor(me, slot)
        to = pl.ds(pl.multiple_of(block * share, share), share)
        if slot < 2:
            target = out_ref.at[to, :]
        else:
            target = out_ref.at[to, pl.ds(pl.multiple_of(side, half), half)]
        copies.append(pltpu.make_async_copy(ref, target, sems.at[slot]))
    for copy in copies:
        copy.start()
    for copy in copies:
        copy.wait()

    @pl.when(me >= 2)
    def _():
        for a in range(0, half, LANES):
            for b in range(0, half, LANES):
                out_ref[a : a + LANES, half + b : half + b + LANES] = out_ref[
                    half + b : half + b + LANES, a : a + LANES
                ].T

    for k in panels:
        eliminate(out_ref, k)


def panels_kernel(panels, in_ref, out_ref):
    del in_ref
    for k in panels:
        eliminate(out_ref, k)


def panels_pool_kernel(panels, in_ref, len_ref, start_ref, core_ref, *refs):
    del in_ref
    *sources, matrix_ref, out_ref = refs[:10]
    *held, prior_ref, beside_ref, sums_ref, plain_ref, sems = refs[10:]
    half = prior_ref.shape[0] // 2
    own = pl.ds(core_ref[0] * half, half)
    other = pl.ds((1 - core_ref[0]) * half, half)
    targets = held + [prior_ref.at[own], prior_ref.at[other], beside_ref]
    copies = [
        pltpu.make_async_copy(source, to, sems.at[i])
        for i, (source, to) in enumerate(zip(sources, targets))
    ]
    h_ref, fq_ref, num_ref, den_ref, wo_ref = held
    last = copies.pop(4)
    for copy in copies + [last]:
        copy.start()

    def arrived():
        for copy in copies:
            copy.wait()

        @pl.when(core_ref[0] == 1)
        def _():
            prior_ref[...] += beside_ref[...]

    def unit(module, pair):
        def run():
            cols = slice(pair * LANES, (pair + 1) * LANES)
            rows = slice(module, module + 1)
            sums_ref[rows, cols], plain_ref[rows, cols] = pool_unit(
                module, pair, cols, len_ref, start_ref, h_ref, fq_ref, num_ref, den_ref, prior_ref
            )

        return run

    count = h_ref.shape[0]
    units = [unit(m, pair) for pair in range(prior_ref.shape[0]) for m in range(count)]
    groups = LANES // GROUP
    gaps = range(groups - POOL_GAPS, groups)
    later = {g: units[i::POOL_GAPS] for i, g in enumerate(gaps)}
    later[gaps[0]] = [arrived] + later[gaps[0]]
    for k in panels:
        eliminate(matrix_ref, k, later if k == panels[-1] else {})
    last.wait()
    pooled = plain_ref[...] + project(sums_ref[...], wo_ref[...])
    for module in range(count):
        out_ref[module : module + 1, :] = pooled[module : module + 1] / len_ref[module].astype(F32)


def factor_next_pool(
    panels, matrix, flat_len, start, core, hidden, fq, num, den, w_out, far_half, other_half, beside
):
    n = matrix.shape[1]
    count, span, width = hidden.shape
    whole, anywhere = pl.BlockSpec(memory_space=VMEM), pl.BlockSpec(memory_space=pl.ANY)
    operands = [hbm(x) for x in (hidden, fq, num, den, w_out)]
    states = [far_half, other_half, beside]
    return pl.pallas_call(
        functools.partial(panels_pool_kernel, panels),
        in_specs=[whole] + [pl.BlockSpec(memory_space=SMEM)] * 3 + [anywhere] * 8,
        out_specs=[whole, whole],
        out_shape=[pltpu.VMEM((n, n), F32), jax.ShapeDtypeStruct((count, width), F32)],
        scratch_shapes=[pltpu.VMEM(x.shape, x.dtype) for x in operands + [beside, beside]]
        + [pltpu.VMEM((count, width), F32)] * 2
        + [pltpu.SemaphoreType.DMA((8,))],
        input_output_aliases={0: 0},
        compiler_params=params(24),
        name="factor_next_pool",
        cost_estimate=pl.CostEstimate(flops=8_000_000_000, transcendentals=0, bytes_accessed=12 << 20),
    )(vmem(matrix), flat_len, start, core, *operands, *states)


def factor_first(panels, me, own, core, far, far_core):
    n = own.shape[1]
    anywhere = pl.BlockSpec(memory_space=pl.ANY)
    return pl.pallas_call(
        functools.partial(load_kernel, panels),
        in_specs=[pl.BlockSpec(memory_space=SMEM)] + [anywhere] * 4,
        out_specs=pl.BlockSpec(memory_space=VMEM),
        out_shape=pltpu.VMEM((n, n), F32),
        scratch_shapes=[pltpu.SemaphoreType.DMA((4,))],
        compiler_params=params(14),
        name="factor_first",
        cost_estimate=pl.CostEstimate(flops=8_000_000_000, transcendentals=0, bytes_accessed=4 << 20),
    )(me, own, core, far, far_core)


def factor_next(panels, matrix):
    n = matrix.shape[1]
    return pl.pallas_call(
        functools.partial(panels_kernel, panels),
        in_specs=[pl.BlockSpec(memory_space=VMEM)],
        out_specs=pl.BlockSpec(memory_space=VMEM),
        out_shape=pltpu.VMEM((n, n), F32),
        input_output_aliases={0: 0},
        compiler_params=params(14),
        name="factor_next",
        cost_estimate=pl.CostEstimate(flops=8_000_000_000, transcendentals=0, bytes_accessed=4 << 20),
    )(vmem(matrix))


def whiten_kernel(
    at_ref, *refs
):
    *piece_refs, inv_ref, cov_ref, white_ref, cov_out_ref, loss_ref = refs[:-5]
    rows_ref, centred_ref, held_ref, new_cov_ref, sem = refs[-5:]
    count, n = white_ref.shape
    total = centred_ref.shape[0]
    chunks = n // LANES
    share = cov_ref.shape[0]
    slot = 0
    for ref in piece_refs:
        for b in range(ref.shape[0]):
            held_ref[slot] = ref[b]
            slot += 1
    embed = jnp.concatenate(
        [held_ref[jnp.bitwise_xor(at_ref[0], d)] for d in range(total // count)], axis=0
    )
    centred = embed - jnp.sum(embed, axis=0, keepdims=True) / total
    weight = 0.5 / (total - 1)
    root = 2.0**0.5
    start = pl.multiple_of(at_ref[1] * share, share)
    centred_ref[...] = centred
    left, right = split_six(centred_ref[:, pl.ds(start, share)], 0)[0], split_six(centred, 0)[1]
    new_cov_ref[...] = 0.5 * cov_ref[...] + weight * dot(left, right, 0, 0)
    written = pltpu.make_async_copy(new_cov_ref, cov_out_ref, sem)
    written.start()
    thirds = jnp.concatenate(split(root * centred, 3), axis=0)
    for k in range(0, chunks, 2):
        upto = (k + 2) * LANES
        one, two, three = split(inv_ref[k * LANES : upto, :upto], 3)
        by_one = dot(thirds[:, :upto], one, 1, 1)
        by_two = dot(thirds[: 2 * total, :upto], two, 1, 1)
        product = by_one[:total] + (by_one[total : 2 * total] + by_two[:total])
        product = product + (
            by_one[2 * total :] + by_two[total:] + dot(thirds[:total, :upto], three, 1, 1)
        )
        rows_ref[:, k, :] = product[:, :LANES]
        rows_ref[:, k + 1, :] = product[:, LANES:]
    w = [rows_ref[a] for a in range(total)]
    pairs = [(a, b) for a in range(total) for b in range(a, total)]
    products = jnp.concatenate([w[a] * w[b] for a, b in pairs], axis=0)
    before = iota((LANES, 2 * LANES), 0) < iota((LANES, 2 * LANES), 1)
    earlier = before.astype(BF16)
    sums = [dot(piece, earlier) for piece in split(products, 3)]
    sums = sums[0] + sums[1] + sums[2]
    chunk = iota((8, LANES), 0)
    entry = {}
    for i, (a, b) in enumerate(pairs):
        inside = sums[8 * i : 8 * i + 8, :LANES]
        whole = sums[8 * i : 8 * i + 8, LANES:]
        carry = jnp.where(chunk >= 1, pltpu.roll(whole, 1, 0), 0.0)
        for by in (1, 2, 4):
            carry = carry + jnp.where(chunk >= by, pltpu.roll(carry, by, 0), 0.0)
        entry[a, b] = weight * (inside + carry) + (1.0 if a == b else 0.0)
    right = list(w)
    inverse = []
    spread = jnp.ones((8, LANES), F32)
    for p in range(total):
        inv = 1.0 / entry[p, p]
        inverse.append(inv)
        spread = spread + weight * right[p] * right[p] * inv
        for a in range(p + 1, total):
            f = entry[p, a] * inv
            for b in range(a, total):
                entry[a, b] = entry[a, b] - f * entry[p, b]
            right[a] = right[a] - f * right[p]
    scale = lax.rsqrt(spread)
    solved = [None] * total
    for p in reversed(range(total)):
        x = right[p]
        for b in range(p + 1, total):
            x = x - entry[p, b] * solved[b]
        solved[p] = x * inverse[p]
    solved = [x * scale for x in solved]
    gap = jnp.zeros((8, LANES), F32)
    normed = []
    for a in range(total):
        norm = jnp.sum(jnp.sum(solved[a] * solved[a], axis=1, keepdims=True), axis=0, keepdims=True)
        normed.append(solved[a] / jnp.sqrt(norm + 1e-06))
    for pair in range(total // 2):
        diff = normed[2 * pair] - normed[2 * pair + 1]
        gap = gap + diff * diff
    gap = jnp.sum(jnp.sum(gap, axis=1, keepdims=True), axis=0, keepdims=True)
    loss_ref[...] = gap / (total // 2)
    for a in range(total):
        rows_ref[a] = solved[a]
    for m in range(count):
        own = rows_ref[at_ref[0] * count + m]
        for k in range(chunks):
            white_ref[m : m + 1, k * LANES : (k + 1) * LANES] = own[k : k + 1, :]
    written.wait()


def whiten(at, pieces, inverse, running_cov):
    groups = sum(piece.shape[0] for piece in pieces)
    count, n = pieces[0].shape[1:]
    total = groups * count
    whole = pl.BlockSpec(memory_space=VMEM)
    return pl.pallas_call(
        whiten_kernel,
        in_specs=[pl.BlockSpec(memory_space=SMEM)] + [whole] * (len(pieces) + 2),
        out_specs=[whole, pl.BlockSpec(memory_space=pl.ANY), whole],
        out_shape=[
            jax.ShapeDtypeStruct((count, n), F32),
            jax.ShapeDtypeStruct(running_cov.shape, F32),
            jax.ShapeDtypeStruct((1, 1), F32),
        ],
        scratch_shapes=[
            pltpu.VMEM((total, n // LANES, LANES), F32),
            pltpu.VMEM((total, n), F32),
            pltpu.VMEM((groups, count, n), F32),
            pltpu.VMEM(running_cov.shape, F32),
            pltpu.SemaphoreType.DMA,
        ],
        compiler_params=params(12),
        name="whiten",
    )(at, *pieces, inverse, running_cov)


def bits(size):
    return [1 << b for b in range(size.bit_length() - 1)]


def swap(x, axis, by):
    size = lax.axis_size(axis)
    return lax.ppermute(x, axis, [(i, i ^ by) for i in range(size)])


def earlier_sum(x, axis):
    size = lax.axis_size(axis)
    me = lax.axis_index(axis)
    prior = jnp.zeros_like(x)
    whole = x
    for by in bits(size):
        upper = (me & by) != 0
        if by == size // 2:
            got = lax.ppermute(whole, axis, [(i, i + by) for i in range(by)])
            prior = prior + got
        else:
            got = swap(whole, axis, by)
            prior = prior + jnp.where(upper, got, 0.0)
            whole = whole + got
    return prior


def body(hidden_states, lengths, w_query, w_key, w_value, w_out, running_cov):
    pairs, two, span, width = hidden_states.shape
    count = pairs * two
    seq, dp = lax.axis_size("seq"), lax.axis_size("dp")
    me, group = lax.axis_index("seq"), lax.axis_index("dp")
    hidden = hidden_states.reshape(count, span, width)
    flat_len = lengths.reshape(count)

    start = (me * span).astype(jnp.int32).reshape(1)
    if seq == 4 and dp == 8 and count == 2:
        white, cov, loss = body_fixed(hidden, flat_len, start, w_query, w_key, w_value, w_out, running_cov)
    else:
        fq, num, den, states = encode(hidden, w_query, w_key, w_value)
        prior = earlier_sum(states, "seq")
        partial = pooled_rows(flat_len, start, hidden, fq, num, den, prior, w_out)
        gathered = lax.all_gather(partial, ("dp", "seq"))
        embed = gathered.reshape(dp, seq, count, width).sum(axis=1).reshape(dp * count, width)
        white, cov, loss = whiten_many(embed, running_cov, count)
    return white.reshape(pairs, two, width), cov, loss


def body_fixed(hidden, flat_len, start, w_query, w_key, w_value, w_out, running_cov):
    me, group = lax.axis_index("seq"), lax.axis_index("dp")
    width = hidden.shape[2]
    half = width // 2
    core = me & 1
    at = jnp.stack([group, me]).astype(jnp.int32)
    chip_columns = lax.dynamic_slice_in_dim(running_cov, (me >> 1) * half, half, 1)
    far_cov = swap(chip_columns, "seq", 2)
    core_cov = swap(running_cov, "seq", 1)
    fq, num, den, states = encode(hidden, w_query, w_key, w_value)
    far_cov, core_cov, states = lax.optimization_barrier((far_cov, core_cov, states))
    core_states = swap(states, "seq", 1)
    far_core_cov = swap(far_cov, "seq", 1)
    quarter = states.shape[0] // 2
    matrix = factor_first((0,), at[1:], running_cov, core_cov, far_cov, far_core_cov)
    core_states, matrix = lax.optimization_barrier((core_states, matrix))
    mine = lax.dynamic_slice_in_dim(states, core * quarter, quarter, 0)
    mine = mine + lax.dynamic_slice_in_dim(core_states, core * quarter, quarter, 0)
    far_half = lax.ppermute(mine, "seq", [(0, 2), (1, 3)])
    matrix = factor_next((1, 2), matrix)
    far_half, matrix = lax.optimization_barrier((far_half, matrix))
    other_half = swap(far_half, "seq", 1)
    matrix = factor_next((3,), matrix)
    other_half, matrix = lax.optimization_barrier((other_half, matrix))
    matrix, partial = factor_next_pool(
        (4,),
        matrix,
        flat_len,
        start,
        core.astype(jnp.int32).reshape(1),
        hidden,
        fq,
        num,
        den,
        w_out,
        far_half,
        other_half,
        core_states,
    )
    got = [swap(partial, "seq", by) for by in (1, 2, 3)]
    matrix = factor_next((5,), matrix)
    partial, got, matrix = lax.optimization_barrier((partial, got, matrix))
    embed = ((partial + got[0]) + (got[1] + got[2]))[None]
    near = [swap(embed, "dp", by) for by in (1, 2, 3)]
    matrix = factor_next((6,), matrix)
    embed, near, matrix = lax.optimization_barrier((embed, near, matrix))
    embed = jnp.concatenate([embed] + near, axis=0)
    pieces = [embed, swap(embed, "dp", 4)]
    matrix = factor_next((7,), matrix)
    white, cov, loss = whiten(at, pieces, matrix, running_cov)
    return white, cov, loss.reshape(())


def whiten_many(embed, running_cov, count):
    total = embed.shape[0]
    share = running_cov.shape[0]
    centred = embed - jnp.sum(embed, axis=0) / total
    full = lax.all_gather(running_cov, "seq", axis=0, tiled=True)
    full = 0.5 * full + (0.5 / (total - 1)) * jnp.dot(centred.T, centred, precision=HIGHEST)
    chol = jnp.linalg.cholesky(full)
    rows = lax.linalg.triangular_solve(chol, centred.T, left_side=True, lower=True).T
    normed = rows / jnp.sqrt(jnp.sum(rows * rows, axis=1, keepdims=True) + 1e-06)
    normed = normed.reshape(total // 2, 2, -1)
    gap = normed[:, 0] - normed[:, 1]
    loss = jnp.sum(gap * gap) / (total // 2)
    white = lax.dynamic_slice_in_dim(rows, lax.axis_index("dp") * count, count, 0)
    cov = lax.dynamic_slice_in_dim(full, lax.axis_index("seq") * share, share, 0)
    return white, cov, loss


def solution(mesh):
    placed = (P("dp", None, "seq", None), P("dp", None), P(), P(), P(), P(), P("seq", None))
    return jax.shard_map(
        body,
        mesh=mesh,
        in_specs=placed,
        out_specs=(P("dp", None, None), P("seq", None), P()),
        check_vma=False,
    )
```

```python
import functools

import jax
import jax.numpy as jnp
from jax import lax
from jax.experimental import pallas as pl
from jax.experimental.pallas import tpu as pltpu
from jax.sharding import PartitionSpec as P

HEADS = 16
HEAD_DIM = 64
LANES = 128
COLS = 256
WIDE = 512
F32 = jnp.float32
BF16 = jnp.bfloat16
HIGHEST = lax.Precision.HIGHEST
VMEM = pltpu.VMEM
SMEM = pltpu.SMEM


def hbm(x):
    return pltpu.with_memory_space_constraint(x, pltpu.HBM)


def vmem(x):
    return pltpu.with_memory_space_constraint(x, VMEM)


def params(mib):
    return pltpu.CompilerParams(vmem_limit_bytes=mib << 20)


def feature(u):
    return jnp.where(u > 0.0, u + 1.0, jnp.exp(jnp.minimum(u, 0.0)))


def split(x, parts):
    out = []
    for _ in range(parts):
        piece = x.astype(BF16)
        out.append(piece)
        x = x - piece.astype(F32)
    return out


def dot(a, b, ca=1, cb=0):
    return lax.dot_general(a, b, (((ca,), (cb,)), ((), ())), preferred_element_type=F32)


def dot_f32(a, b, ca=1, cb=0):
    return lax.dot_general(
        a, b, (((ca,), (cb,)), ((), ())), precision=HIGHEST, preferred_element_type=F32
    )


def iota(shape, dim):
    return lax.broadcasted_iota(jnp.int32, shape, dim)


def encode_kernel(*refs):
    (hidden_ref, *weight_refs), results = refs[:4], refs[4:8]
    (h_ref, w_ref, *held), (in_sems, out_sems) = refs[8:14], refs[14:]
    steps = w_ref.shape[2] // WIDE
    pairs = WIDE // LANES

    def window(j):
        return pl.ds(pl.multiple_of(j * WIDE, WIDE), WIDE)

    def arriving(i, j):
        return pltpu.make_async_copy(
            weight_refs[i].at[:, window(j)], w_ref.at[i, :, window(j)], in_sems.at[i, j]
        )

    def blocks(refs, j):
        *arrays, state_ref = refs
        return [x.at[:, :, window(j)] for x in arrays] + [state_ref.at[pl.ds(j * pairs, pairs)]]

    def leaving(j):
        return [
            pltpu.make_async_copy(source, target, out_sems.at[i, j])
            for i, (source, target) in enumerate(zip(blocks(held, j), blocks(results, j)))
        ]

    first = pltpu.make_async_copy(hidden_ref, h_ref, in_sems.at[3, 0])
    first.start()
    for j in range(steps):
        for i in range(3):
            arriving(i, j).start()
    first.wait()

    def run(j, carried):
        for i in range(3):
            arriving(i, j).wait()
        encode_columns(h_ref, *[w_ref.at[i, :, window(j)] for i in range(3)], *blocks(held, j))
        for copy in leaving(j):
            copy.start()
        return carried

    lax.fori_loop(0, steps, run, 0)
    for j in range(steps):
        for copy in leaving(j):
            copy.wait()


def encode_columns(h_ref, wq_ref, wk_ref, wv_ref, fq_ref, num_ref, den_ref, state_ref):
    count, span = h_ref.shape[0], h_ref.shape[1]
    rows = h_ref[...].reshape(count * span, h_ref.shape[2])
    fq = feature(dot(rows, wq_ref[...])).astype(BF16)
    fk = feature(dot(rows, wk_ref[...])).astype(BF16)
    values = dot(rows, wv_ref[...]).astype(BF16)
    fq_ref[...] = fq.reshape(fq_ref.shape)
    causal = iota((span, span), 0) >= iota((span, span), 1)
    ones_below = causal.astype(BF16)
    low = iota((span, LANES), 1) < HEAD_DIM
    same_head = (iota((LANES, LANES), 0) < HEAD_DIM) == (iota((LANES, LANES), 1) < HEAD_DIM)
    summing = jnp.concatenate([same_head.astype(BF16)] * 2, axis=0)
    for module in range(count):
        at = slice(module * span, (module + 1) * span)
        running = dot(ones_below, fk[at])
        for pair in range(WIDE // LANES):
            cols = slice(pair * LANES, (pair + 1) * LANES)
            q, k, v = fq[at, cols], fk[at, cols], values[at, cols]
            state = dot(k, v, 0, 0)
            merged = jnp.where(low[:HEAD_DIM], state[:HEAD_DIM], state[HEAD_DIM:])
            state_ref[pair, module] = jnp.concatenate(
                [merged, jnp.broadcast_to(running[span - 1 :, cols], (8, LANES))], axis=0
            )
            hi, lo = split(q.astype(F32) * running[:, cols], 2)
            den_ref[module, :, cols] = dot(jnp.concatenate([hi, lo], axis=1), summing)
            parts = []
            for half in range(2):
                own = low if half == 0 else jnp.logical_not(low)
                scores = dot(jnp.where(own, q, jnp.zeros_like(q)), k, 1, 1)
                weights = jnp.where(causal, scores, 0.0).astype(BF16)
                parts.append(dot(weights, v))
            num_ref[module, :, cols] = jnp.where(low, parts[0], parts[1])


def encode(hidden, w_query, w_key, w_value):
    count, span, width = hidden.shape
    steps = width // WIDE
    shape = (count, span, width)
    state_shape = (width // LANES, count, HEAD_DIM + 8, LANES)
    anywhere = pl.BlockSpec(memory_space=pl.ANY)
    results = [(shape, BF16), (shape, F32), (shape, F32), (state_shape, F32)]
    return pl.pallas_call(
        encode_kernel,
        in_specs=[anywhere] * 4,
        out_specs=[anywhere] * 4,
        out_shape=[pltpu.HBM(*x) for x in results],
        scratch_shapes=[VMEM(shape, BF16), VMEM((3, width, width), BF16)]
        + [VMEM(*x) for x in results]
        + [pltpu.SemaphoreType.DMA((4, steps)), pltpu.SemaphoreType.DMA((4, steps))],
        compiler_params=params(28),
        name="encode",
    )(hbm(hidden), hbm(w_query), hbm(w_key), hbm(w_value))


def pool_unit(module, pair, cols, len_ref, start_ref, h_ref, fq_ref, num_ref, den_ref, prior_ref):
    span = fq_ref.shape[1]
    low = iota((HEAD_DIM, LANES), 1) < HEAD_DIM
    same_head = (iota((LANES, LANES), 0) < HEAD_DIM) == (iota((LANES, LANES), 1) < HEAD_DIM)
    summing = jnp.concatenate([same_head.astype(BF16)] * 2, axis=0)
    valid = iota((span, LANES), 0) + start_ref[0] < len_ref[module]
    q = fq_ref[module, :, cols]
    prior = prior_ref[pair, module]
    state = prior[:HEAD_DIM].astype(BF16)
    empty = jnp.zeros_like(state)
    state = jnp.concatenate([jnp.where(low, state, empty), jnp.where(low, empty, state)], axis=0)
    hi, lo = split(q.astype(F32) * prior[HEAD_DIM : HEAD_DIM + 1], 2)
    numer = num_ref[module, :, cols] + dot(q, state)
    denom = den_ref[module, :, cols] + dot(jnp.concatenate([hi, lo], axis=1), summing)
    attended = (numer / denom).astype(BF16).astype(F32)
    plain = h_ref[module, :, cols].astype(F32)
    return [
        jnp.sum(jnp.where(valid, x, 0.0), axis=0, keepdims=True) for x in (attended, plain)
    ]


def project(sums, w_out):
    count = sums.shape[0]
    part = dot(jnp.concatenate(split(sums, 3), axis=0), w_out)
    return part[:count] + part[count : 2 * count] + part[2 * count :]


def pool_columns(step, steps, *refs):
    *sources, wo_ref, out_ref = refs
    len_ref = refs[0]
    count = sources[2].shape[0]
    units = [
        [
            pool_unit(module, pair, slice(pair * LANES, (pair + 1) * LANES), *sources)
            for pair in range(COLS // LANES)
        ]
        for module in range(count)
    ]
    sums, plain = [
        jnp.concatenate([jnp.concatenate([u[i] for u in row], axis=1) for row in units], axis=0)
        for i in range(2)
    ]
    part = project(sums, wo_ref[...])

    @pl.when(step == 0)
    def _():
        out_ref[...] = part

    @pl.when(step > 0)
    def _():
        out_ref[...] += part

    here = pl.ds(pl.multiple_of(step * COLS, COLS), COLS)
    out_ref[:, here] += plain

    @pl.when(step == steps - 1)
    def _():
        for module in range(count):
            out_ref[module : module + 1, :] /= len_ref[module].astype(F32)


def pool_kernel(*refs):
    pool_columns(pl.program_id(0), pl.num_programs(0), *refs)


def pooled_rows(flat_len, start, hidden, fq, num, den, prior, w_out):
    count, span, width = hidden.shape
    block = pl.BlockSpec((count, span, COLS), lambda j: (0, 0, j))
    pairs = COLS // LANES
    return pl.pallas_call(
        pool_kernel,
        grid=(width // COLS,),
        in_specs=[
            pl.BlockSpec(memory_space=SMEM),
            pl.BlockSpec(memory_space=SMEM),
            block,
            block,
            block,
            block,
            pl.BlockSpec((pairs,) + prior.shape[1:], lambda j: (j, 0, 0, 0)),
            pl.BlockSpec((COLS, width), lambda j: (j, 0)),
        ],
        out_specs=pl.BlockSpec((count, width), lambda j: (0, 0)),
        out_shape=jax.ShapeDtypeStruct((count, width), F32),
        compiler_params=params(10),
        name="pool",
    )(flat_len, start, hbm(hidden), hbm(fq), hbm(num), hbm(den), prior, hbm(w_out))


def split_six(x, axis):
    one, two, three = split(x, 3)
    left = jnp.concatenate([one, one, two, two, one, three], axis=axis)
    right = jnp.concatenate([one, two, one, two, three, one], axis=axis)
    return left, right


GROUP = 16
POOL_GAPS = 2


def leaf_factor(mat, jobs=(), later={}):
    groups, tiles = LANES // GROUP, GROUP // 8
    sub, lane = iota((8, LANES), 0), iota((8, LANES), 1)
    rows = [
        [mat[GROUP * g + 8 * v : GROUP * g + 8 * v + 8, :] for v in range(tiles)]
        for g in range(groups)
    ]

    def row_of(x, i):
        return jnp.broadcast_to(x[i : i + 1, :], (8, LANES))

    def col_of(x, c):
        return jnp.broadcast_to(x[:, c : c + 1], (8, LANES))

    for g in range(groups):
        for job in jobs[g::groups]:
            job()
        for job in later.get(g, ()):
            job()
        base = GROUP * g
        own = (lane >= base) & (lane < base + GROUP)
        here = [[col_of(rows[g][v], base + c) for v in range(tiles)] for c in range(GROUP)]
        now = [
            jnp.where(own, (lane - base == sub + 8 * v).astype(F32), rows[g][v])
            for v in range(tiles)
        ]
        following = g + 1 < groups
        if following:
            after = [[col_of(rows[g + 1][v], base + c) for v in range(tiles)] for c in range(GROUP)]
            then = [jnp.where(own, 0.0, rows[g + 1][v]) for v in range(tiles)]
        done = []
        for i in range(GROUP):
            tile, at = divmod(i, 8)
            r = lax.rsqrt(row_of(here[i][tile], at))
            u = row_of(now[tile], at) * r
            done.append(u)
            below = [v for v in range(tile, tiles) if not (v == tile and at == 7)]
            m = {v: here[i][v] * r for v in below}
            for v in below:
                now[v] = now[v] - m[v] * u
            if following:
                mh = [after[i][v] * r for v in range(tiles)]
                then = [then[v] - mh[v] * u for v in range(tiles)]
            for c in range(i + 1, GROUP):
                s = row_of(here[c][tile], at) * r
                for v in below:
                    here[c][v] = here[c][v] - m[v] * s
                if following:
                    after[c] = [after[c][v] - mh[v] * s for v in range(tiles)]
        final = []
        for v in range(tiles):
            x = done[8 * v]
            for i in range(1, 8):
                x = jnp.where(sub == i, done[8 * v + i], x)
            final.append(x)
        rows[g] = final
        if following:
            rows[g + 1] = then
        if g + 2 < groups:
            left, right = split_six(jnp.concatenate(final, axis=0), 0)
            product = dot(left, right, 0, 0)
            for h in range(g + 2, groups):
                rows[h] = [
                    jnp.where(own, 0.0, rows[h][v])
                    - product[GROUP * h + 8 * v : GROUP * h + 8 * v + 8, :]
                    for v in range(tiles)
                ]
    return jnp.concatenate([x for pair in rows for x in pair], axis=0)


def deferred(ref, p):
    n = ref.shape[0]
    panels, k = n // LANES, p + 1
    low, high = p * LANES, k * LANES
    one, two, three = split(ref[low:high, :], 3)
    right = jnp.concatenate([one, two, one, two, three, one], axis=0)
    one, two, three = one[:, high:], two[:, high:], three[:, high:]
    left = jnp.concatenate([one, one, two, two, one, three], axis=0)

    def job(rows, lanes, fresh=False):
        def run():
            product = dot(left[:, : rows.stop - high], right[:, lanes], 0, 0)
            if fresh:
                ref[rows, lanes] = -product
            else:
                ref[rows, lanes] -= product

        return run

    below = slice(high, n)
    jobs = [job(below, slice(low, high), fresh=True)]
    for at in range(0, low, COLS):
        jobs.append(job(below, slice(at, min(at + COLS, low))))
    for b in range(k + 1, panels, 2):
        end = min(b + 2, panels) * LANES
        jobs.append(job(slice(high, end), slice(b * LANES, end)))
    return jobs


def eliminate(ref, k, later={}):
    n = ref.shape[0]
    panels = n // LANES
    low, high = k * LANES, (k + 1) * LANES
    row, col = iota((LANES, LANES), 0), iota((LANES, LANES), 1)
    jobs = deferred(ref, k - 1) if k > 0 else ()
    inverse = jnp.where(col <= row, leaf_factor(ref[low:high, low:high], jobs, later), 0.0)
    if k % 2 == 1:
        ref[low - LANES : low, low:high] = jnp.zeros((LANES, LANES), F32)
    one, two, three = split(inverse, 3)
    left = jnp.concatenate([one, one, two, two, one, three], axis=1)
    ref[low:high, low:high] = inverse
    if k + 1 < panels:
        one, two, three = split(ref[low:high, high:], 3)
        scaled = dot(left, jnp.concatenate([one, two, one, two, three, one], axis=0))
        ref[low:high, high:] = scaled
        coefs, beyond = split_six(scaled[:, :LANES], 0)
        near = slice(high, high + LANES)
        ref[near, near] -= dot(coefs, beyond, 0, 0)
    if k > 0:
        one, two, three = split(ref[low:high, :low], 3)
        ref[low:high, :low] = dot(
            left, jnp.concatenate([one, two, one, two, three, one], axis=0)
        )


def load_kernel(panels, me_ref, own_ref, core_ref, far_ref, far_core_ref, out_ref, sems):
    n = out_ref.shape[0]
    share, half = own_ref.shape[0], n // 2
    me = me_ref[0]
    side = jnp.where(me >= 2, 0, half)
    copies = []
    for slot, ref in enumerate((own_ref, core_ref, far_ref, far_core_ref)):
        block = jnp.bitwise_xor(me, slot)
        to = pl.ds(pl.multiple_of(block * share, share), share)
        if slot < 2:
            target = out_ref.at[to, :]
        else:
            target = out_ref.at[to, pl.ds(pl.multiple_of(side, half), half)]
        copies.append(pltpu.make_async_copy(ref, target, sems.at[slot]))
    for copy in copies:
        copy.start()
    for copy in copies:
        copy.wait()

    @pl.when(me >= 2)
    def _():
        for a in range(0, half, LANES):
            for b in range(0, half, LANES):
                out_ref[a : a + LANES, half + b : half + b + LANES] = out_ref[
                    half + b : half + b + LANES, a : a + LANES
                ].T

    for k in panels:
        eliminate(out_ref, k)


def panels_kernel(panels, in_ref, out_ref):
    del in_ref
    for k in panels:
        eliminate(out_ref, k)


def panels_pool_kernel(panels, in_ref, len_ref, start_ref, core_ref, *refs):
    del in_ref
    *sources, matrix_ref, out_ref = refs[:10]
    *held, prior_ref, beside_ref, sums_ref, plain_ref, sems = refs[10:]
    half = prior_ref.shape[0] // 2
    own = pl.ds(core_ref[0] * half, half)
    other = pl.ds((1 - core_ref[0]) * half, half)
    targets = held + [prior_ref.at[own], prior_ref.at[other], beside_ref]
    copies = [
        pltpu.make_async_copy(source, to, sems.at[i])
        for i, (source, to) in enumerate(zip(sources, targets))
    ]
    h_ref, fq_ref, num_ref, den_ref, wo_ref = held
    last = copies.pop(4)
    for copy in copies + [last]:
        copy.start()

    def arrived():
        for copy in copies:
            copy.wait()

        @pl.when(core_ref[0] == 1)
        def _():
            prior_ref[...] += beside_ref[...]

    def unit(module, pair):
        def run():
            cols = slice(pair * LANES, (pair + 1) * LANES)
            rows = slice(module, module + 1)
            sums_ref[rows, cols], plain_ref[rows, cols] = pool_unit(
                module, pair, cols, len_ref, start_ref, h_ref, fq_ref, num_ref, den_ref, prior_ref
            )

        return run

    count = h_ref.shape[0]
    units = [unit(m, pair) for pair in range(prior_ref.shape[0]) for m in range(count)]
    groups = LANES // GROUP
    gaps = range(groups - POOL_GAPS, groups)
    later = {g: units[i::POOL_GAPS] for i, g in enumerate(gaps)}
    later[gaps[0]] = [arrived] + later[gaps[0]]
    for k in panels:
        eliminate(matrix_ref, k, later if k == panels[-1] else {})
    last.wait()
    pooled = plain_ref[...] + project(sums_ref[...], wo_ref[...])
    for module in range(count):
        out_ref[module : module + 1, :] = pooled[module : module + 1] / len_ref[module].astype(F32)


def factor_next_pool(
    panels, matrix, flat_len, start, core, hidden, fq, num, den, w_out, far_half, other_half, beside
):
    n = matrix.shape[1]
    count, span, width = hidden.shape
    whole, anywhere = pl.BlockSpec(memory_space=VMEM), pl.BlockSpec(memory_space=pl.ANY)
    operands = [hbm(x) for x in (hidden, fq, num, den, w_out)]
    states = [far_half, other_half, beside]
    return pl.pallas_call(
        functools.partial(panels_pool_kernel, panels),
        in_specs=[whole] + [pl.BlockSpec(memory_space=SMEM)] * 3 + [anywhere] * 8,
        out_specs=[whole, whole],
        out_shape=[pltpu.VMEM((n, n), F32), jax.ShapeDtypeStruct((count, width), F32)],
        scratch_shapes=[pltpu.VMEM(x.shape, x.dtype) for x in operands + [beside, beside]]
        + [pltpu.VMEM((count, width), F32)] * 2
        + [pltpu.SemaphoreType.DMA((8,))],
        input_output_aliases={0: 0},
        compiler_params=params(24),
        name="factor_next_pool",
        cost_estimate=pl.CostEstimate(flops=8_000_000_000, transcendentals=0, bytes_accessed=12 << 20),
    )(vmem(matrix), flat_len, start, core, *operands, *states)


def factor_first(panels, me, own, core, far, far_core):
    n = own.shape[1]
    anywhere = pl.BlockSpec(memory_space=pl.ANY)
    return pl.pallas_call(
        functools.partial(load_kernel, panels),
        in_specs=[pl.BlockSpec(memory_space=SMEM)] + [anywhere] * 4,
        out_specs=pl.BlockSpec(memory_space=VMEM),
        out_shape=pltpu.VMEM((n, n), F32),
        scratch_shapes=[pltpu.SemaphoreType.DMA((4,))],
        compiler_params=params(14),
        name="factor_first",
        cost_estimate=pl.CostEstimate(flops=8_000_000_000, transcendentals=0, bytes_accessed=4 << 20),
    )(me, own, core, far, far_core)


def factor_next(panels, matrix):
    n = matrix.shape[1]
    return pl.pallas_call(
        functools.partial(panels_kernel, panels),
        in_specs=[pl.BlockSpec(memory_space=VMEM)],
        out_specs=pl.BlockSpec(memory_space=VMEM),
        out_shape=pltpu.VMEM((n, n), F32),
        input_output_aliases={0: 0},
        compiler_params=params(14),
        name="factor_next",
        cost_estimate=pl.CostEstimate(flops=8_000_000_000, transcendentals=0, bytes_accessed=4 << 20),
    )(vmem(matrix))


def whiten_kernel(
    at_ref, *refs
):
    *piece_refs, inv_ref, cov_ref, white_ref, cov_out_ref, loss_ref = refs[:-5]
    rows_ref, centred_ref, held_ref, new_cov_ref, sem = refs[-5:]
    count, n = white_ref.shape
    total = centred_ref.shape[0]
    chunks = n // LANES
    share = cov_ref.shape[0]
    slot = 0
    for ref in piece_refs:
        for b in range(ref.shape[0]):
            held_ref[slot] = ref[b]
            slot += 1
    embed = jnp.concatenate(
        [held_ref[jnp.bitwise_xor(at_ref[0], d)] for d in range(total // count)], axis=0
    )
    centred = embed - jnp.sum(embed, axis=0, keepdims=True) / total
    weight = 0.5 / (total - 1)
    root = 2.0**0.5
    start = pl.multiple_of(at_ref[1] * share, share)
    centred_ref[...] = centred
    left, right = split_six(centred_ref[:, pl.ds(start, share)], 0)[0], split_six(centred, 0)[1]
    new_cov_ref[...] = 0.5 * cov_ref[...] + weight * dot(left, right, 0, 0)
    written = pltpu.make_async_copy(new_cov_ref, cov_out_ref, sem)
    written.start()
    thirds = jnp.concatenate(split(root * centred, 3), axis=0)
    for k in range(0, chunks, 2):
        upto = (k + 2) * LANES
        one, two, three = split(inv_ref[k * LANES : upto, :upto], 3)
        by_one = dot(thirds[:, :upto], one, 1, 1)
        by_two = dot(thirds[: 2 * total, :upto], two, 1, 1)
        product = by_one[:total] + (by_one[total : 2 * total] + by_two[:total])
        product = product + (
            by_one[2 * total :] + by_two[total:] + dot(thirds[:total, :upto], three, 1, 1)
        )
        rows_ref[:, k, :] = product[:, :LANES]
        rows_ref[:, k + 1, :] = product[:, LANES:]
    w = [rows_ref[a] for a in range(total)]
    pairs = [(a, b) for a in range(total) for b in range(a, total)]
    products = jnp.concatenate([w[a] * w[b] for a, b in pairs], axis=0)
    before = iota((LANES, 2 * LANES), 0) < iota((LANES, 2 * LANES), 1)
    earlier = before.astype(BF16)
    sums = [dot(piece, earlier) for piece in split(products, 3)]
    sums = sums[0] + sums[1] + sums[2]
    chunk = iota((8, LANES), 0)
    entry = {}
    for i, (a, b) in enumerate(pairs):
        inside = sums[8 * i : 8 * i + 8, :LANES]
        whole = sums[8 * i : 8 * i + 8, LANES:]
        carry = jnp.where(chunk >= 1, pltpu.roll(whole, 1, 0), 0.0)
        for by in (1, 2, 4):
            carry = carry + jnp.where(chunk >= by, pltpu.roll(carry, by, 0), 0.0)
        entry[a, b] = weight * (inside + carry) + (1.0 if a == b else 0.0)
    right = list(w)
    inverse = []
    spread = jnp.ones((8, LANES), F32)
    for p in range(total):
        inv = 1.0 / entry[p, p]
        inverse.append(inv)
        spread = spread + weight * right[p] * right[p] * inv
        for a in range(p + 1, total):
            f = entry[p, a] * inv
            for b in range(a, total):
                entry[a, b] = entry[a, b] - f * entry[p, b]
            right[a] = right[a] - f * right[p]
    scale = lax.rsqrt(spread)
    solved = [None] * total
    for p in reversed(range(total)):
        x = right[p]
        for b in range(p + 1, total):
            x = x - entry[p, b] * solved[b]
        solved[p] = x * inverse[p]
    solved = [x * scale for x in solved]
    gap = jnp.zeros((8, LANES), F32)
    normed = []
    for a in range(total):
        norm = jnp.sum(jnp.sum(solved[a] * solved[a], axis=1, keepdims=True), axis=0, keepdims=True)
        normed.append(solved[a] / jnp.sqrt(norm + 1e-06))
    for pair in range(total // 2):
        diff = normed[2 * pair] - normed[2 * pair + 1]
        gap = gap + diff * diff
    gap = jnp.sum(jnp.sum(gap, axis=1, keepdims=True), axis=0, keepdims=True)
    loss_ref[...] = gap / (total // 2)
    for a in range(total):
        rows_ref[a] = solved[a]
    for m in range(count):
        own = rows_ref[at_ref[0] * count + m]
        for k in range(chunks):
            white_ref[m : m + 1, k * LANES : (k + 1) * LANES] = own[k : k + 1, :]
    written.wait()


def whiten(at, pieces, inverse, running_cov):
    groups = sum(piece.shape[0] for piece in pieces)
    count, n = pieces[0].shape[1:]
    total = groups * count
    whole = pl.BlockSpec(memory_space=VMEM)
    return pl.pallas_call(
        whiten_kernel,
        in_specs=[pl.BlockSpec(memory_space=SMEM)] + [whole] * (len(pieces) + 2),
        out_specs=[whole, pl.BlockSpec(memory_space=pl.ANY), whole],
        out_shape=[
            jax.ShapeDtypeStruct((count, n), F32),
            jax.ShapeDtypeStruct(running_cov.shape, F32),
            jax.ShapeDtypeStruct((1, 1), F32),
        ],
        scratch_shapes=[
            pltpu.VMEM((total, n // LANES, LANES), F32),
            pltpu.VMEM((total, n), F32),
            pltpu.VMEM((groups, count, n), F32),
            pltpu.VMEM(running_cov.shape, F32),
            pltpu.SemaphoreType.DMA,
        ],
        compiler_params=params(12),
        name="whiten",
    )(at, *pieces, inverse, running_cov)


def bits(size):
    return [1 << b for b in range(size.bit_length() - 1)]


def swap(x, axis, by):
    size = lax.axis_size(axis)
    return lax.ppermute(x, axis, [(i, i ^ by) for i in range(size)])


def earlier_sum(x, axis):
    size = lax.axis_size(axis)
    me = lax.axis_index(axis)
    prior = jnp.zeros_like(x)
    whole = x
    for by in bits(size):
        upper = (me & by) != 0
        if by == size // 2:
            got = lax.ppermute(whole, axis, [(i, i + by) for i in range(by)])
            prior = prior + got
        else:
            got = swap(whole, axis, by)
            prior = prior + jnp.where(upper, got, 0.0)
            whole = whole + got
    return prior


def body(hidden_states, lengths, w_query, w_key, w_value, w_out, running_cov):
    pairs, two, span, width = hidden_states.shape
    count = pairs * two
    seq, dp = lax.axis_size("seq"), lax.axis_size("dp")
    me, group = lax.axis_index("seq"), lax.axis_index("dp")
    hidden = hidden_states.reshape(count, span, width)
    flat_len = lengths.reshape(count)

    start = (me * span).astype(jnp.int32).reshape(1)
    if seq == 4 and dp == 8 and count == 2:
        white, cov, loss = body_fixed(hidden, flat_len, start, w_query, w_key, w_value, w_out, running_cov)
    else:
        fq, num, den, states = encode(hidden, w_query, w_key, w_value)
        prior = earlier_sum(states, "seq")
        partial = pooled_rows(flat_len, start, hidden, fq, num, den, prior, w_out)
        gathered = lax.all_gather(partial, ("dp", "seq"))
        embed = gathered.reshape(dp, seq, count, width).sum(axis=1).reshape(dp * count, width)
        white, cov, loss = whiten_many(embed, running_cov, count)
    return white.reshape(pairs, two, width), cov, loss


def body_fixed(hidden, flat_len, start, w_query, w_key, w_value, w_out, running_cov):
    me, group = lax.axis_index("seq"), lax.axis_index("dp")
    width = hidden.shape[2]
    half = width // 2
    core = me & 1
    at = jnp.stack([group, me]).astype(jnp.int32)
    chip_columns = lax.dynamic_slice_in_dim(running_cov, (me >> 1) * half, half, 1)
    far_cov = swap(chip_columns, "seq", 2)
    core_cov = swap(running_cov, "seq", 1)
    fq, num, den, states = encode(hidden, w_query, w_key, w_value)
    far_cov, core_cov, states = lax.optimization_barrier((far_cov, core_cov, states))
    core_states = swap(states, "seq", 1)
    far_core_cov = swap(far_cov, "seq", 1)
    quarter = states.shape[0] // 2
    matrix = factor_first((0,), at[1:], running_cov, core_cov, far_cov, far_core_cov)
    core_states, matrix = lax.optimization_barrier((core_states, matrix))
    mine = lax.dynamic_slice_in_dim(states, core * quarter, quarter, 0)
    mine = mine + lax.dynamic_slice_in_dim(core_states, core * quarter, quarter, 0)
    far_half = lax.ppermute(mine, "seq", [(0, 2), (1, 3)])
    matrix = factor_next((1, 2), matrix)
    far_half, matrix = lax.optimization_barrier((far_half, matrix))
    other_half = swap(far_half, "seq", 1)
    matrix = factor_next((3,), matrix)
    other_half, matrix = lax.optimization_barrier((other_half, matrix))
    matrix, partial = factor_next_pool(
        (4,),
        matrix,
        flat_len,
        start,
        core.astype(jnp.int32).reshape(1),
        hidden,
        fq,
        num,
        den,
        w_out,
        far_half,
        other_half,
        core_states,
    )
    got = [swap(partial, "seq", by) for by in (1, 2, 3)]
    matrix = factor_next((5,), matrix)
    partial, got, matrix = lax.optimization_barrier((partial, got, matrix))
    embed = ((partial + got[0]) + (got[1] + got[2]))[None]
    near = [swap(embed, "dp", by) for by in (1, 2, 3)]
    matrix = factor_next((6,), matrix)
    embed, near, matrix = lax.optimization_barrier((embed, near, matrix))
    embed = jnp.concatenate([embed] + near, axis=0)
    pieces = [embed, swap(embed, "dp", 4)]
    matrix = factor_next((7,), matrix)
    white, cov, loss = whiten(at, pieces, matrix, running_cov)
    return white, cov, loss.reshape(())


def whiten_many(embed, running_cov, count):
    total = embed.shape[0]
    share = running_cov.shape[0]
    centred = embed - jnp.sum(embed, axis=0) / total
    full = lax.all_gather(running_cov, "seq", axis=0, tiled=True)
    full = 0.5 * full + (0.5 / (total - 1)) * jnp.dot(centred.T, centred, precision=HIGHEST)
    chol = jnp.linalg.cholesky(full)
    rows = lax.linalg.triangular_solve(chol, centred.T, left_side=True, lower=True).T
    normed = rows / jnp.sqrt(jnp.sum(rows * rows, axis=1, keepdims=True) + 1e-06)
    normed = normed.reshape(total // 2, 2, -1)
    gap = normed[:, 0] - normed[:, 1]
    loss = jnp.sum(gap * gap) / (total // 2)
    white = lax.dynamic_slice_in_dim(rows, lax.axis_index("dp") * count, count, 0)
    cov = lax.dynamic_slice_in_dim(full, lax.axis_index("seq") * share, share, 0)
    return white, cov, loss


def solution(mesh):
    placed = (P("dp", None, "seq", None), P("dp", None), P(), P(), P(), P(), P("seq", None))
    return jax.shard_map(
        body,
        mesh=mesh,
        in_specs=placed,
        out_specs=(P("dp", None, None), P("seq", None), P()),
        check_vma=False,
    )
```
